32 devices in a mesh: fsdp: 2 (over x), heads: 4 (over y, core), tensor: 4 (over z).
Axes of the slice: x: 2, y: 2, z: 4, core: 2. Of those that a mesh axis runs over, the one named last changes fastest.
Arguments:
- tokens: bfloat16 [8, 1024, 2048], P('fsdp', 'heads'), may hold values from -6 to 6
- segments: int32 [8, 1024], P('fsdp'), may hold values from 0 to 3, never falling along the last dimension, each value on 1 to 768 neighbouring positions
- q_weight: bfloat16 [2048, 2048], P(('fsdp', 'heads'), 'tensor'), may hold values from -0.125 to 0.125
- k_weight: bfloat16 [2048, 512], P(('fsdp', 'heads'), 'tensor'), may hold values from -0.125 to 0.125
- v_weight: bfloat16 [2048, 512], P(('fsdp', 'heads'), 'tensor'), may hold values from -0.125 to 0.125
- o_weight: bfloat16 [2048, 2048], P(('fsdp', 'heads'), 'tensor'), may hold values from -0.75 to 0.75
- attn_gain: bfloat16 [2048], P(('fsdp', 'heads')), may hold values from 0.25 to 1.75
- gate_weight: bfloat16 [2048, 8192], P(('fsdp', 'heads'), 'tensor'), may hold values from -0.125 to 0.125
- up_weight: bfloat16 [2048, 8192], P(('fsdp', 'heads'), 'tensor'), may hold values from -0.125 to 0.125
- down_weight: bfloat16 [2048, 8192], P(('fsdp', 'heads'), 'tensor'), may hold values from -0.0625 to 0.0625
- ffn_gain: bfloat16 [2048], P(('fsdp', 'heads')), may hold values from 0.25 to 1.75
- cotangent: bfloat16 [8, 1024, 2048], P('fsdp', 'heads'), may hold values from -6 to 6
Outputs:
- output: bfloat16 [8, 1024, 2048], P('fsdp', 'heads')
- input_grad: float32 [8, 1024, 2048], P('fsdp', 'heads')
- q_weight_grad: float32 [2048, 2048], P(('fsdp', 'heads'), 'tensor')
- k_weight_grad: float32 [2048, 512], P(('fsdp', 'heads'), 'tensor')
- v_weight_grad: float32 [2048, 512], P(('fsdp', 'heads'), 'tensor')
- o_weight_grad: float32 [2048, 2048], P(('fsdp', 'heads'), 'tensor')
- attn_gain_grad: float32 [2048], P(('fsdp', 'heads'))
- gate_grad: float32 [2048, 8192], P(('fsdp', 'heads'), 'tensor')
- up_grad: float32 [2048, 8192], P(('fsdp', 'heads'), 'tensor')
- down_grad: float32 [2048, 8192], P(('fsdp', 'heads'), 'tensor')
- ffn_gain_grad: float32 [2048], P(('fsdp', 'heads'))
The draws below stay inside these ranges and needn't reach their ends.
Inputs may be any that keep to these rules, and one draw needn't show every extreme that they name: `segments`: in each sequence the document numbers start at 0, never fall, and take every value up to the largest; a document holds 1 to 768 tokens.
All inputs are finite; a program needn't handle non-finite values.
Results may differ from the reference program's by a relative error of at most 0.02.
Values may be sent and summed in bfloat16 or wider, within the bound.
No kernel may reach another device: no remote copies, remote signals or barrier semaphores. Data moves between devices by JAX's collectives and lax.ppermute only.
A program may use at most 256 MiB of HBM per device.

```python
import math
import jax
import jax.numpy as jnp
import numpy as np
from jax import lax

D = 2048
H = 32
KV = 8
HD = 64
FF = 8192
SEQ_LEN = 1024
QPD = 2
SEQS_TOTAL = 8


def shard_levels(own_key, extent, cuts, smallest, largest):
    def one(position, parts):
        steps = jax.random.uniform(jax.random.fold_in(jax.random.fold_in(own_key, 6), position), (parts,), jnp.float32, smallest / len(cuts), largest / len(cuts))
        return jnp.repeat(jnp.exp(steps), extent[position] // parts).reshape((-1,) + (1,) * (len(extent) - position - 1))

    level = one(*cuts[0])
    for cut in cuts[1:]:
        level = level * one(*cut)
    return level


def length_profile(amount, total, bound, lean):
    weights = [(1 << 20) // math.isqrt(grade ** lean) + 1 for grade in range(2, amount + 1)]
    surplus, holding = total - bound - (amount - 1), [1] * (amount - 1)
    while surplus > 0:
        free = [i for i in range(amount - 1) if holding[i] < bound]
        mass, left = sum([weights[i] for i in free]), surplus
        for i in free:
            more = min(bound - holding[i], max(1, left * weights[i] // mass), surplus)
            holding[i] = holding[i] + more
            surplus = surplus - more
    return np.array([bound] + holding)


def ragged_sizes(rng, amount, total, most, skew):
    if amount == 2:
        one = jax.random.randint(rng, (), max(1, total - most), min(most, total - 1) + 1)
        return jnp.stack([one, total - one])
    tallies = jnp.asarray(length_profile(amount, total, most, skew), jnp.int32)
    couples = (amount - 1) // 2
    source_of, sink = tallies[1:1 + 2 * couples:2], tallies[2:2 + 2 * couples:2]
    margin = jnp.minimum(source_of - 1, most - sink)
    moved = jax.random.randint(jax.random.fold_in(rng, 1), (couples,), 0, 1 << 20) % (margin + 1)
    tallies = tallies.at[1:1 + 2 * couples:2].set(source_of - moved).at[2:2 + 2 * couples:2].set(sink + moved)
    return tallies[jax.random.permutation(jax.random.fold_in(rng, 2), amount)]


def centred(own_key, extent, scale, limit, split=(), held_as=jnp.bfloat16):
    factor_of = shard_levels(own_key, extent, split, -0.22, 0.18) if split else 1.0
    values = jax.random.normal(own_key, extent, jnp.float32) * scale * factor_of
    return jnp.minimum(jnp.maximum(values, -limit), limit).astype(held_as)


def setup_inputs(seed: int = 0) -> dict:
    arg_keys = jax.random.split(jax.random.key(seed), 13)
    return {
        "tokens": centred(arg_keys[0], (SEQS_TOTAL, SEQ_LEN, D), 1.0, 6.0, ((0, 2), (1, 4))),
        "segments": jax.vmap(lambda own: jnp.searchsorted(jnp.cumsum(ragged_sizes(own, 4, SEQ_LEN, SEQ_LEN * 3 // 4, 0)), jnp.arange(SEQ_LEN), side="right"))(jax.random.split(arg_keys[1], SEQS_TOTAL)).reshape((SEQS_TOTAL, SEQ_LEN)).astype(jnp.int32),
        "q_weight": centred(arg_keys[2], (D, H * HD), D ** -0.5, 0.125, ((0, 8), (1, 4))),
        "k_weight": centred(arg_keys[3], (D, KV * HD), D ** -0.5, 0.125, ((0, 8), (1, 4))),
        "v_weight": centred(arg_keys[4], (D, KV * HD), D ** -0.5, 0.125, ((0, 8), (1, 4))),
        "o_weight": centred(arg_keys[5], (D, H * HD), (H * HD // 32) ** -0.5, 0.75, ((0, 8), (1, 4))),
        "attn_gain": jnp.clip(1.0 + 0.15 * jax.random.normal(arg_keys[6], (D,), jnp.float32), 0.25, 1.75).astype(jnp.bfloat16),
        "gate_weight": centred(arg_keys[7], (D, FF), D ** -0.5, 0.125, ((0, 8), (1, 4))),
        "up_weight": centred(arg_keys[8], (D, FF), D ** -0.5, 0.125, ((0, 8), (1, 4))),
        "down_weight": centred(arg_keys[9], (D, FF), FF ** -0.5, 0.0625, ((0, 8), (1, 4))),
        "ffn_gain": jnp.clip(1.0 + 0.15 * jax.random.normal(arg_keys[10], (D,), jnp.float32), 0.25, 1.75).astype(jnp.bfloat16),
        "cotangent": centred(arg_keys[11], (SEQS_TOTAL, SEQ_LEN, D), 1.0, 6.0, ((0, 2), (1, 4))),
    }


EPSILON = 1e-05
ROPE_BASE = 500000.0
NEG_FILL = -1e+30
PRECISE = lax.Precision.HIGHEST

@jax.custom_vjp
def low(v):
    return lax.optimization_barrier(v.astype(jnp.bfloat16)).astype(jnp.float32)

@jax.custom_vjp
def low_back(v):
    return v

def low_keep(v):
    return (low(v), None)

def low_pass(kept, grad):
    return (grad,)

def back_keep(v):
    return (v, None)

def back_low(kept, grad):
    return (low(grad),)
low.defvjp(low_keep, low_pass)
low_back.defvjp(back_keep, back_low)

def positions(segments):
    length_of = segments.shape[-1]
    column = jnp.arange(length_of, dtype=jnp.int32)
    before = jnp.concatenate([segments[..., :1] - 1, segments[..., :-1]], axis=-1)
    firsts = jnp.where(segments != before, column, jnp.zeros_like(column))
    starts = lax.cummax(firsts, axis=firsts.ndim - 1)
    return (column - starts).astype(jnp.int32)

def rotate(values_in, where_at, direction):
    half_dim = values_in.shape[-1] // 2
    frequency = ROPE_BASE ** (-2.0 * jnp.arange(half_dim, dtype=jnp.float32) / values_in.shape[-1])
    angles = where_at.astype(jnp.float32)[..., None, None] * frequency
    cosine = jnp.cos(angles)
    sine_part = direction * jnp.sin(angles)
    first_half = values_in[..., :half_dim]
    second_half = values_in[..., half_dim:]
    return jnp.concatenate([first_half * cosine - second_half * sine_part, second_half * cosine + first_half * sine_part], axis=-1)

def normed(values_in, gain_in):
    return values_in * lax.rsqrt(lax.optimization_barrier(jnp.mean(values_in * values_in, axis=-1, keepdims=True)) + EPSILON) * gain_in

def attend(queries, key_copy, value_copy, segments):
    seq_len = queries.shape[1]
    span_rows = min(512, seq_len)
    scale_by = 1.0 / math.sqrt(queries.shape[-1])
    column = jnp.arange(seq_len, dtype=jnp.int32)

    @jax.checkpoint
    def one_block(number):
        begin_at = number * span_rows
        q_block = lax.dynamic_slice_in_dim(queries, begin_at, span_rows, 1)
        seg_block = lax.dynamic_slice_in_dim(segments, begin_at, span_rows, 1)
        row_pos = begin_at + jnp.arange(span_rows, dtype=jnp.int32)
        raw_scores = jnp.einsum('gqnhd,gknd->gnhqk', q_block, key_copy, precision=PRECISE)
        scores = low_back(raw_scores) * scale_by
        allowed = (seg_block[:, :, None] == segments[:, None, :]) & (row_pos[:, None] >= column[None, :])[None]
        scores = jnp.where(allowed[:, None, None], scores, NEG_FILL)
        peak_val = lax.optimization_barrier(jnp.max(scores, axis=-1, keepdims=True))
        weights = jnp.exp(scores - peak_val)
        probs_f = weights / lax.optimization_barrier(jnp.sum(weights, axis=-1, keepdims=True))
        return jnp.einsum('gnhqk,gknd->gqnhd', low(probs_f), value_copy, precision=PRECISE)
    blocks = lax.map(one_block, jnp.arange(seq_len // span_rows, dtype=jnp.int32))
    return jnp.moveaxis(blocks, 0, 1).reshape(queries.shape)

def block_layer(tokens_in, segments, q_weight, k_weight, v_weight, o_weight, attn_gain, gate_weight, up_weight, down_weight, ffn_gain):
    seq_count, seq_len, width_d = tokens_in.shape
    head_count = q_weight.shape[1] // HD
    kv_count = k_weight.shape[1] // HD
    group_count = head_count // QPD
    where_at = positions(segments)
    normed_one = low(normed(tokens_in, attn_gain))
    query_pre = low_back(jnp.einsum('gld,de->gle', normed_one, q_weight, precision=PRECISE))
    key_pre = low_back(jnp.einsum('gld,de->gle', normed_one, k_weight, precision=PRECISE))
    value_pre = low_back(jnp.einsum('gld,de->gle', normed_one, v_weight, precision=PRECISE))
    queries = low_back(low(rotate(query_pre.reshape(seq_count, seq_len, head_count, HD), where_at, 1.0)))
    key_rot = low(rotate(key_pre.reshape(seq_count, seq_len, kv_count, HD), where_at, 1.0))
    values = low(value_pre.reshape(seq_count, seq_len, kv_count, HD))
    copy_map = np.arange(group_count) * QPD // (head_count // kv_count)
    key_copy = low_back(key_rot[:, :, copy_map])
    value_copy = low_back(values[:, :, copy_map])
    attended = attend(queries.reshape(seq_count, seq_len, group_count, QPD, HD), key_copy, value_copy, segments)
    attended = low_back(low(attended)).reshape(seq_count, seq_len, head_count * HD)
    residual = tokens_in + low_back(jnp.einsum('gle,de->gld', attended, o_weight, precision=PRECISE))
    normed_two = low(normed(residual, ffn_gain))
    gate_pre = low_back(jnp.einsum('gld,df->glf', normed_two, gate_weight, precision=PRECISE))
    up_pre = low_back(jnp.einsum('gld,df->glf', normed_two, up_weight, precision=PRECISE))
    hidden = low(jax.nn.silu(gate_pre) * up_pre)
    return residual + low_back(jnp.einsum('glf,df->gld', hidden, down_weight, precision=PRECISE))

def reference(tokens, segments, q_weight, k_weight, v_weight, o_weight, attn_gain, gate_weight, up_weight, down_weight, ffn_gain, cotangent):
    per_group = math.gcd(SEQS_TOTAL, max(1, 4096 // SEQ_LEN))
    group_count = SEQS_TOTAL // per_group
    params = tuple((weight_in.astype(jnp.float32) for weight_in in (q_weight, k_weight, v_weight, o_weight, attn_gain, gate_weight, up_weight, down_weight, ffn_gain)))
    inputs_all = (tokens.reshape(group_count, per_group, SEQ_LEN, D), segments.reshape(group_count, per_group, SEQ_LEN), cotangent.reshape(group_count, per_group, SEQ_LEN, D))

    def one_group(totals, item_in):
        tokens_part, segments_part, cot_part = item_in

        def forward(tokens_in, *weights_in):
            return block_layer(tokens_in, segments_part, *weights_in)
        result, pull_back = jax.vjp(forward, tokens_part.astype(jnp.float32), *params)
        grad_list = pull_back(cot_part.astype(jnp.float32))
        new_totals = tuple((total_in + grad_in for total_in, grad_in in zip(totals, grad_list[1:])))
        return (new_totals, (result.astype(jnp.bfloat16), grad_list[0]))
    zeros_init = tuple((jnp.zeros(weight_in.shape, jnp.float32) for weight_in in params))
    totals, (outputs, input_grads) = lax.scan(one_group, zeros_init, inputs_all)
    return (outputs.reshape(SEQS_TOTAL, SEQ_LEN, D), input_grads.reshape(SEQS_TOTAL, SEQ_LEN, D), totals[0], totals[1], totals[2], totals[3], totals[4], totals[5], totals[6], totals[7], totals[8])
```

```python
import functools
import math

import jax
import jax.numpy as jnp
import numpy as np
from jax import lax
from jax.experimental import pallas as pl
from jax.experimental.pallas import tpu as pltpu
from jax.sharding import PartitionSpec as P

HD = 64
EPSILON = 1e-05
ROPE_BASE = 500000.0
NEG_FILL = -1e30
LOG2E = math.log2(math.e)
BF = jnp.bfloat16
F32 = jnp.float32
CHUNKS = 2


def positions(segments):
    length_of = segments.shape[-1]
    column = jnp.arange(length_of, dtype=jnp.int32)
    before = jnp.concatenate([segments[..., :1] - 1, segments[..., :-1]], axis=-1)
    firsts = jnp.where(segments != before, column, jnp.zeros_like(column))
    starts = lax.cummax(firsts, axis=firsts.ndim - 1)
    return column - starts


def dot_plain(left_in, right_in):
    return jnp.dot(left_in, right_in, preferred_element_type=F32)


def dot_rows(left_in, right_in):
    return lax.dot_general(
        left_in, right_in, (((0,), (0,)), ((), ())), preferred_element_type=F32
    )


def dot_cols(left_in, right_in):
    return lax.dot_general(
        left_in, right_in, (((1,), (1,)), ((), ())), preferred_element_type=F32
    )


def line_sum(parts):
    count = parts.shape[0]
    me = lax.axis_index("tensor")

    def pick(j):
        return lax.dynamic_index_in_dim(parts, jnp.clip(j, 0, count - 1), 0, keepdims=False)

    from_left = from_right = None
    for t in range(1, count):
        to_right = pick(count - t + me)
        to_left = pick(t + me - count)
        if from_left is not None:
            to_right = (to_right.astype(F32) + from_left.astype(F32)).astype(BF)
            to_left = (to_left.astype(F32) + from_right.astype(F32)).astype(BF)
        from_left = lax.ppermute(to_right, "tensor", [(k, k + 1) for k in range(t)])
        from_right = lax.ppermute(
            to_left, "tensor", [(count - 1 - k, count - 2 - k) for k in range(t)]
        )
    return pick(me).astype(F32) + from_left.astype(F32) + from_right.astype(F32)


def line_gather(own):
    count = lax.axis_size("tensor")
    me = lax.axis_index("tensor")
    from_left = [None] * count
    from_right = [None] * count
    right = left = own
    for t in range(1, count):
        right = lax.ppermute(right, "tensor", [(k, k + 1) for k in range(t - 1, count - 1)])
        left = lax.ppermute(
            left, "tensor", [(count - 1 - k, count - 2 - k) for k in range(t - 1, count - 1)]
        )
        from_left[t], from_right[t] = right, left
    out = jnp.zeros((count,) + own.shape, own.dtype)
    out = lax.dynamic_update_index_in_dim(out, own, me, 0)
    for t in range(1, count):
        block = jnp.where(me >= t, from_left[t], from_right[count - t])
        out = lax.dynamic_update_index_in_dim(out, block, lax.rem(me - t + count, count), 0)
    return out


def pairs(count, bit):
    return [(k, k ^ bit) for k in range(count)]


def turn(values, cosine, sine):
    lane = lax.broadcasted_iota(jnp.int32, values.shape, 1)
    swapped = jnp.where(
        lax.rem(lane, 64) < 32, pltpu.roll(values, 96, 1), pltpu.roll(values, 32, 1)
    )
    return values * cosine + swapped * sine


def turn_kernel(turned, x_ref, cos_ref, sin_ref, out_ref):
    cosine, sine = cos_ref[...], sin_ref[...]
    for begin in range(0, x_ref.shape[1], 128):
        piece = x_ref[:, begin : begin + 128].astype(F32)
        if begin < turned:
            piece = turn(piece, cosine, sine)
        out_ref[:, begin : begin + 128] = piece.astype(out_ref.dtype)


def turn_call(x, cosine, sine, turned):
    rows, width = x.shape
    tile = min(256, rows)
    return pl.pallas_call(
        functools.partial(turn_kernel, turned),
        grid=(rows // tile,),
        in_specs=[
            pl.BlockSpec((tile, width), lambda i: (i, 0)),
            pl.BlockSpec((tile, 128), lambda i: (i, 0)),
            pl.BlockSpec((tile, 128), lambda i: (i, 0)),
        ],
        out_specs=pl.BlockSpec((tile, width), lambda i: (i, 0)),
        out_shape=jax.ShapeDtypeStruct((rows, width), BF),
        cost_estimate=pl.CostEstimate(
            flops=4 * rows * width, bytes_accessed=6 * rows * width, transcendentals=0
        ),
        name="turn",
    )(x, cosine, sine)


def attend_kernel(
    group, place_ref, q_ref, k0, k1, k2, k3, segq_ref, segk_ref, out_ref, lse_ref
):
    block = q_ref.shape[1]
    kv_heads = k0.shape[2] // (2 * HD)
    me = place_ref[0]
    scale = LOG2E / math.sqrt(HD)
    row = lax.broadcasted_iota(jnp.int32, (block, block), 0)
    col = lax.broadcasted_iota(jnp.int32, (block, block), 1)
    seg_q = segq_ref[0]
    refs = (k0, k1, k2, k3)
    bias = []
    for k in range(len(refs)):
        there = place_ref[1 + k]
        seg_k = segk_ref[0, :, pl.ds(pl.multiple_of(there * block, block), block)]
        ahead = (there - me) * block
        allowed = (seg_q == seg_k) & (row >= col + ahead)
        bias.append(jnp.where(allowed, 0.0, NEG_FILL))
    sums = []
    for g in range(kv_heads):
        keys = [r[0, :, g * HD : (g + 1) * HD] for r in refs]
        values = [r[0, :, (kv_heads + g) * HD : (kv_heads + g + 1) * HD] for r in refs]
        for j in range(group):
            head = g * group + j
            q = q_ref[0, :, head * HD : (head + 1) * HD]
            scores = [
                dot_cols(q, keys[k]) * scale + bias[k] for k in range(len(refs))
            ]
            peak = functools.reduce(jnp.maximum, scores)
            peak = jnp.max(peak, axis=1, keepdims=True)
            weights = [jnp.exp2(s - peak) for s in scores]
            total = functools.reduce(jnp.add, weights)
            total = jnp.sum(total, axis=1, keepdims=True)
            mixed = functools.reduce(
                jnp.add, [dot_plain(w.astype(BF), v) for w, v in zip(weights, values)]
            )
            out_ref[0, :, head * HD : (head + 1) * HD] = (mixed / total).astype(BF)
            sums.append(peak + jnp.log2(total))
    lane = lax.broadcasted_iota(jnp.int32, (block, 128), 1)
    stacked = jnp.zeros((block, 128), F32)
    for head, value in enumerate(sums):
        stacked = jnp.where(lane == head, value, stacked)
    lse_ref[0] = jnp.transpose(stacked)[: len(sums)]


def attend_call(place, q, blocks, seg_q, seg_k):
    seqs, block, width = q.shape
    heads = width // HD
    kv_width = blocks[0].shape[2]
    group = heads // (kv_width // (2 * HD))
    seq_len = seg_k.shape[2]
    keys = pl.BlockSpec((1, block, kv_width), lambda s, p: (s, 0, 0))
    work = seqs * heads * block * seq_len
    return pl.pallas_call(
        functools.partial(attend_kernel, group),
        grid_spec=pltpu.PrefetchScalarGridSpec(
            num_scalar_prefetch=1,
            grid=(seqs,),
            in_specs=[
                pl.BlockSpec((1, block, width), lambda s, p: (s, 0, 0)),
                keys,
                keys,
                keys,
                keys,
                pl.BlockSpec((1, block, 1), lambda s, p: (s, 0, 0)),
                pl.BlockSpec((1, 1, seq_len), lambda s, p: (s, 0, 0)),
            ],
            out_specs=[
                pl.BlockSpec((1, block, width), lambda s, p: (s, 0, 0)),
                pl.BlockSpec((1, heads, block), lambda s, p: (s, 0, 0)),
            ],
        ),
        out_shape=[
            jax.ShapeDtypeStruct((seqs, block, width), BF),
            jax.ShapeDtypeStruct((seqs, heads, block), F32),
        ],
        cost_estimate=pl.CostEstimate(
            flops=4 * work * HD * 4, bytes_accessed=6 * q.size, transcendentals=work
        ),
        name="attend",
    )(place, q, *blocks, seg_q, seg_k)


def attend_back_kernel(
    group,
    place_ref,
    q_ref,
    k0,
    k1,
    k2,
    k3,
    segq_ref,
    segk_ref,
    out_ref,
    grad_ref,
    lse_ref,
    dq_ref,
    d0,
    d1,
    d2,
    d3,
    bias_ref,
    dsc_ref,
):
    block = q_ref.shape[1]
    kv_heads = k0.shape[2] // (2 * HD)
    me = place_ref[0]
    scale = LOG2E / math.sqrt(HD)
    back_scale = 1.0 / math.sqrt(HD)
    refs, d_refs = (k0, k1, k2, k3), (d0, d1, d2, d3)
    key_row = lax.broadcasted_iota(jnp.int32, (block, block), 0)
    q_col = lax.broadcasted_iota(jnp.int32, (block, block), 1)
    seg_q = segq_ref[0]
    for k in range(len(refs)):
        there = place_ref[1 + k]
        seg_k = segk_ref[0, pl.ds(pl.multiple_of(there * block, block), block), :]
        ahead = (there - me) * block
        allowed = (seg_q == seg_k) & (q_col >= key_row + ahead)
        bias_ref[k] = jnp.where(allowed, 0.0, NEG_FILL)
    width = group * block
    product = out_ref[0].astype(F32) * grad_ref[0].astype(F32)
    total_heads = kv_heads * group
    feature = lax.broadcasted_iota(jnp.int32, (total_heads, product.shape[1]), 1)
    owner = lax.broadcasted_iota(jnp.int32, (total_heads, product.shape[1]), 0)
    picks = jnp.where(feature // HD == owner, 1.0, 0.0).astype(F32)
    deltas = lax.dot_general(
        picks,
        product,
        (((1,), (1,)), ((), ())),
        preferred_element_type=F32,
        precision=lax.Precision.HIGHEST,
    )
    for g in range(kv_heads):
        heads = range(g * group, (g + 1) * group)
        q = jnp.concatenate([q_ref[0, :, h * HD : (h + 1) * HD] for h in heads], 0)
        grad = jnp.concatenate([grad_ref[0, :, h * HD : (h + 1) * HD] for h in heads], 0)
        d_query = None
        for k in range(len(refs)):
            keys = refs[k][0, :, g * HD : (g + 1) * HD]
            values = refs[k][0, :, (kv_heads + g) * HD : (kv_heads + g + 1) * HD]
            scores = dot_cols(keys, q)
            d_probs = dot_cols(values, grad)
            probs_low = []
            for j, h in enumerate(heads):
                cols = slice(j * block, (j + 1) * block)
                probs = jnp.exp2(
                    scores[:, cols] * scale + (bias_ref[k] - lse_ref[0, h : h + 1, :])
                )
                probs_low.append(probs.astype(BF))
                dsc_ref[:, cols] = (
                    probs * (d_probs[:, cols] - deltas[h : h + 1, :])
                ).astype(BF)
            d_scores = dsc_ref[...]
            d_value = dot_plain(jnp.concatenate(probs_low, 1), grad)
            d_key = dot_plain(d_scores, q) * back_scale
            d_refs[k][0, :, g * HD : (g + 1) * HD] = d_key.astype(BF)
            d_refs[k][0, :, (kv_heads + g) * HD : (kv_heads + g + 1) * HD] = d_value.astype(BF)
            part = dot_rows(d_scores, keys)
            d_query = part if d_query is None else d_query + part
        d_query = d_query * back_scale
        for j, h in enumerate(heads):
            dq_ref[0, :, h * HD : (h + 1) * HD] = d_query[j * block : (j + 1) * block].astype(BF)


def attend_back_call(place, q, blocks, seg_q, seg_k, out, grad, lse):
    seqs, block, width = q.shape
    heads = width // HD
    kv_width = blocks[0].shape[2]
    group = heads // (kv_width // (2 * HD))
    seq_len = seg_k.shape[1]
    keys = pl.BlockSpec((1, block, kv_width), lambda s, p: (s, 0, 0))
    rows = pl.BlockSpec((1, block, width), lambda s, p: (s, 0, 0))
    work = seqs * heads * block * seq_len
    return pl.pallas_call(
        functools.partial(attend_back_kernel, group),
        grid_spec=pltpu.PrefetchScalarGridSpec(
            num_scalar_prefetch=1,
            grid=(seqs,),
            in_specs=[
                rows,
                keys,
                keys,
                keys,
                keys,
                pl.BlockSpec((1, 1, block), lambda s, p: (s, 0, 0)),
                pl.BlockSpec((1, seq_len, 1), lambda s, p: (s, 0, 0)),
                rows,
                rows,
                pl.BlockSpec((1, heads, block), lambda s, p: (s, 0, 0)),
            ],
            out_specs=[rows, keys, keys, keys, keys],
            scratch_shapes=[
                pltpu.VMEM((4, block, block), F32),
                pltpu.VMEM((block, group * block), BF),
            ],
        ),
        out_shape=[jax.ShapeDtypeStruct(q.shape, BF)]
        + [jax.ShapeDtypeStruct(blocks[0].shape, BF)] * 4,
        cost_estimate=pl.CostEstimate(
            flops=10 * work * HD * 4, bytes_accessed=12 * q.size, transcendentals=work
        ),
        name="attend_back",
    )(place, q, *blocks, seg_q, seg_k, out, grad, lse)


def inverse_rms(values):
    return lax.rsqrt(jnp.mean(values * values, axis=-1, keepdims=True) + EPSILON)


def norm_back(values, gain, incoming):
    scale = inverse_rms(values)
    gain_terms = jnp.sum(incoming * values * scale, axis=0)
    weighted = incoming * gain
    inner = jnp.mean(weighted * values, axis=-1, keepdims=True)
    return scale * weighted - values * (scale * scale * scale) * inner, gain_terms


def per_device(
    tokens,
    segments,
    q_weight,
    k_weight,
    v_weight,
    o_weight,
    attn_gain,
    gate_weight,
    up_weight,
    down_weight,
    ffn_gain,
    cotangent,
):
    seqs, block, width = tokens.shape
    seq_len = segments.shape[1]
    parts = lax.axis_size("heads")
    ways = lax.axis_size("tensor")
    owners = ("fsdp", "heads")
    here = lax.axis_index("heads")
    me = lax.axis_index("tensor")
    q_width, k_width = q_weight.shape[1], k_weight.shape[1]
    kv_width = 2 * k_width
    qkv_width = q_width + kv_width
    per_chunk = seqs // CHUNKS
    rows = per_chunk * block
    own_rows = rows // ways

    pad = jnp.zeros((q_weight.shape[0], 126), BF)
    packed = jnp.concatenate(
        [q_weight, k_weight, v_weight, attn_gain[:, None], ffn_gain[:, None], pad], axis=1
    )

    def gathered(shard):
        return lax.all_gather(shard, owners, axis=0, tiled=True)

    packed = gathered(packed)
    full_o = gathered(o_weight)
    full_g = gathered(gate_weight)
    full_u = gathered(up_weight)
    full_d = gathered(down_weight)
    full_qkv = packed[:, :qkv_width]
    gains = packed[:, qkv_width : qkv_width + 2].T.astype(F32)
    gain_one, gain_two = gains[0:1], gains[1:2]

    where_all = positions(segments)
    where_here = lax.dynamic_slice_in_dim(where_all, here * block, block, 1)
    seg_here = lax.dynamic_slice_in_dim(segments, here * block, block, 1)
    lane = np.arange(128)
    frequency = jnp.asarray(
        ROPE_BASE ** (-2.0 * (np.arange(128) % 32).astype(np.float32) / HD), F32
    )
    angles = where_here.reshape(seqs * block, 1).astype(F32) * frequency
    cosine = jnp.cos(angles)
    sine = jnp.sin(angles) * jnp.asarray(np.where(lane % 64 < 32, -1.0, 1.0), F32)
    place = jnp.stack([here] + [here ^ k for k in range(parts)]).astype(jnp.int32)

    def chunk_of(x, c):
        return lax.slice_in_dim(x, c * per_chunk, (c + 1) * per_chunk, axis=0)

    def own(x):
        return lax.dynamic_slice_in_dim(x, me * own_rows, own_rows, 0)

    state = []
    for c in range(CHUNKS):
        s = {}
        tok = chunk_of(tokens, c).reshape(rows, width)
        tok_f = tok.astype(F32)
        s["tok"] = tok
        s["normed_one"] = (tok_f * inverse_rms(tok_f) * gain_one).astype(BF)
        s["cos"] = lax.slice_in_dim(cosine, c * rows, (c + 1) * rows, axis=0)
        s["sin"] = lax.slice_in_dim(sine, c * rows, (c + 1) * rows, axis=0)
        kv = turn_call(
            dot_plain(s["normed_one"], full_qkv[:, q_width:]), s["cos"], s["sin"], k_width
        ).reshape(per_chunk, block, kv_width)
        kv2 = lax.ppermute(kv, "heads", pairs(parts, 2))
        kv1 = lax.ppermute(kv, "heads", pairs(parts, 1))
        kv3 = lax.ppermute(kv2, "heads", pairs(parts, 1))
        s["kv"] = (kv, kv1, kv2, kv3)
        s["q"] = turn_call(
            dot_plain(s["normed_one"], full_qkv[:, :q_width]), s["cos"], s["sin"], q_width
        ).reshape(per_chunk, block, q_width)
        state.append(s)
    for c, s in enumerate(state):
        seg_q = chunk_of(seg_here, c)
        seg_k = chunk_of(segments, c)
        s["attended"], s["lse"] = attend_call(
            place, s["q"], s["kv"], seg_q[:, :, None], seg_k[:, None, :]
        )
        s["seg"] = (seg_q[:, None, :], seg_k[:, :, None])
        attn = dot_cols(s["attended"].reshape(rows, q_width), full_o).astype(BF)
        s["residual"] = own(s["tok"]).astype(F32) + line_sum(
            attn.reshape(ways, own_rows, width)
        )
        normed_two = (s["residual"] * inverse_rms(s["residual"]) * gain_two).astype(BF)
        s["normed_two"] = line_gather(normed_two).reshape(rows, width)
    for c, s in enumerate(state):
        cot = chunk_of(cotangent, c).reshape(rows, width)
        gate = dot_plain(s["normed_two"], full_g)
        up = dot_plain(s["normed_two"], full_u)
        sig = jax.nn.sigmoid(gate)
        s["hidden"] = (gate * sig * up).astype(BF)
        d_hidden = dot_plain(cot, full_d)
        s["d_gate"] = (d_hidden * up * (sig * (1.0 + gate * (1.0 - sig)))).astype(BF)
        s["d_up"] = (d_hidden * gate * sig).astype(BF)
        back = (dot_cols(s["d_gate"], full_g) + dot_cols(s["d_up"], full_u)).astype(BF)
        d_normed_two = line_sum(back.reshape(ways, own_rows, width))
        d_norm, s["gain_two"] = norm_back(s["residual"], gain_two, d_normed_two)
        s["d_resid"] = own(cot).astype(F32) + d_norm
        s["d_attn"] = line_gather(s["d_resid"].astype(BF)).reshape(rows, width)
        ffn = dot_cols(s["hidden"], full_d).astype(BF)
        out = s["residual"] + line_sum(ffn.reshape(ways, own_rows, width))
        s["output"] = line_gather(out.astype(BF)).reshape(per_chunk, block, width)

    def joined(name):
        return jnp.concatenate([s[name] for s in state], axis=0)

    def scattered(grad):
        return lax.psum_scatter(
            grad.astype(BF), owners, scatter_dimension=0, tiled=True
        ).astype(F32)

    cot_rows = cotangent.reshape(seqs * block, width)
    n_two = joined("normed_two")
    down_grad = scattered(dot_rows(cot_rows, joined("hidden")))
    gate_grad = scattered(dot_rows(n_two, joined("d_gate")))
    up_grad = scattered(dot_rows(n_two, joined("d_up")))

    for c, s in enumerate(state):
        d_attended = dot_plain(s["d_attn"], full_o).astype(BF).reshape(per_chunk, block, q_width)
        dq, b0, b1, b2, b3 = attend_back_call(
            place, s["q"], s["kv"], s["seg"][0], s["seg"][1], s["attended"], d_attended, s["lse"]
        )
        from3 = lax.ppermute(b3, "heads", pairs(parts, 1))
        from1 = lax.ppermute(b1, "heads", pairs(parts, 1))
        far = (b2.astype(F32) + from3.astype(F32)).astype(BF)
        from2 = lax.ppermute(far, "heads", pairs(parts, 2))
        d_kv = b0.astype(F32) + from1.astype(F32) + from2.astype(F32)
        d_q = turn_call(dq.reshape(rows, q_width), s["cos"], -s["sin"], q_width)
        d_kv = turn_call(d_kv.reshape(rows, kv_width), s["cos"], -s["sin"], k_width)
        s["d_qkv"] = jnp.concatenate([d_q, d_kv], axis=1)
        back = dot_cols(s["d_qkv"], full_qkv).astype(BF)
        d_normed_one = line_sum(back.reshape(ways, own_rows, width))
        d_norm, s["gain_one"] = norm_back(own(s["tok"]).astype(F32), gain_one, d_normed_one)
        s["input_grad"] = (
            line_gather((s["d_resid"] + d_norm).astype(BF))
            .astype(F32)
            .reshape(per_chunk, block, width)
        )
    attended = joined("attended").reshape(seqs * block, q_width)
    o_grad = scattered(dot_rows(joined("d_attn"), attended))
    qkv_grad = scattered(dot_rows(joined("normed_one"), joined("d_qkv")))
    gain_grads = jnp.stack(
        [sum(s["gain_one"] for s in state), sum(s["gain_two"] for s in state)]
    )
    gain_grads = lax.psum(gain_grads, ("fsdp", "heads", "tensor"))
    share = attn_gain.shape[0]
    index = lax.axis_index("fsdp") * parts + here
    gain_grads = lax.dynamic_slice_in_dim(gain_grads, index * share, share, 1)
    return (
        joined("output"),
        joined("input_grad"),
        qkv_grad[:, :q_width],
        qkv_grad[:, q_width : q_width + k_width],
        qkv_grad[:, q_width + k_width :],
        o_grad,
        gain_grads[0],
        gate_grad,
        up_grad,
        down_grad,
        gain_grads[1],
    )


def solution(mesh):
    rows = P("fsdp", "heads", None)
    matrix = P(("fsdp", "heads"), "tensor")
    vector = P(("fsdp", "heads"))
    return jax.shard_map(
        per_device,
        mesh=mesh,
        in_specs=(
            rows,
            P("fsdp", None),
            matrix,
            matrix,
            matrix,
            matrix,
            vector,
            matrix,
            matrix,
            matrix,
            vector,
            rows,
        ),
        out_specs=(
            rows,
            rows,
            matrix,
            matrix,
            matrix,
            matrix,
            vector,
            matrix,
            matrix,
            matrix,
            vector,
        ),
        check_vma=False,
    )
```

```python
import functools
import math

import jax
import jax.numpy as jnp
import numpy as np
from jax import lax
from jax.experimental import pallas as pl
from jax.experimental.pallas import tpu as pltpu
from jax.sharding import PartitionSpec as P

HD = 64
EPSILON = 1e-05
ROPE_BASE = 500000.0
NEG_FILL = -1e30
LOG2E = math.log2(math.e)
BF = jnp.bfloat16
F32 = jnp.float32
CHUNKS = 2


def positions(segments):
    length_of = segments.shape[-1]
    column = jnp.arange(length_of, dtype=jnp.int32)
    before = jnp.concatenate([segments[..., :1] - 1, segments[..., :-1]], axis=-1)
    firsts = jnp.where(segments != before, column, jnp.zeros_like(column))
    starts = lax.cummax(firsts, axis=firsts.ndim - 1)
    return column - starts


def dot_plain(left_in, right_in):
    return jnp.dot(left_in, right_in, preferred_element_type=F32)


def dot_rows(left_in, right_in):
    return lax.dot_general(
        left_in, right_in, (((0,), (0,)), ((), ())), preferred_element_type=F32
    )


def dot_cols(left_in, right_in):
    return lax.dot_general(
        left_in, right_in, (((1,), (1,)), ((), ())), preferred_element_type=F32
    )


class LineSum:
    def __init__(self, parts):
        self.parts = parts
        self.step = 1
        self.from_left = self.from_right = None

    def pick(self, j):
        last = self.parts.shape[0] - 1
        return lax.dynamic_index_in_dim(self.parts, jnp.clip(j, 0, last), 0, keepdims=False)

    def sends(self):
        count, t = self.parts.shape[0], self.step
        me = lax.axis_index("tensor")
        to_right = self.pick(count - t + me)
        to_left = self.pick(t + me - count)
        if self.from_left is not None:
            to_right = (to_right.astype(F32) + self.from_left.astype(F32)).astype(BF)
            to_left = (to_left.astype(F32) + self.from_right.astype(F32)).astype(BF)
        return [
            (to_right, "tensor", [(k, k + 1) for k in range(t)]),
            (to_left, "tensor", [(count - 1 - k, count - 2 - k) for k in range(t)]),
        ]

    def take(self, moved):
        self.from_left, self.from_right = moved
        self.step += 1

    def result(self):
        own = self.pick(lax.axis_index("tensor"))
        return own.astype(F32) + self.from_left.astype(F32) + self.from_right.astype(F32)


class LineGather:
    def __init__(self, own):
        self.own = self.right = self.left = own
        self.step = 1
        self.from_left, self.from_right = {}, {}

    def sends(self):
        count, t = lax.axis_size("tensor"), self.step
        steps = range(t - 1, count - 1)
        return [
            (self.right, "tensor", [(k, k + 1) for k in steps]),
            (self.left, "tensor", [(count - 1 - k, count - 2 - k) for k in steps]),
        ]

    def take(self, moved):
        self.right, self.left = moved
        self.from_left[self.step], self.from_right[self.step] = moved
        self.step += 1

    def result(self):
        count, me = lax.axis_size("tensor"), lax.axis_index("tensor")
        out = jnp.zeros((count,) + self.own.shape, self.own.dtype)
        out = lax.dynamic_update_index_in_dim(out, self.own, me, 0)
        for t in range(1, count):
            block = jnp.where(me >= t, self.from_left[t], self.from_right[count - t])
            out = lax.dynamic_update_index_in_dim(out, block, lax.rem(me - t + count, count), 0)
        return out


class Butterfly:
    def __init__(self, value, axes):
        self.value = value
        self.moves = []
        for axis in axes:
            bit = 1
            while bit < lax.axis_size(axis):
                self.moves.append((axis, pairs(lax.axis_size(axis), bit)))
                bit *= 2

    def sends(self):
        axis, pattern = self.moves.pop(0)
        return [(self.value, axis, pattern)]

    def take(self, moved):
        self.value = self.value + moved[0]


class Clock:
    def __init__(self):
        self.last = ()

    def expect(self, value):
        self.last += (value,)

    def slot(self, tasks, work=None, args=()):
        sends = [task.sends() for task in tasks]
        flat = [send for group in sends for send in group]
        before = len(self.last)
        gated = lax.optimization_barrier(
            tuple(self.last) + tuple(s[0] for s in flat) + tuple(args)
        )[before:]
        moved = [lax.ppermute(g, s[1], s[2]) for g, s in zip(gated, flat)]
        done = tuple(work(*gated[len(flat) :])) if work else ()
        self.last = tuple(moved) + done
        at = 0
        for task, group in zip(tasks, sends):
            task.take(moved[at : at + len(group)])
            at += len(group)
        return done


def pairs(count, bit):
    return [(k, k ^ bit) for k in range(count)]


def turn(values, cosine, sine):
    lane = lax.broadcasted_iota(jnp.int32, values.shape, 1)
    swapped = jnp.where(
        lax.rem(lane, 64) < 32, pltpu.roll(values, 96, 1), pltpu.roll(values, 32, 1)
    )
    return values * cosine + swapped * sine


def turn_kernel(turned, x_ref, cos_ref, sin_ref, out_ref):
    cosine, sine = cos_ref[...], sin_ref[...]
    for begin in range(0, x_ref.shape[1], 128):
        piece = x_ref[:, begin : begin + 128].astype(F32)
        if begin < turned:
            piece = turn(piece, cosine, sine)
        out_ref[:, begin : begin + 128] = piece.astype(out_ref.dtype)


def turn_call(x, cosine, sine, turned):
    rows, width = x.shape
    tile = min(256, rows)
    return pl.pallas_call(
        functools.partial(turn_kernel, turned),
        grid=(rows // tile,),
        in_specs=[
            pl.BlockSpec((tile, width), lambda i: (i, 0)),
            pl.BlockSpec((tile, 128), lambda i: (i, 0)),
            pl.BlockSpec((tile, 128), lambda i: (i, 0)),
        ],
        out_specs=pl.BlockSpec((tile, width), lambda i: (i, 0)),
        out_shape=jax.ShapeDtypeStruct((rows, width), BF),
        cost_estimate=pl.CostEstimate(
            flops=4 * rows * width, bytes_accessed=6 * rows * width, transcendentals=0
        ),
        name="turn",
    )(x, cosine, sine)


def attend_kernel(
    group, place_ref, q_ref, k0, k1, k2, k3, segq_ref, segk_ref, out_ref, lse_ref
):
    block = q_ref.shape[1]
    kv_heads = k0.shape[2] // (2 * HD)
    me = place_ref[0]
    scale = LOG2E / math.sqrt(HD)
    row = lax.broadcasted_iota(jnp.int32, (block, block), 0)
    col = lax.broadcasted_iota(jnp.int32, (block, block), 1)
    seg_q = segq_ref[0]
    refs = (k0, k1, k2, k3)
    bias = []
    for k in range(len(refs)):
        there = place_ref[1 + k]
        seg_k = segk_ref[0, :, pl.ds(pl.multiple_of(there * block, block), block)]
        ahead = (there - me) * block
        allowed = (seg_q == seg_k) & (row >= col + ahead)
        bias.append(jnp.where(allowed, 0.0, NEG_FILL))
    sums = []
    for g in range(kv_heads):
        keys = [r[0, :, g * HD : (g + 1) * HD] for r in refs]
        values = [r[0, :, (kv_heads + g) * HD : (kv_heads + g + 1) * HD] for r in refs]
        for j in range(group):
            head = g * group + j
            q = q_ref[0, :, head * HD : (head + 1) * HD]
            scores = [
                dot_cols(q, keys[k]) * scale + bias[k] for k in range(len(refs))
            ]
            peak = functools.reduce(jnp.maximum, scores)
            peak = jnp.max(peak, axis=1, keepdims=True)
            weights = [jnp.exp2(s - peak) for s in scores]
            total = functools.reduce(jnp.add, weights)
            total = jnp.sum(total, axis=1, keepdims=True)
            mixed = functools.reduce(
                jnp.add, [dot_plain(w.astype(BF), v) for w, v in zip(weights, values)]
            )
            out_ref[0, :, head * HD : (head + 1) * HD] = (mixed / total).astype(BF)
            sums.append(peak + jnp.log2(total))
    lane = lax.broadcasted_iota(jnp.int32, (block, 128), 1)
    stacked = jnp.zeros((block, 128), F32)
    for head, value in enumerate(sums):
        stacked = jnp.where(lane == head, value, stacked)
    lse_ref[0] = jnp.transpose(stacked)[: len(sums)]


def attend_call(place, q, blocks, seg_q, seg_k):
    seqs, block, width = q.shape
    heads = width // HD
    kv_width = blocks[0].shape[2]
    group = heads // (kv_width // (2 * HD))
    seq_len = seg_k.shape[2]
    keys = pl.BlockSpec((1, block, kv_width), lambda s, p: (s, 0, 0))
    work = seqs * heads * block * seq_len
    return pl.pallas_call(
        functools.partial(attend_kernel, group),
        grid_spec=pltpu.PrefetchScalarGridSpec(
            num_scalar_prefetch=1,
            grid=(seqs,),
            in_specs=[
                pl.BlockSpec((1, block, width), lambda s, p: (s, 0, 0)),
                keys,
                keys,
                keys,
                keys,
                pl.BlockSpec((1, block, 1), lambda s, p: (s, 0, 0)),
                pl.BlockSpec((1, 1, seq_len), lambda s, p: (s, 0, 0)),
            ],
            out_specs=[
                pl.BlockSpec((1, block, width), lambda s, p: (s, 0, 0)),
                pl.BlockSpec((1, heads, block), lambda s, p: (s, 0, 0)),
            ],
        ),
        out_shape=[
            jax.ShapeDtypeStruct((seqs, block, width), BF),
            jax.ShapeDtypeStruct((seqs, heads, block), F32),
        ],
        cost_estimate=pl.CostEstimate(
            flops=4 * work * HD * 4, bytes_accessed=6 * q.size, transcendentals=work
        ),
        name="attend",
    )(place, q, *blocks, seg_q, seg_k)


def attend_back_kernel(
    group,
    place_ref,
    q_ref,
    k0,
    k1,
    k2,
    k3,
    segq_ref,
    segk_ref,
    out_ref,
    grad_ref,
    lse_ref,
    dq_ref,
    d0,
    d1,
    d2,
    d3,
    bias_ref,
    dsc_ref,
):
    block = q_ref.shape[1]
    kv_heads = k0.shape[2] // (2 * HD)
    me = place_ref[0]
    scale = LOG2E / math.sqrt(HD)
    back_scale = 1.0 / math.sqrt(HD)
    refs, d_refs = (k0, k1, k2, k3), (d0, d1, d2, d3)
    key_row = lax.broadcasted_iota(jnp.int32, (block, block), 0)
    q_col = lax.broadcasted_iota(jnp.int32, (block, block), 1)
    seg_q = segq_ref[0]
    for k in range(len(refs)):
        there = place_ref[1 + k]
        seg_k = segk_ref[0, pl.ds(pl.multiple_of(there * block, block), block), :]
        ahead = (there - me) * block
        allowed = (seg_q == seg_k) & (q_col >= key_row + ahead)
        bias_ref[k] = jnp.where(allowed, 0.0, NEG_FILL)
    width = group * block
    product = out_ref[0].astype(F32) * grad_ref[0].astype(F32)
    total_heads = kv_heads * group
    feature = lax.broadcasted_iota(jnp.int32, (total_heads, product.shape[1]), 1)
    owner = lax.broadcasted_iota(jnp.int32, (total_heads, product.shape[1]), 0)
    picks = jnp.where(feature // HD == owner, 1.0, 0.0).astype(F32)
    deltas = lax.dot_general(
        picks,
        product,
        (((1,), (1,)), ((), ())),
        preferred_element_type=F32,
        precision=lax.Precision.HIGHEST,
    )
    for g in range(kv_heads):
        heads = range(g * group, (g + 1) * group)
        q = jnp.concatenate([q_ref[0, :, h * HD : (h + 1) * HD] for h in heads], 0)
        grad = jnp.concatenate([grad_ref[0, :, h * HD : (h + 1) * HD] for h in heads], 0)
        d_query = None
        for k in range(len(refs)):
            keys = refs[k][0, :, g * HD : (g + 1) * HD]
            values = refs[k][0, :, (kv_heads + g) * HD : (kv_heads + g + 1) * HD]
            scores = dot_cols(keys, q)
            d_probs = dot_cols(values, grad)
            probs_low = []
            for j, h in enumerate(heads):
                cols = slice(j * block, (j + 1) * block)
                probs = jnp.exp2(
                    scores[:, cols] * scale + (bias_ref[k] - lse_ref[0, h : h + 1, :])
                )
                probs_low.append(probs.astype(BF))
                dsc_ref[:, cols] = (
                    probs * (d_probs[:, cols] - deltas[h : h + 1, :])
                ).astype(BF)
            d_scores = dsc_ref[...]
            d_value = dot_plain(jnp.concatenate(probs_low, 1), grad)
            d_key = dot_plain(d_scores, q) * back_scale
            d_refs[k][0, :, g * HD : (g + 1) * HD] = d_key.astype(BF)
            d_refs[k][0, :, (kv_heads + g) * HD : (kv_heads + g + 1) * HD] = d_value.astype(BF)
            part = dot_rows(d_scores, keys)
            d_query = part if d_query is None else d_query + part
        d_query = d_query * back_scale
        for j, h in enumerate(heads):
            dq_ref[0, :, h * HD : (h + 1) * HD] = d_query[j * block : (j + 1) * block].astype(BF)


def attend_back_call(place, q, blocks, seg_q, seg_k, out, grad, lse):
    seqs, block, width = q.shape
    heads = width // HD
    kv_width = blocks[0].shape[2]
    group = heads // (kv_width // (2 * HD))
    seq_len = seg_k.shape[1]
    keys = pl.BlockSpec((1, block, kv_width), lambda s, p: (s, 0, 0))
    rows = pl.BlockSpec((1, block, width), lambda s, p: (s, 0, 0))
    work = seqs * heads * block * seq_len
    return pl.pallas_call(
        functools.partial(attend_back_kernel, group),
        grid_spec=pltpu.PrefetchScalarGridSpec(
            num_scalar_prefetch=1,
            grid=(seqs,),
            in_specs=[
                rows,
                keys,
                keys,
                keys,
                keys,
                pl.BlockSpec((1, 1, block), lambda s, p: (s, 0, 0)),
                pl.BlockSpec((1, seq_len, 1), lambda s, p: (s, 0, 0)),
                rows,
                rows,
                pl.BlockSpec((1, heads, block), lambda s, p: (s, 0, 0)),
            ],
            out_specs=[rows, keys, keys, keys, keys],
            scratch_shapes=[
                pltpu.VMEM((4, block, block), F32),
                pltpu.VMEM((block, group * block), BF),
            ],
        ),
        out_shape=[jax.ShapeDtypeStruct(q.shape, BF)]
        + [jax.ShapeDtypeStruct(blocks[0].shape, BF)] * 4,
        cost_estimate=pl.CostEstimate(
            flops=10 * work * HD * 4, bytes_accessed=12 * q.size, transcendentals=work
        ),
        name="attend_back",
    )(place, q, *blocks, seg_q, seg_k, out, grad, lse)


def inverse_rms(values):
    return lax.rsqrt(jnp.mean(values * values, axis=-1, keepdims=True) + EPSILON)


def norm_back(values, gain, incoming):
    scale = inverse_rms(values)
    gain_terms = jnp.sum(incoming * values * scale, axis=0)
    weighted = incoming * gain
    inner = jnp.mean(weighted * values, axis=-1, keepdims=True)
    return scale * weighted - values * (scale * scale * scale) * inner, gain_terms


def per_device(
    tokens,
    segments,
    q_weight,
    k_weight,
    v_weight,
    o_weight,
    attn_gain,
    gate_weight,
    up_weight,
    down_weight,
    ffn_gain,
    cotangent,
):
    seqs, block, width = tokens.shape
    seq_len = segments.shape[1]
    parts = lax.axis_size("heads")
    ways = lax.axis_size("tensor")
    owners = ("fsdp", "heads")
    here = lax.axis_index("heads")
    me = lax.axis_index("tensor")
    q_width, k_width = q_weight.shape[1], k_weight.shape[1]
    kv_width = 2 * k_width
    qkv_width = q_width + kv_width
    per_chunk = seqs // CHUNKS
    rows = per_chunk * block
    own_rows = rows // ways

    pad = jnp.zeros((q_weight.shape[0], 126), BF)
    packed = jnp.concatenate(
        [q_weight, k_weight, v_weight, attn_gain[:, None], ffn_gain[:, None], pad], axis=1
    )

    def gathered(shard):
        return lax.all_gather(shard, owners, axis=0, tiled=True)

    packed = gathered(packed)
    full_o = gathered(o_weight)
    full_g = gathered(gate_weight)
    full_u = gathered(up_weight)
    full_d = gathered(down_weight)
    full_qkv = packed[:, :qkv_width]
    gains = packed[:, qkv_width : qkv_width + 2].T.astype(F32)
    gain_one, gain_two = gains[0:1], gains[1:2]

    where_all = positions(segments)
    where_here = lax.dynamic_slice_in_dim(where_all, here * block, block, 1)
    seg_here = lax.dynamic_slice_in_dim(segments, here * block, block, 1)
    lane = np.arange(128)
    frequency = jnp.asarray(
        ROPE_BASE ** (-2.0 * (np.arange(128) % 32).astype(np.float32) / HD), F32
    )
    angles = where_here.reshape(seqs * block, 1).astype(F32) * frequency
    cosine = jnp.cos(angles)
    sine = jnp.sin(angles) * jnp.asarray(np.where(lane % 64 < 32, -1.0, 1.0), F32)
    place = jnp.stack([here] + [here ^ k for k in range(parts)]).astype(jnp.int32)

    def chunk_of(x, c):
        return lax.slice_in_dim(x, c * per_chunk, (c + 1) * per_chunk, axis=0)

    def own(x):
        return lax.dynamic_slice_in_dim(x, me * own_rows, own_rows, 0)

    def blocks(x):
        return x.reshape(ways, own_rows, width)

    state = []
    for c in range(CHUNKS):
        s = {}
        tok = chunk_of(tokens, c).reshape(rows, width)
        tok_f = tok.astype(F32)
        s["tok"] = tok
        s["cot"] = chunk_of(cotangent, c).reshape(rows, width)
        s["normed_one"] = (tok_f * inverse_rms(tok_f) * gain_one).astype(BF)
        s["cos"] = lax.slice_in_dim(cosine, c * rows, (c + 1) * rows, axis=0)
        s["sin"] = lax.slice_in_dim(sine, c * rows, (c + 1) * rows, axis=0)
        kv = turn_call(
            dot_plain(s["normed_one"], full_qkv[:, q_width:]), s["cos"], s["sin"], k_width
        ).reshape(per_chunk, block, kv_width)
        kv2 = lax.ppermute(kv, "heads", pairs(parts, 2))
        kv1 = lax.ppermute(kv, "heads", pairs(parts, 1))
        kv3 = lax.ppermute(kv2, "heads", pairs(parts, 1))
        s["kv"] = (kv, kv1, kv2, kv3)
        s["q"] = turn_call(
            dot_plain(s["normed_one"], full_qkv[:, :q_width]), s["cos"], s["sin"], q_width
        ).reshape(per_chunk, block, q_width)
        seg_q, seg_k = chunk_of(seg_here, c), chunk_of(segments, c)
        s["seg_fwd"] = (seg_q[:, :, None], seg_k[:, None, :])
        s["seg_back"] = (seg_q[:, None, :], seg_k[:, :, None])
        state.append(s)
    first, second = state

    def attend(s, q):
        attended, lse = attend_call(place, q, s["kv"], *s["seg_fwd"])
        s["attended"], s["lse"] = attended, lse
        attn = dot_cols(attended.reshape(rows, q_width), full_o).astype(BF)
        return attended, lse, attn

    def enter_ffn(s, summed):
        s["residual"] = own(s["tok"]).astype(F32) + summed
        return (s["residual"] * inverse_rms(s["residual"]) * gain_two).astype(BF)

    def ffn_up(normed_two):
        return dot_plain(normed_two, full_g), dot_plain(normed_two, full_u)

    def ffn_mid(gate, up, cot):
        sig = jax.nn.sigmoid(gate)
        hidden = (gate * sig * up).astype(BF)
        d_hidden = dot_plain(cot, full_d)
        d_gate = (d_hidden * up * (sig * (1.0 + gate * (1.0 - sig)))).astype(BF)
        d_up = (d_hidden * gate * sig).astype(BF)
        return hidden, d_gate, d_up

    def ffn_back(d_gate, d_up):
        return ((dot_cols(d_gate, full_g) + dot_cols(d_up, full_u)).astype(BF),)

    def ffn_out(hidden):
        return (dot_cols(hidden, full_d).astype(BF),)

    def leave_ffn(s, summed):
        d_norm, s["gain_two"] = norm_back(s["residual"], gain_two, summed)
        s["d_resid"] = own(s["cot"]).astype(F32) + d_norm
        return s["d_resid"].astype(BF)

    def attend_back(s, d_attn):
        d_attended = dot_plain(d_attn, full_o).astype(BF).reshape(per_chunk, block, q_width)
        return attend_back_call(
            place, s["q"], s["kv"], *s["seg_back"], s["attended"], d_attended, s["lse"]
        )

    def project_back(s, dq, b0, b1, b2, b3):
        from3 = lax.ppermute(b3, "heads", pairs(parts, 1))
        from1 = lax.ppermute(b1, "heads", pairs(parts, 1))
        far = (b2.astype(F32) + from3.astype(F32)).astype(BF)
        from2 = lax.ppermute(far, "heads", pairs(parts, 2))
        d_kv = b0.astype(F32) + from1.astype(F32) + from2.astype(F32)
        d_q = turn_call(dq.reshape(rows, q_width), s["cos"], -s["sin"], q_width)
        d_kv = turn_call(d_kv.reshape(rows, kv_width), s["cos"], -s["sin"], k_width)
        d_qkv = jnp.concatenate([d_q, d_kv], axis=1)
        return d_qkv, dot_cols(d_qkv, full_qkv).astype(BF)

    def leave_attention(s, summed):
        d_norm, s["gain_one"] = norm_back(own(s["tok"]).astype(F32), gain_one, summed)
        return (s["d_resid"] + d_norm).astype(BF)

    def scattered(grad):
        return lax.psum_scatter(grad, owners, scatter_dimension=0, tiled=True)

    def weight_grad(*halves):
        left = jnp.concatenate(halves[:CHUNKS], axis=0)
        right = jnp.concatenate(halves[CHUNKS:], axis=0)
        return (dot_rows(left, right).astype(BF),)

    def of_both(*names):
        return tuple(s[name] for name in names for s in state)

    axes = ("tensor", "heads", "fsdp")
    clock = Clock()
    slot = clock.slot

    _, _, attn = attend(first, first["q"])
    sum_a0 = LineSum(blocks(attn))
    second["attended"], second["lse"], attn = slot(
        [sum_a0], functools.partial(attend, second), (second["q"],)
    )
    sum_a1 = LineSum(blocks(attn))
    slot([sum_a0])
    slot([sum_a0])
    gather_a0 = LineGather(enter_ffn(first, sum_a0.result()))
    slot([gather_a0])
    slot([gather_a0, sum_a1])
    slot([gather_a0, sum_a1])
    first["normed_two"] = gather_a0.result().reshape(rows, width)
    gate, up = slot([sum_a1], ffn_up, (first["normed_two"],))
    gather_a1 = LineGather(enter_ffn(second, sum_a1.result()))
    first["hidden"], first["d_gate"], first["d_up"] = slot(
        [gather_a1], ffn_mid, (gate, up, first["cot"])
    )
    (back,) = slot([gather_a1], ffn_back, (first["d_gate"], first["d_up"]))
    sum_d0 = LineSum(blocks(back))
    (ffn,) = slot([gather_a1, sum_d0], ffn_out, (first["hidden"],))
    sum_f0 = LineSum(blocks(ffn))
    second["normed_two"] = gather_a1.result().reshape(rows, width)
    gate, up = slot([sum_d0], ffn_up, (second["normed_two"],))
    second["hidden"], second["d_gate"], second["d_up"] = slot(
        [sum_d0], ffn_mid, (gate, up, second["cot"])
    )
    gather_d0 = LineGather(leave_ffn(first, sum_d0.result()))
    (back,) = slot([gather_d0], ffn_back, (second["d_gate"], second["d_up"]))
    sum_d1 = LineSum(blocks(back))
    (grad,) = slot(
        [gather_d0, sum_d1],
        weight_grad,
        of_both("cot", "hidden"),
    )
    down_grad = scattered(grad)
    (grad,) = slot([gather_d0, sum_d1], weight_grad, of_both("normed_two", "d_gate"))
    gate_grad = scattered(grad)
    first["d_attn"] = gather_d0.result().reshape(rows, width)
    (grad,) = slot([sum_d1], weight_grad, of_both("normed_two", "d_up"))
    up_grad = scattered(grad)
    gather_d1 = LineGather(leave_ffn(second, sum_d1.result()))
    gains_two = Butterfly(first["gain_two"] + second["gain_two"], axes)
    pieces = slot(
        [gather_d1, gains_two], functools.partial(attend_back, first), (first["d_attn"],)
    )
    first["d_qkv"], back = slot(
        [gather_d1, sum_f0, gains_two], functools.partial(project_back, first), pieces
    )
    sum_n0 = LineSum(blocks(back))
    (ffn,) = slot([gather_d1, sum_f0, gains_two], ffn_out, (second["hidden"],))
    sum_f1 = LineSum(blocks(ffn))
    second["d_attn"] = gather_d1.result().reshape(rows, width)
    pieces = slot(
        [sum_f0, gains_two], functools.partial(attend_back, second), (second["d_attn"],)
    )
    clock.expect(down_grad)
    gather_f0 = LineGather((first["residual"] + sum_f0.result()).astype(BF))
    second["d_qkv"], back = slot(
        [gather_f0, gains_two], functools.partial(project_back, second), pieces
    )
    sum_n1 = LineSum(blocks(back))
    (grad,) = slot(
        [gather_f0, sum_n0], weight_grad, of_both("normed_one", "d_qkv")
    )
    qkv_grad = scattered(grad)
    for s in state:
        s["attended_rows"] = s["attended"].reshape(rows, q_width)
    (grad,) = slot([gather_f0, sum_n0], weight_grad, of_both("d_attn", "attended_rows"))
    o_grad = scattered(grad)
    first["output"] = gather_f0.result()
    slot([sum_n0])
    gather_n0 = LineGather(leave_attention(first, sum_n0.result()))
    slot([gather_n0])
    slot([gather_n0, sum_n1])
    slot([gather_n0, sum_n1])
    first["input_grad"] = gather_n0.result()
    clock.expect(gate_grad)
    slot([sum_n1])
    gather_n1 = LineGather(leave_attention(second, sum_n1.result()))
    gains_one = Butterfly(first["gain_one"] + second["gain_one"], axes)
    slot([gather_n1, gains_one])
    slot([gather_n1, sum_f1, gains_one])
    slot([gather_n1, sum_f1, gains_one])
    second["input_grad"] = gather_n1.result()
    slot([sum_f1, gains_one])
    clock.expect(up_grad)
    gather_f1 = LineGather((second["residual"] + sum_f1.result()).astype(BF))
    slot([gather_f1, gains_one])
    slot([gather_f1])
    slot([gather_f1])
    second["output"] = gather_f1.result()
    while gains_one.moves:
        slot([gains_one])
    while gains_two.moves:
        slot([gains_two])

    qkv_grad, o_grad, down_grad, gate_grad, up_grad = (
        g.astype(F32) for g in (qkv_grad, o_grad, down_grad, gate_grad, up_grad)
    )
    share = attn_gain.shape[0]
    index = lax.axis_index("fsdp") * parts + here

    def owned(gain):
        return lax.dynamic_slice_in_dim(gain, index * share, share, 0)

    def whole(name):
        return jnp.concatenate(
            [s[name].reshape(per_chunk, block, width) for s in state], axis=0
        )

    return (
        whole("output"),
        whole("input_grad").astype(F32),
        qkv_grad[:, :q_width],
        qkv_grad[:, q_width : q_width + k_width],
        qkv_grad[:, q_width + k_width :],
        o_grad,
        owned(gains_one.value),
        gate_grad,
        up_grad,
        down_grad,
        owned(gains_two.value),
    )


def solution(mesh):
    rows = P("fsdp", "heads", None)
    matrix = P(("fsdp", "heads"), "tensor")
    vector = P(("fsdp", "heads"))
    return jax.shard_map(
        per_device,
        mesh=mesh,
        in_specs=(
            rows,
            P("fsdp", None),
            matrix,
            matrix,
            matrix,
            matrix,
            vector,
            matrix,
            matrix,
            matrix,
            vector,
            rows,
        ),
        out_specs=(
            rows,
            rows,
            matrix,
            matrix,
            matrix,
            matrix,
            vector,
            matrix,
            matrix,
            matrix,
            vector,
        ),
        check_vma=False,
    )
```

```python
import functools
import math

import jax
import jax.numpy as jnp
import numpy as np
from jax import lax
from jax.experimental import pallas as pl
from jax.experimental.pallas import tpu as pltpu
from jax.sharding import PartitionSpec as P

HD = 64
EPSILON = 1e-05
ROPE_BASE = 500000.0
NEG_FILL = -1e30
LOG2E = math.log2(math.e)
BF = jnp.bfloat16
F32 = jnp.float32
CHUNKS = 2


def positions(segments):
    length_of = segments.shape[-1]
    column = jnp.arange(length_of, dtype=jnp.int32)
    before = jnp.concatenate([segments[..., :1] - 1, segments[..., :-1]], axis=-1)
    firsts = jnp.where(segments != before, column, jnp.zeros_like(column))
    starts = lax.cummax(firsts, axis=firsts.ndim - 1)
    return column - starts


def dot_plain(left_in, right_in):
    return jnp.dot(left_in, right_in, preferred_element_type=F32)


def dot_rows(left_in, right_in):
    return lax.dot_general(
        left_in, right_in, (((0,), (0,)), ((), ())), preferred_element_type=F32
    )


def dot_cols(left_in, right_in):
    return lax.dot_general(
        left_in, right_in, (((1,), (1,)), ((), ())), preferred_element_type=F32
    )


class LineSum:
    def __init__(self, parts):
        self.parts = parts
        self.step = 1
        self.from_left = self.from_right = None

    def pick(self, j):
        last = self.parts.shape[0] - 1
        return lax.dynamic_index_in_dim(self.parts, jnp.clip(j, 0, last), 0, keepdims=False)

    def sends(self):
        count, t = self.parts.shape[0], self.step
        me = lax.axis_index("tensor")
        to_right = self.pick(count - t + me)
        to_left = self.pick(t + me - count)
        if self.from_left is not None:
            to_right = (to_right.astype(F32) + self.from_left.astype(F32)).astype(BF)
            to_left = (to_left.astype(F32) + self.from_right.astype(F32)).astype(BF)
        return [
            (to_right, "tensor", [(k, k + 1) for k in range(t)]),
            (to_left, "tensor", [(count - 1 - k, count - 2 - k) for k in range(t)]),
        ]

    def take(self, moved):
        self.from_left, self.from_right = moved
        self.step += 1

    def result(self):
        own = self.pick(lax.axis_index("tensor"))
        return own.astype(F32) + self.from_left.astype(F32) + self.from_right.astype(F32)


class LineGather:
    def __init__(self, own):
        self.own = self.right = self.left = own
        self.step = 1
        self.from_left, self.from_right = {}, {}

    def sends(self):
        count, t = lax.axis_size("tensor"), self.step
        steps = range(t - 1, count - 1)
        return [
            (self.right, "tensor", [(k, k + 1) for k in steps]),
            (self.left, "tensor", [(count - 1 - k, count - 2 - k) for k in steps]),
        ]

    def take(self, moved):
        self.right, self.left = moved
        self.from_left[self.step], self.from_right[self.step] = moved
        self.step += 1

    def result(self):
        count = lax.axis_size("tensor")
        steps = range(1, count)
        return place_call(
            self.own, [self.from_left[t] for t in steps], [self.from_right[t] for t in steps]
        )


class Both:
    def __init__(self, gather, total):
        self.gather, self.total = gather, total

    def sends(self):
        me, count = lax.axis_index("tensor"), lax.axis_size("tensor")
        first = self.gather.step - 1
        out = []
        for rank, whole, part in zip(
            (me, count - 1 - me), self.gather.sends(), self.total.sends()
        ):
            value = jnp.where(rank >= first, whole[0], part[0])
            out.append((value, "tensor", sorted(whole[2] + part[2])))
        return out

    def take(self, moved):
        self.gather.take(moved)
        self.total.take(moved)


FLIP = [(0, 1), (1, 0)]


class NearGather:
    def __init__(self, shard):
        self.shard = shard
        self.step = 1
        self.near = lax.axis_size("fsdp") == 2 and lax.axis_size("yy") == 2

    def sends(self):
        if not self.near:
            return []
        half = self.shard.shape[0] // 2
        if self.step == 1:
            return [(self.shard, "fsdp", FLIP), (self.shard, "yy", FLIP)]
        if self.step == 2:
            return [(self.by_y[:half], "fsdp", FLIP), (self.by_x[half:], "yy", FLIP)]
        self.mine = jnp.concatenate([self.shard, self.by_y, self.by_x, self.lo, self.hi], axis=0)
        return [(self.mine, "core", FLIP)]

    def take(self, moved):
        if self.near:
            if self.step == 1:
                self.by_x, self.by_y = moved
            elif self.step == 2:
                self.lo, self.hi = moved
            else:
                (self.other,) = moved
        self.step += 1

    def result(self):
        if not self.near:
            return lax.all_gather(self.shard, ("fsdp", "yy", "core"), axis=0, tiled=True)
        return spread_call(self.mine, self.other)


class KeyExchange:
    def __init__(self, kv):
        self.kv = kv
        self.step = 1

    def sends(self):
        if self.step == 1:
            return [(self.kv, "yy", FLIP), (self.kv, "core", FLIP)]
        return [(self.kv2, "core", FLIP)]

    def take(self, moved):
        if self.step == 1:
            self.kv2, self.kv1 = moved
        else:
            (self.kv3,) = moved
        self.step += 1

    def result(self):
        return self.kv, self.kv1, self.kv2, self.kv3


class Butterfly:
    def __init__(self, value, axes):
        self.value = value
        self.moves = []
        for axis in axes:
            bit = 1
            while bit < lax.axis_size(axis):
                self.moves.append((axis, pairs(lax.axis_size(axis), bit)))
                bit *= 2

    def sends(self):
        axis, pattern = self.moves.pop(0)
        return [(self.value, axis, pattern)]

    def take(self, moved):
        self.value = self.value + moved[0]


class Clock:
    def __init__(self):
        self.last = ()

    def expect(self, value):
        self.last += (value,)

    def slot(self, tasks, work=None, args=()):
        sends = [task.sends() for task in tasks]
        flat = [send for group in sends for send in group]
        before = len(self.last)
        gated = lax.optimization_barrier(
            tuple(self.last) + tuple(s[0] for s in flat) + tuple(args)
        )[before:]
        moved = [lax.ppermute(g, s[1], s[2]) for g, s in zip(gated, flat)]
        done = tuple(work(*gated[len(flat) :])) if work else ()
        self.last = tuple(moved) + done
        at = 0
        for task, group in zip(tasks, sends):
            task.take(moved[at : at + len(group)])
            at += len(group)
        return done


def pairs(count, bit):
    return [(k, k ^ bit) for k in range(count)]


def turn(values, cosine, sine):
    lane = lax.broadcasted_iota(jnp.int32, values.shape, 1)
    swapped = jnp.where(
        lax.rem(lane, 64) < 32, pltpu.roll(values, 96, 1), pltpu.roll(values, 32, 1)
    )
    return values * cosine + swapped * sine


def place_kernel(count, me_ref, *refs):
    own, from_left, from_right = refs[0], refs[1:count], refs[count : 2 * count - 1]
    out = refs[2 * count - 1]
    me = me_ref[0]
    for k in range(count):
        todo = [(me == k, own)]
        for t in range(1, count):
            if k + t < count:
                todo.append((me == k + t, from_left[t - 1]))
            if k - t >= 0:
                todo.append((me == k - t, from_right[t - 1]))
        for chosen, source in todo:

            @pl.when(chosen)
            def _(source=source, k=k):
                out[k] = source[...]


def place_call(own, from_left, from_right):
    count = len(from_left) + 1
    rows, width = own.shape
    tile = min(64, rows)
    me = lax.axis_index("tensor").astype(jnp.int32)[None]
    return pl.pallas_call(
        functools.partial(place_kernel, count),
        grid_spec=pltpu.PrefetchScalarGridSpec(
            num_scalar_prefetch=1,
            grid=(rows // tile,),
            in_specs=[pl.BlockSpec((tile, width), lambda i, p: (i, 0))] * (2 * count - 1),
            out_specs=pl.BlockSpec((count, tile, width), lambda i, p: (0, i, 0)),
        ),
        out_shape=jax.ShapeDtypeStruct((count,) + own.shape, own.dtype),
        cost_estimate=pl.CostEstimate(
            flops=0, bytes_accessed=6 * count * own.size, transcendentals=0
        ),
        name="place",
    )(me, own, *from_left, *from_right)


def spread_kernel(at_ref, mine_ref, other_ref, out_ref):
    for core in range(2):

        @pl.when(at_ref[1] == core)
        def _(core=core):
            out_ref[0, core] = mine_ref[0]
            out_ref[0, 1 - core] = other_ref[0]


def spread_call(mine, other):
    rows, width = mine.shape[0] // 4, mine.shape[1]
    chip = lax.axis_index("fsdp") * 2 + lax.axis_index("yy")
    at = jnp.stack([chip, lax.axis_index("core")]).astype(jnp.int32)
    block = pl.BlockSpec((1, rows, width), lambda i, at: (jnp.bitwise_xor(i, at[0]), 0, 0))
    out = pl.pallas_call(
        spread_kernel,
        grid_spec=pltpu.PrefetchScalarGridSpec(
            num_scalar_prefetch=1,
            grid=(4,),
            in_specs=[block, block],
            out_specs=pl.BlockSpec((1, 2, rows, width), lambda i, at: (i, 0, 0, 0)),
        ),
        out_shape=jax.ShapeDtypeStruct((4, 2, rows, width), mine.dtype),
        cost_estimate=pl.CostEstimate(
            flops=0, bytes_accessed=8 * mine.size, transcendentals=0
        ),
        name="spread",
    )(at, mine.reshape(4, rows, width), other.reshape(4, rows, width))
    return out.reshape(8 * rows, width)


def ffn_kernel(x_ref, cot_ref, g_ref, u_ref, d_ref, hidden_ref, d_gate_ref, d_up_ref):
    x = x_ref[...]
    gate = dot_plain(x, g_ref[...])
    up = dot_plain(x, u_ref[...])
    d_hidden = dot_plain(cot_ref[...], d_ref[...])
    sig = jax.nn.sigmoid(gate)
    act = gate * sig
    hidden_ref[...] = (act * up).astype(BF)
    d_up_ref[...] = (d_hidden * act).astype(BF)
    d_gate_ref[...] = (d_hidden * up * (sig * (1.0 + gate * (1.0 - sig)))).astype(BF)


def ffn_call(x, cot, g, u, d):
    rows, width = x.shape
    units = g.shape[1]
    tile = min(256, units)
    whole = pl.BlockSpec((rows, width), lambda i: (0, 0))
    weight = pl.BlockSpec((width, tile), lambda i: (0, i))
    part = pl.BlockSpec((rows, tile), lambda i: (0, i))
    return pl.pallas_call(
        ffn_kernel,
        grid=(units // tile,),
        in_specs=[whole, whole, weight, weight, weight],
        out_specs=[part] * 3,
        out_shape=[jax.ShapeDtypeStruct((rows, units), BF)] * 3,
        cost_estimate=pl.CostEstimate(
            flops=6 * rows * width * units,
            bytes_accessed=6 * width * units + 6 * rows * units,
            transcendentals=rows * units,
        ),
        name="ffn",
    )(x, cot, g, u, d)


def product_kernel(count, *refs):
    total = None
    for k in range(count):
        part = dot_plain(refs[k][...], refs[count + k][...])
        total = part if total is None else total + part
    refs[2 * count][...] = total.astype(BF)


def product_call(lefts, rights):
    count = len(lefts)
    rows, depth = lefts[0].shape
    width = rights[0].shape[1]
    tile = min(512, width)
    return pl.pallas_call(
        functools.partial(product_kernel, count),
        grid=(width // tile,),
        in_specs=[pl.BlockSpec((rows, depth), lambda i: (0, 0))] * count
        + [pl.BlockSpec((depth, tile), lambda i: (0, i))] * count,
        out_specs=pl.BlockSpec((rows, tile), lambda i: (0, i)),
        out_shape=jax.ShapeDtypeStruct((rows, width), BF),
        cost_estimate=pl.CostEstimate(
            flops=2 * count * rows * depth * width,
            bytes_accessed=2 * count * depth * (rows + width),
            transcendentals=0,
        ),
        name="product",
    )(*lefts, *rights)


def transpose_kernel(x_ref, out_ref):
    out_ref[...] = jnp.transpose(x_ref[...])


def transpose_call(x):
    rows, columns = x.shape
    tile = min(256, rows)
    return pl.pallas_call(
        transpose_kernel,
        grid=(rows // tile,),
        in_specs=[pl.BlockSpec((tile, columns), lambda i: (i, 0))],
        out_specs=pl.BlockSpec((columns, tile), lambda i: (0, i)),
        out_shape=jax.ShapeDtypeStruct((columns, rows), x.dtype),
        cost_estimate=pl.CostEstimate(
            flops=0, bytes_accessed=4 * x.size, transcendentals=0
        ),
        name="turn_over",
    )(x)


def turn_kernel(turned, x_ref, cos_ref, sin_ref, out_ref):
    cosine, sine = cos_ref[...], sin_ref[...]
    for begin in range(0, x_ref.shape[1], 128):
        piece = x_ref[:, begin : begin + 128].astype(F32)
        if begin < turned:
            piece = turn(piece, cosine, sine)
        out_ref[:, begin : begin + 128] = piece.astype(out_ref.dtype)


def turn_call(x, cosine, sine, turned):
    rows, width = x.shape
    tile = min(256, rows)
    return pl.pallas_call(
        functools.partial(turn_kernel, turned),
        grid=(rows // tile,),
        in_specs=[
            pl.BlockSpec((tile, width), lambda i: (i, 0)),
            pl.BlockSpec((tile, 128), lambda i: (i, 0)),
            pl.BlockSpec((tile, 128), lambda i: (i, 0)),
        ],
        out_specs=pl.BlockSpec((tile, width), lambda i: (i, 0)),
        out_shape=jax.ShapeDtypeStruct((rows, width), BF),
        cost_estimate=pl.CostEstimate(
            flops=4 * rows * width, bytes_accessed=6 * rows * width, transcendentals=0
        ),
        name="turn",
    )(x, cosine, sine)


def attend_kernel(
    group, place_ref, q_ref, k0, k1, k2, k3, segq_ref, segk_ref, out_ref, lse_ref
):
    block = q_ref.shape[1]
    kv_heads = k0.shape[2] // (2 * HD)
    me = place_ref[0]
    scale = LOG2E / math.sqrt(HD)
    row = lax.broadcasted_iota(jnp.int32, (block, block), 0)
    col = lax.broadcasted_iota(jnp.int32, (block, block), 1)
    seg_q = segq_ref[0]
    refs = (k0, k1, k2, k3)
    bias = []
    for k in range(len(refs)):
        there = place_ref[1 + k]
        seg_k = segk_ref[0, :, pl.ds(pl.multiple_of(there * block, block), block)]
        ahead = (there - me) * block
        allowed = (seg_q == seg_k) & (row >= col + ahead)
        bias.append(jnp.where(allowed, 0.0, NEG_FILL))
    sums = []
    for g in range(kv_heads):
        keys = [r[0, :, g * HD : (g + 1) * HD] for r in refs]
        values = [r[0, :, (kv_heads + g) * HD : (kv_heads + g + 1) * HD] for r in refs]
        for j in range(group):
            head = g * group + j
            q = q_ref[0, :, head * HD : (head + 1) * HD]
            scores = [
                dot_cols(q, keys[k]) * scale + bias[k] for k in range(len(refs))
            ]
            peak = functools.reduce(jnp.maximum, scores)
            peak = jnp.max(peak, axis=1, keepdims=True)
            weights = [jnp.exp2(s - peak) for s in scores]
            total = functools.reduce(jnp.add, weights)
            total = jnp.sum(total, axis=1, keepdims=True)
            mixed = functools.reduce(
                jnp.add, [dot_plain(w.astype(BF), v) for w, v in zip(weights, values)]
            )
            out_ref[0, :, head * HD : (head + 1) * HD] = (mixed / total).astype(BF)
            sums.append(peak + jnp.log2(total))
    lane = lax.broadcasted_iota(jnp.int32, (block, 128), 1)
    stacked = jnp.zeros((block, 128), F32)
    for head, value in enumerate(sums):
        stacked = jnp.where(lane == head, value, stacked)
    lse_ref[0] = jnp.transpose(stacked)[: len(sums)]


def attend_call(place, q, blocks, seg_q, seg_k):
    seqs, block, width = q.shape
    heads = width // HD
    kv_width = blocks[0].shape[2]
    group = heads // (kv_width // (2 * HD))
    seq_len = seg_k.shape[2]
    keys = pl.BlockSpec((1, block, kv_width), lambda s, p: (s, 0, 0))
    work = seqs * heads * block * seq_len
    return pl.pallas_call(
        functools.partial(attend_kernel, group),
        grid_spec=pltpu.PrefetchScalarGridSpec(
            num_scalar_prefetch=1,
            grid=(seqs,),
            in_specs=[
                pl.BlockSpec((1, block, width), lambda s, p: (s, 0, 0)),
                keys,
                keys,
                keys,
                keys,
                pl.BlockSpec((1, block, 1), lambda s, p: (s, 0, 0)),
                pl.BlockSpec((1, 1, seq_len), lambda s, p: (s, 0, 0)),
            ],
            out_specs=[
                pl.BlockSpec((1, block, width), lambda s, p: (s, 0, 0)),
                pl.BlockSpec((1, heads, block), lambda s, p: (s, 0, 0)),
            ],
        ),
        out_shape=[
            jax.ShapeDtypeStruct((seqs, block, width), BF),
            jax.ShapeDtypeStruct((seqs, heads, block), F32),
        ],
        cost_estimate=pl.CostEstimate(
            flops=4 * work * HD * 4, bytes_accessed=6 * q.size, transcendentals=work
        ),
        name="attend",
    )(place, q, *blocks, seg_q, seg_k)


def attend_back_kernel(
    group,
    place_ref,
    q_ref,
    k0,
    k1,
    k2,
    k3,
    segq_ref,
    segk_ref,
    out_ref,
    grad_ref,
    lse_ref,
    dq_ref,
    d0,
    d1,
    d2,
    d3,
    bias_ref,
    dsc_ref,
):
    block = q_ref.shape[1]
    kv_heads = k0.shape[2] // (2 * HD)
    me = place_ref[0]
    scale = LOG2E / math.sqrt(HD)
    back_scale = 1.0 / math.sqrt(HD)
    refs, d_refs = (k0, k1, k2, k3), (d0, d1, d2, d3)
    key_row = lax.broadcasted_iota(jnp.int32, (block, block), 0)
    q_col = lax.broadcasted_iota(jnp.int32, (block, block), 1)
    seg_q = segq_ref[0]
    for k in range(len(refs)):
        there = place_ref[1 + k]
        seg_k = segk_ref[0, pl.ds(pl.multiple_of(there * block, block), block), :]
        ahead = (there - me) * block
        allowed = (seg_q == seg_k) & (q_col >= key_row + ahead)
        bias_ref[k] = jnp.where(allowed, 0.0, NEG_FILL)
    width = group * block
    product = out_ref[0].astype(F32) * grad_ref[0].astype(F32)
    total_heads = kv_heads * group
    feature = lax.broadcasted_iota(jnp.int32, (total_heads, product.shape[1]), 1)
    owner = lax.broadcasted_iota(jnp.int32, (total_heads, product.shape[1]), 0)
    picks = jnp.where(feature // HD == owner, 1.0, 0.0).astype(F32)
    deltas = lax.dot_general(
        picks,
        product,
        (((1,), (1,)), ((), ())),
        preferred_element_type=F32,
        precision=lax.Precision.HIGHEST,
    )
    for g in range(kv_heads):
        heads = range(g * group, (g + 1) * group)
        q = jnp.concatenate([q_ref[0, :, h * HD : (h + 1) * HD] for h in heads], 0)
        grad = jnp.concatenate([grad_ref[0, :, h * HD : (h + 1) * HD] for h in heads], 0)
        d_query = None
        for k in range(len(refs)):
            keys = refs[k][0, :, g * HD : (g + 1) * HD]
            values = refs[k][0, :, (kv_heads + g) * HD : (kv_heads + g + 1) * HD]
            scores = dot_cols(keys, q)
            d_probs = dot_cols(values, grad)
            probs_low = []
            for j, h in enumerate(heads):
                cols = slice(j * block, (j + 1) * block)
                probs = jnp.exp2(
                    scores[:, cols] * scale + (bias_ref[k] - lse_ref[0, h : h + 1, :])
                )
                probs_low.append(probs.astype(BF))
                dsc_ref[:, cols] = (
                    probs * (d_probs[:, cols] - deltas[h : h + 1, :])
                ).astype(BF)
            d_scores = dsc_ref[...]
            d_value = dot_plain(jnp.concatenate(probs_low, 1), grad)
            d_key = dot_plain(d_scores, q) * back_scale
            d_refs[k][0, :, g * HD : (g + 1) * HD] = d_key.astype(BF)
            d_refs[k][0, :, (kv_heads + g) * HD : (kv_heads + g + 1) * HD] = d_value.astype(BF)
            part = dot_rows(d_scores, keys)
            d_query = part if d_query is None else d_query + part
        d_query = d_query * back_scale
        for j, h in enumerate(heads):
            dq_ref[0, :, h * HD : (h + 1) * HD] = d_query[j * block : (j + 1) * block].astype(BF)


def attend_back_call(place, q, blocks, seg_q, seg_k, out, grad, lse):
    seqs, block, width = q.shape
    heads = width // HD
    kv_width = blocks[0].shape[2]
    group = heads // (kv_width // (2 * HD))
    seq_len = seg_k.shape[1]
    keys = pl.BlockSpec((1, block, kv_width), lambda s, p: (s, 0, 0))
    rows = pl.BlockSpec((1, block, width), lambda s, p: (s, 0, 0))
    work = seqs * heads * block * seq_len
    return pl.pallas_call(
        functools.partial(attend_back_kernel, group),
        grid_spec=pltpu.PrefetchScalarGridSpec(
            num_scalar_prefetch=1,
            grid=(seqs,),
            in_specs=[
                rows,
                keys,
                keys,
                keys,
                keys,
                pl.BlockSpec((1, 1, block), lambda s, p: (s, 0, 0)),
                pl.BlockSpec((1, seq_len, 1), lambda s, p: (s, 0, 0)),
                rows,
                rows,
                pl.BlockSpec((1, heads, block), lambda s, p: (s, 0, 0)),
            ],
            out_specs=[rows, keys, keys, keys, keys],
            scratch_shapes=[
                pltpu.VMEM((4, block, block), F32),
                pltpu.VMEM((block, group * block), BF),
            ],
        ),
        out_shape=[jax.ShapeDtypeStruct(q.shape, BF)]
        + [jax.ShapeDtypeStruct(blocks[0].shape, BF)] * 4,
        cost_estimate=pl.CostEstimate(
            flops=10 * work * HD * 4, bytes_accessed=12 * q.size, transcendentals=work
        ),
        name="attend_back",
    )(place, q, *blocks, seg_q, seg_k, out, grad, lse)


def inverse_rms(values):
    return lax.rsqrt(jnp.mean(values * values, axis=-1, keepdims=True) + EPSILON)


def norm_back(values, gain, incoming):
    scale = inverse_rms(values)
    gain_terms = jnp.sum(incoming * values * scale, axis=0)
    weighted = incoming * gain
    inner = jnp.mean(weighted * values, axis=-1, keepdims=True)
    return scale * weighted - values * (scale * scale * scale) * inner, gain_terms


def per_device(
    tokens,
    segments,
    q_weight,
    k_weight,
    v_weight,
    o_weight,
    attn_gain,
    gate_weight,
    up_weight,
    down_weight,
    ffn_gain,
    cotangent,
):
    heads_axes = ("yy", "core")
    seqs, block, width = tokens.shape
    seq_len = segments.shape[1]
    parts = lax.axis_size(heads_axes)
    ways = lax.axis_size("tensor")
    owners = ("fsdp",) + heads_axes
    here = lax.axis_index(heads_axes)
    me = lax.axis_index("tensor")
    q_width, k_width = q_weight.shape[1], k_weight.shape[1]
    kv_width = 2 * k_width
    qkv_width = q_width + kv_width
    per_chunk = seqs // CHUNKS
    rows = per_chunk * block
    own_rows = rows // ways

    pad = jnp.zeros((q_weight.shape[0], 126), BF)
    packed = jnp.concatenate(
        [q_weight, k_weight, v_weight, attn_gain[:, None], ffn_gain[:, None], pad], axis=1
    )

    def gathered(shard):
        return lax.all_gather(shard, owners, axis=0, tiled=True)

    packed = gathered(packed)
    full_g = gathered(gate_weight)
    full_u = gathered(up_weight)
    full_d = gathered(down_weight)

    where_all = positions(segments)
    where_here = lax.dynamic_slice_in_dim(where_all, here * block, block, 1)
    seg_here = lax.dynamic_slice_in_dim(segments, here * block, block, 1)
    lane = np.arange(128)
    frequency = jnp.asarray(
        ROPE_BASE ** (-2.0 * (np.arange(128) % 32).astype(np.float32) / HD), F32
    )
    angles = where_here.reshape(seqs * block, 1).astype(F32) * frequency
    cosine = jnp.cos(angles)
    sine = jnp.sin(angles) * jnp.asarray(np.where(lane % 64 < 32, -1.0, 1.0), F32)
    place = jnp.stack([here] + [here ^ k for k in range(parts)]).astype(jnp.int32)

    def chunk_of(x, c):
        return lax.slice_in_dim(x, c * per_chunk, (c + 1) * per_chunk, axis=0)

    def own(x):
        return lax.dynamic_slice_in_dim(x, me * own_rows, own_rows, 0)

    def blocks(x):
        return x.reshape(ways, own_rows, width)

    state = []
    for c in range(CHUNKS):
        s = {}
        tok = chunk_of(tokens, c).reshape(rows, width)
        s["tok"] = tok
        s["cot"] = chunk_of(cotangent, c).reshape(rows, width)
        s["cos"] = lax.slice_in_dim(cosine, c * rows, (c + 1) * rows, axis=0)
        s["sin"] = lax.slice_in_dim(sine, c * rows, (c + 1) * rows, axis=0)
        seg_q, seg_k = chunk_of(seg_here, c), chunk_of(segments, c)
        s["seg_fwd"] = (seg_q[:, :, None], seg_k[:, None, :])
        s["seg_back"] = (seg_q[:, None, :], seg_k[:, :, None])
        state.append(s)
    first, second = state

    clock = Clock()
    slot = clock.slot
    gather_o = NearGather(o_weight)
    slot([gather_o])
    slot([gather_o])
    slot([gather_o])
    full_o = gather_o.result()
    full_qkv = packed[:, :qkv_width]
    gains = packed[:, qkv_width : qkv_width + 2].T.astype(F32)
    gain_one, gain_two = gains[0:1], gains[1:2]

    def project_kv(s, tok):
        tok_f = tok.astype(F32)
        normed = (tok_f * inverse_rms(tok_f) * gain_one).astype(BF)
        kv = turn_call(dot_plain(normed, full_qkv[:, q_width:]), s["cos"], s["sin"], k_width)
        return normed, kv.reshape(per_chunk, block, kv_width)

    def project_q(s, normed):
        q = turn_call(dot_plain(normed, full_qkv[:, :q_width]), s["cos"], s["sin"], q_width)
        return (q.reshape(per_chunk, block, q_width),)

    def project(s, tok):
        normed, kv = project_kv(s, tok)
        return (normed, kv) + project_q(s, normed)

    def attend(s, q, *kv):
        attended, lse = attend_call(place, q, kv, *s["seg_fwd"])
        s["attended"], s["lse"] = attended, lse
        attn = dot_cols(attended.reshape(rows, q_width), full_o).astype(BF)
        return attended, lse, attn

    def enter_ffn(s, summed):
        s["residual"] = own(s["tok"]).astype(F32) + summed
        return (s["residual"] * inverse_rms(s["residual"]) * gain_two).astype(BF)

    turned = {}

    def turn_over(weight):
        return (transpose_call(weight),)

    def ffn_mid(normed_two, cot):
        return ffn_call(normed_two, cot, full_g, full_u, full_d)

    def ffn_back(d_gate, d_up):
        return (product_call((d_gate, d_up), (turned["g"], turned["u"])),)

    def ffn_out(hidden):
        return (product_call((hidden,), (turned["d"],)),)

    def leave_ffn(s, summed):
        d_norm, s["gain_two"] = norm_back(s["residual"], gain_two, summed)
        s["d_resid"] = own(s["cot"]).astype(F32) + d_norm
        return s["d_resid"].astype(BF)

    def attend_back(s, d_attn):
        d_attended = dot_plain(d_attn, full_o).astype(BF).reshape(per_chunk, block, q_width)
        return attend_back_call(
            place, s["q"], s["kv"], *s["seg_back"], s["attended"], d_attended, s["lse"]
        )

    def project_back(s, dq, b0, b1, b2, b3):
        from3 = lax.ppermute(b3, "core", FLIP)
        from1 = lax.ppermute(b1, "core", FLIP)
        far = (b2.astype(F32) + from3.astype(F32)).astype(BF)
        from2 = lax.ppermute(far, "yy", FLIP)
        d_kv = b0.astype(F32) + from1.astype(F32) + from2.astype(F32)
        d_q = turn_call(dq.reshape(rows, q_width), s["cos"], -s["sin"], q_width)
        d_kv = turn_call(d_kv.reshape(rows, kv_width), s["cos"], -s["sin"], k_width)
        d_qkv = jnp.concatenate([d_q, d_kv], axis=1)
        return d_qkv, dot_cols(d_qkv, full_qkv).astype(BF)

    def leave_attention(s, summed):
        d_norm, s["gain_one"] = norm_back(own(s["tok"]).astype(F32), gain_one, summed)
        return (s["d_resid"] + d_norm).astype(BF)

    def scattered(grad):
        return lax.psum_scatter(grad, owners, scatter_dimension=0, tiled=True)

    def weight_grad(*halves):
        left = jnp.concatenate(halves[:-CHUNKS], axis=0)
        right = jnp.concatenate(halves[-CHUNKS:], axis=0)
        return (dot_rows(left, right).astype(BF),)

    def of_both(*names):
        return tuple(s[name] for name in names for s in state)

    def leave_layer(s, ffn):
        mine = own(ffn).astype(F32) + s["residual"]
        ffn = lax.dynamic_update_slice_in_dim(ffn, mine.astype(BF), me * own_rows, 0)
        s["output"] = lax.psum(ffn, "tensor")

    axes = ("tensor", "core", "yy", "fsdp")
    first["normed_one"], kv = slot(
        [], functools.partial(project_kv, first), (first["tok"],)
    )
    keys = KeyExchange(kv)
    (first["q"],) = slot(
        [keys], functools.partial(project_q, first), (first["normed_one"],)
    )
    slot([keys])
    first["kv"] = keys.result()
    first["attended"], first["lse"], attn = slot(
        [], functools.partial(attend, first), (first["q"],) + first["kv"]
    )
    sum_a0 = LineSum(blocks(attn))
    second["normed_one"], kv, second["q"] = slot(
        [sum_a0], functools.partial(project, second), (second["tok"],)
    )
    keys = KeyExchange(kv)
    slot([sum_a0, keys])
    slot([sum_a0, keys])
    second["kv"] = keys.result()
    gather_a0 = LineGather(enter_ffn(first, sum_a0.result()))
    second["attended"], second["lse"], attn = slot(
        [gather_a0], functools.partial(attend, second), (second["q"],) + second["kv"]
    )
    sum_a1 = LineSum(blocks(attn))
    (turned["g"],) = slot([Both(gather_a0, sum_a1)], turn_over, (full_g,))
    (turned["u"],) = slot([Both(gather_a0, sum_a1)], turn_over, (full_u,))
    first["normed_two"] = gather_a0.result().reshape(rows, width)
    first["hidden"], first["d_gate"], first["d_up"] = slot(
        [sum_a1], ffn_mid, (first["normed_two"], first["cot"])
    )
    gather_a1 = LineGather(enter_ffn(second, sum_a1.result()))
    (back,) = slot([gather_a1], ffn_back, (first["d_gate"], first["d_up"]))
    sum_d0 = LineSum(blocks(back))
    (turned["d"],) = slot([Both(gather_a1, sum_d0)], turn_over, (full_d,))
    (ffn,) = slot([Both(gather_a1, sum_d0)], ffn_out, (first["hidden"],))
    leave_layer(first, ffn)
    second["normed_two"] = gather_a1.result().reshape(rows, width)
    second["hidden"], second["d_gate"], second["d_up"] = slot(
        [sum_d0], ffn_mid, (second["normed_two"], second["cot"])
    )
    gather_d0 = LineGather(leave_ffn(first, sum_d0.result()))
    (back,) = slot([gather_d0], ffn_back, (second["d_gate"], second["d_up"]))
    sum_d1 = LineSum(blocks(back))
    (grad,) = slot(
        [Both(gather_d0, sum_d1)],
        weight_grad,
        (cotangent.reshape(seqs * block, width),) + of_both("hidden"),
    )
    down_grad = scattered(grad)
    (grad,) = slot([Both(gather_d0, sum_d1)], weight_grad, of_both("normed_two", "d_gate"))
    gate_grad = scattered(grad)
    first["d_attn"] = gather_d0.result().reshape(rows, width)
    pieces = slot([sum_d1], functools.partial(attend_back, first), (first["d_attn"],))
    gather_d1 = LineGather(leave_ffn(second, sum_d1.result()))
    gains_two = Butterfly(first["gain_two"] + second["gain_two"], axes)
    first["d_qkv"], back = slot(
        [gather_d1, gains_two], functools.partial(project_back, first), pieces
    )
    sum_n0 = LineSum(blocks(back))
    (grad,) = slot(
        [Both(gather_d1, sum_n0), gains_two], weight_grad, of_both("normed_two", "d_up")
    )
    up_grad = scattered(grad)
    (ffn,) = slot([Both(gather_d1, sum_n0), gains_two], ffn_out, (second["hidden"],))
    sum_f1 = LineSum(blocks(ffn))
    second["d_attn"] = gather_d1.result().reshape(rows, width)
    pieces = slot(
        [sum_n0, gains_two], functools.partial(attend_back, second), (second["d_attn"],)
    )
    gather_n0 = LineGather(leave_attention(first, sum_n0.result()))
    second["d_qkv"], back = slot(
        [gather_n0, gains_two], functools.partial(project_back, second), pieces
    )
    sum_n1 = LineSum(blocks(back))
    clock.expect(first["output"])
    (grad,) = slot(
        [Both(gather_n0, sum_n1)], weight_grad, of_both("normed_one", "d_qkv")
    )
    qkv_grad = scattered(grad)
    for s in state:
        s["attended_rows"] = s["attended"].reshape(rows, q_width)
    (grad,) = slot(
        [Both(gather_n0, sum_n1)], weight_grad, of_both("d_attn", "attended_rows")
    )
    o_grad = scattered(grad)
    first["input_grad"] = gather_n0.result()
    slot([sum_n1])
    gather_n1 = LineGather(leave_attention(second, sum_n1.result()))
    gains_one = Butterfly(first["gain_one"] + second["gain_one"], axes)
    slot([gather_n1, gains_one])
    clock.expect(down_grad)
    slot([Both(gather_n1, sum_f1), gains_one])
    slot([Both(gather_n1, sum_f1), gains_one])
    second["input_grad"] = gather_n1.result()
    clock.expect(gate_grad)
    slot([sum_f1, gains_one])
    gather_f1 = LineGather((second["residual"] + sum_f1.result()).astype(BF))
    clock.expect(up_grad)
    slot([gather_f1, gains_one])
    slot([gather_f1])
    slot([gather_f1])
    second["output"] = gather_f1.result()
    while gains_one.moves:
        slot([gains_one])
    while gains_two.moves:
        slot([gains_two])

    qkv_grad, o_grad, down_grad, gate_grad, up_grad = (
        g.astype(F32) for g in (qkv_grad, o_grad, down_grad, gate_grad, up_grad)
    )
    share = attn_gain.shape[0]
    index = lax.axis_index("fsdp") * parts + here

    def owned(gain):
        return lax.dynamic_slice_in_dim(gain, index * share, share, 0)

    def whole(name):
        return jnp.concatenate(
            [s[name].reshape(per_chunk, block, width) for s in state], axis=0
        )

    return (
        whole("output"),
        whole("input_grad").astype(F32),
        qkv_grad[:, :q_width],
        qkv_grad[:, q_width : q_width + k_width],
        qkv_grad[:, q_width + k_width :],
        o_grad,
        owned(gains_one.value),
        gate_grad,
        up_grad,
        down_grad,
        owned(gains_two.value),
    )


def solution(mesh):
    sizes = mesh.shape
    split = (sizes["fsdp"], sizes["heads"] // 2, 2, sizes["tensor"])
    mesh = jax.sharding.Mesh(mesh.devices.reshape(split), ("fsdp", "yy", "core", "tensor"))
    heads = ("yy", "core")
    rows = P("fsdp", heads, None)
    matrix = P(("fsdp",) + heads, "tensor")
    vector = P(("fsdp",) + heads)
    return jax.shard_map(
        per_device,
        mesh=mesh,
        in_specs=(
            rows,
            P("fsdp", None),
            matrix,
            matrix,
            matrix,
            matrix,
            vector,
            matrix,
            matrix,
            matrix,
            vector,
            rows,
        ),
        out_specs=(
            rows,
            rows,
            matrix,
            matrix,
            matrix,
            matrix,
            vector,
            matrix,
            matrix,
            matrix,
            vector,
        ),
        check_vma=False,
    )
```

```python
import functools
import math

import jax
import jax.numpy as jnp
import numpy as np
from jax import lax
from jax.experimental import pallas as pl
from jax.experimental.pallas import tpu as pltpu
from jax.sharding import PartitionSpec as P

HD = 64
EPSILON = 1e-05
ROPE_BASE = 500000.0
NEG_FILL = -1e30
LOG2E = math.log2(math.e)
BF = jnp.bfloat16
F32 = jnp.float32
CHUNKS = 2


def positions(segments):
    length_of = segments.shape[-1]
    column = jnp.arange(length_of, dtype=jnp.int32)
    before = jnp.concatenate([segments[..., :1] - 1, segments[..., :-1]], axis=-1)
    firsts = jnp.where(segments != before, column, jnp.zeros_like(column))
    starts = lax.cummax(firsts, axis=firsts.ndim - 1)
    return column - starts


def dot_plain(left_in, right_in):
    return jnp.dot(left_in, right_in, preferred_element_type=F32)


def dot_rows(left_in, right_in):
    return lax.dot_general(
        left_in, right_in, (((0,), (0,)), ((), ())), preferred_element_type=F32
    )


def dot_cols(left_in, right_in):
    return lax.dot_general(
        left_in, right_in, (((1,), (1,)), ((), ())), preferred_element_type=F32
    )


class LineSum:
    def __init__(self, parts):
        self.parts = parts
        self.step = 1
        self.from_left = self.from_right = None

    def pick(self, j):
        last = self.parts.shape[0] - 1
        return lax.dynamic_index_in_dim(self.parts, jnp.clip(j, 0, last), 0, keepdims=False)

    def sends(self):
        count, t = self.parts.shape[0], self.step
        me = lax.axis_index("tensor")
        to_right = self.pick(count - t + me)
        to_left = self.pick(t + me - count)
        if self.from_left is not None:
            to_right = (to_right.astype(F32) + self.from_left.astype(F32)).astype(BF)
            to_left = (to_left.astype(F32) + self.from_right.astype(F32)).astype(BF)
        return [
            (to_right, "tensor", [(k, k + 1) for k in range(t)]),
            (to_left, "tensor", [(count - 1 - k, count - 2 - k) for k in range(t)]),
        ]

    def take(self, moved):
        self.from_left, self.from_right = moved
        self.step += 1

    def result(self):
        own = self.pick(lax.axis_index("tensor"))
        return own.astype(F32) + self.from_left.astype(F32) + self.from_right.astype(F32)


class LineGather:
    def __init__(self, own):
        self.own = self.right = self.left = own
        self.step = 1
        self.from_left, self.from_right = {}, {}

    def sends(self):
        count, t = lax.axis_size("tensor"), self.step
        steps = range(t - 1, count - 1)
        return [
            (self.right, "tensor", [(k, k + 1) for k in steps]),
            (self.left, "tensor", [(count - 1 - k, count - 2 - k) for k in steps]),
        ]

    def take(self, moved):
        self.right, self.left = moved
        self.from_left[self.step], self.from_right[self.step] = moved
        self.step += 1

    def result(self):
        count = lax.axis_size("tensor")
        steps = range(1, count)
        return place_call(
            self.own, [self.from_left[t] for t in steps], [self.from_right[t] for t in steps]
        )


class Both:
    def __init__(self, gather, total):
        self.gather, self.total = gather, total

    def sends(self):
        me, count = lax.axis_index("tensor"), lax.axis_size("tensor")
        first = self.gather.step - 1
        out = []
        for rank, whole, part in zip(
            (me, count - 1 - me), self.gather.sends(), self.total.sends()
        ):
            value = jnp.where(rank >= first, whole[0], part[0])
            out.append((value, "tensor", sorted(whole[2] + part[2])))
        return out

    def take(self, moved):
        self.gather.take(moved)
        self.total.take(moved)


FLIP = [(0, 1), (1, 0)]


class NearGather:
    def __init__(self, shard):
        self.shard = shard
        self.step = 1
        self.near = lax.axis_size("fsdp") == 2 and lax.axis_size("yy") == 2

    def sends(self):
        if not self.near:
            return []
        half = self.shard.shape[0] // 2
        if self.step == 1:
            return [(self.shard, "fsdp", FLIP), (self.shard, "yy", FLIP)]
        if self.step == 2:
            return [(self.by_y[:half], "fsdp", FLIP), (self.by_x[half:], "yy", FLIP)]
        self.mine = jnp.concatenate([self.shard, self.by_y, self.by_x, self.lo, self.hi], axis=0)
        return [(self.mine, "core", FLIP)]

    def take(self, moved):
        if self.near:
            if self.step == 1:
                self.by_x, self.by_y = moved
            elif self.step == 2:
                self.lo, self.hi = moved
            else:
                (self.other,) = moved
        self.step += 1

    def result(self):
        if not self.near:
            return lax.all_gather(self.shard, ("fsdp", "yy", "core"), axis=0, tiled=True)
        return spread_call(self.mine, self.other)


class KeyExchange:
    def __init__(self, kv):
        self.kv = kv
        self.step = 1

    def sends(self):
        if self.step == 1:
            return [(self.kv, "yy", FLIP), (self.kv, "core", FLIP)]
        return [(self.kv2, "core", FLIP)]

    def take(self, moved):
        if self.step == 1:
            self.kv2, self.kv1 = moved
        else:
            (self.kv3,) = moved
        self.step += 1

    def result(self):
        return self.kv, self.kv1, self.kv2, self.kv3


class Butterfly:
    def __init__(self, value, axes):
        self.value = value
        self.moves = []
        for axis in axes:
            bit = 1
            while bit < lax.axis_size(axis):
                self.moves.append((axis, pairs(lax.axis_size(axis), bit)))
                bit *= 2

    def sends(self):
        axis, pattern = self.moves.pop(0)
        return [(self.value, axis, pattern)]

    def take(self, moved):
        self.value = self.value + moved[0]


class Clock:
    def __init__(self):
        self.last = ()

    def expect(self, value):
        self.last += (value,)

    def slot(self, tasks, work=None, args=(), launch=None, grad=None):
        sends = [task.sends() for task in tasks]
        flat = [send for group in sends for send in group]
        before = len(self.last)
        extra = () if launch is None else (grad,)
        gated = lax.optimization_barrier(
            tuple(self.last) + tuple(s[0] for s in flat) + tuple(args) + extra
        )[before:]
        if launch is not None:
            self.launched = launch(gated[-1])
        moved = [lax.ppermute(g, s[1], s[2]) for g, s in zip(gated, flat)]
        done = tuple(work(*gated[len(flat) : len(flat) + len(args)])) if work else ()
        self.last = tuple(moved) + done
        at = 0
        for task, group in zip(tasks, sends):
            task.take(moved[at : at + len(group)])
            at += len(group)
        return done


def pairs(count, bit):
    return [(k, k ^ bit) for k in range(count)]


def turn(values, cosine, sine):
    lane = lax.broadcasted_iota(jnp.int32, values.shape, 1)
    swapped = jnp.where(
        lax.rem(lane, 64) < 32, pltpu.roll(values, 96, 1), pltpu.roll(values, 32, 1)
    )
    return values * cosine + swapped * sine


def place_kernel(count, me_ref, *refs):
    own, from_left, from_right = refs[0], refs[1:count], refs[count : 2 * count - 1]
    out = refs[2 * count - 1]
    me = me_ref[0]
    for k in range(count):
        todo = [(me == k, own)]
        for t in range(1, count):
            if k + t < count:
                todo.append((me == k + t, from_left[t - 1]))
            if k - t >= 0:
                todo.append((me == k - t, from_right[t - 1]))
        for chosen, source in todo:

            @pl.when(chosen)
            def _(source=source, k=k):
                out[k] = source[...]


def place_call(own, from_left, from_right):
    count = len(from_left) + 1
    rows, width = own.shape
    tile = min(64, rows)
    me = lax.axis_index("tensor").astype(jnp.int32)[None]
    return pl.pallas_call(
        functools.partial(place_kernel, count),
        grid_spec=pltpu.PrefetchScalarGridSpec(
            num_scalar_prefetch=1,
            grid=(rows // tile,),
            in_specs=[pl.BlockSpec((tile, width), lambda i, p: (i, 0))] * (2 * count - 1),
            out_specs=pl.BlockSpec((count, tile, width), lambda i, p: (0, i, 0)),
        ),
        out_shape=jax.ShapeDtypeStruct((count,) + own.shape, own.dtype),
        cost_estimate=pl.CostEstimate(
            flops=0, bytes_accessed=6 * count * own.size, transcendentals=0
        ),
        name="place",
    )(me, own, *from_left, *from_right)


def spread_kernel(at_ref, mine_ref, other_ref, out_ref):
    for core in range(2):

        @pl.when(at_ref[1] == core)
        def _(core=core):
            out_ref[0, core] = mine_ref[0]
            out_ref[0, 1 - core] = other_ref[0]


def spread_call(mine, other):
    rows, width = mine.shape[0] // 4, mine.shape[1]
    chip = lax.axis_index("fsdp") * 2 + lax.axis_index("yy")
    at = jnp.stack([chip, lax.axis_index("core")]).astype(jnp.int32)
    block = pl.BlockSpec((1, rows, width), lambda i, at: (jnp.bitwise_xor(i, at[0]), 0, 0))
    out = pl.pallas_call(
        spread_kernel,
        grid_spec=pltpu.PrefetchScalarGridSpec(
            num_scalar_prefetch=1,
            grid=(4,),
            in_specs=[block, block],
            out_specs=pl.BlockSpec((1, 2, rows, width), lambda i, at: (i, 0, 0, 0)),
        ),
        out_shape=jax.ShapeDtypeStruct((4, 2, rows, width), mine.dtype),
        cost_estimate=pl.CostEstimate(
            flops=0, bytes_accessed=8 * mine.size, transcendentals=0
        ),
        name="spread",
    )(at, mine.reshape(4, rows, width), other.reshape(4, rows, width))
    return out.reshape(8 * rows, width)


def ffn_kernel(x_ref, cot_ref, g_ref, u_ref, d_ref, hidden_ref, d_gate_ref, d_up_ref):
    x = x_ref[...]
    gate = dot_plain(x, g_ref[...])
    up = dot_plain(x, u_ref[...])
    d_hidden = dot_plain(cot_ref[...], d_ref[...])
    sig = jax.nn.sigmoid(gate)
    act = gate * sig
    hidden_ref[...] = (act * up).astype(BF)
    d_up_ref[...] = (d_hidden * act).astype(BF)
    d_gate_ref[...] = (d_hidden * up * (sig * (1.0 + gate * (1.0 - sig)))).astype(BF)


def ffn_call(x, cot, g, u, d, chunk):
    rows, width = x.shape
    units = g.shape[1]
    tile = min(512, units)
    whole = pl.BlockSpec((rows, width), lambda i: (0, 0))
    rows_of = pl.BlockSpec((rows, width), lambda i: (chunk, 0))
    weight = pl.BlockSpec((width, tile), lambda i: (0, i))
    part = pl.BlockSpec((rows, tile), lambda i: (0, i))
    return pl.pallas_call(
        ffn_kernel,
        grid=(units // tile,),
        in_specs=[whole, rows_of, weight, weight, weight],
        out_specs=[part] * 3,
        out_shape=[jax.ShapeDtypeStruct((rows, units), BF)] * 3,
        cost_estimate=pl.CostEstimate(
            flops=6 * rows * width * units,
            bytes_accessed=6 * width * units + 6 * rows * units,
            transcendentals=rows * units,
        ),
        name="ffn",
    )(x, cot, g, u, d)


def product_kernel(count, turned, *refs):
    total = None
    for k in range(count):
        dot = dot_plain if turned else dot_cols
        part = dot(refs[k][...], refs[count + k][...])
        total = part if total is None else total + part
    refs[2 * count][...] = total.astype(BF)


def product_call(lefts, rights, turned):
    count = len(lefts)
    rows, depth = lefts[0].shape
    width = rights[0].shape[1 if turned else 0]
    tile = min(512 if turned else 256, width)
    weight = (
        pl.BlockSpec((depth, tile), lambda i: (0, i))
        if turned
        else pl.BlockSpec((tile, depth), lambda i: (i, 0))
    )
    return pl.pallas_call(
        functools.partial(product_kernel, count, turned),
        grid=(width // tile,),
        in_specs=[pl.BlockSpec((rows, depth), lambda i: (0, 0))] * count
        + [weight] * count,
        out_specs=pl.BlockSpec((rows, tile), lambda i: (0, i)),
        out_shape=jax.ShapeDtypeStruct((rows, width), BF),
        cost_estimate=pl.CostEstimate(
            flops=2 * count * rows * depth * width,
            bytes_accessed=2 * count * depth * (rows + width),
            transcendentals=0,
        ),
        name="product",
    )(*lefts, *rights)


def transpose_kernel(x_ref, out_ref):
    out_ref[...] = jnp.transpose(x_ref[...])


def transpose_call(x):
    rows, columns = x.shape
    tile = min(256, rows)
    return pl.pallas_call(
        transpose_kernel,
        grid=(rows // tile,),
        in_specs=[pl.BlockSpec((tile, columns), lambda i: (i, 0))],
        out_specs=pl.BlockSpec((columns, tile), lambda i: (0, i)),
        out_shape=jax.ShapeDtypeStruct((columns, rows), x.dtype),
        cost_estimate=pl.CostEstimate(
            flops=0, bytes_accessed=4 * x.size, transcendentals=0
        ),
        name="turn_over",
    )(x)


def turn_kernel(turned, x_ref, cos_ref, sin_ref, out_ref):
    cosine, sine = cos_ref[...], sin_ref[...]
    for begin in range(0, x_ref.shape[1], 128):
        piece = x_ref[:, begin : begin + 128].astype(F32)
        if begin < turned:
            piece = turn(piece, cosine, sine)
        out_ref[:, begin : begin + 128] = piece.astype(out_ref.dtype)


def turn_call(x, cosine, sine, turned):
    rows, width = x.shape
    tile = min(256, rows)
    return pl.pallas_call(
        functools.partial(turn_kernel, turned),
        grid=(rows // tile,),
        in_specs=[
            pl.BlockSpec((tile, width), lambda i: (i, 0)),
            pl.BlockSpec((tile, 128), lambda i: (i, 0)),
            pl.BlockSpec((tile, 128), lambda i: (i, 0)),
        ],
        out_specs=pl.BlockSpec((tile, width), lambda i: (i, 0)),
        out_shape=jax.ShapeDtypeStruct((rows, width), BF),
        cost_estimate=pl.CostEstimate(
            flops=4 * rows * width, bytes_accessed=6 * rows * width, transcendentals=0
        ),
        name="turn",
    )(x, cosine, sine)


def attend_kernel(
    group, place_ref, q_ref, k0, k1, k2, k3, segq_ref, segk_ref, out_ref, lse_ref
):
    block = q_ref.shape[1]
    kv_heads = k0.shape[2] // (2 * HD)
    me = place_ref[0]
    scale = LOG2E / math.sqrt(HD)
    row = lax.broadcasted_iota(jnp.int32, (block, block), 0)
    col = lax.broadcasted_iota(jnp.int32, (block, block), 1)
    seg_q = segq_ref[0]
    refs = (k0, k1, k2, k3)
    bias = []
    for k in range(len(refs)):
        there = place_ref[1 + k]
        seg_k = segk_ref[0, :, pl.ds(pl.multiple_of(there * block, block), block)]
        ahead = (there - me) * block
        allowed = (seg_q == seg_k) & (row >= col + ahead)
        bias.append(jnp.where(allowed, 0.0, NEG_FILL))
    sums = []
    for g in range(kv_heads):
        keys = [r[0, :, g * HD : (g + 1) * HD] for r in refs]
        values = [r[0, :, (kv_heads + g) * HD : (kv_heads + g + 1) * HD] for r in refs]
        for j in range(group):
            head = g * group + j
            q = q_ref[0, :, head * HD : (head + 1) * HD]
            scores = [
                dot_cols(q, keys[k]) * scale + bias[k] for k in range(len(refs))
            ]
            peak = functools.reduce(jnp.maximum, scores)
            peak = jnp.max(peak, axis=1, keepdims=True)
            weights = [jnp.exp2(s - peak) for s in scores]
            total = functools.reduce(jnp.add, weights)
            total = jnp.sum(total, axis=1, keepdims=True)
            mixed = functools.reduce(
                jnp.add, [dot_plain(w.astype(BF), v) for w, v in zip(weights, values)]
            )
            out_ref[0, :, head * HD : (head + 1) * HD] = (mixed / total).astype(BF)
            sums.append(peak + jnp.log2(total))
    lane = lax.broadcasted_iota(jnp.int32, (block, 128), 1)
    stacked = jnp.zeros((block, 128), F32)
    for head, value in enumerate(sums):
        stacked = jnp.where(lane == head, value, stacked)
    lse_ref[0] = jnp.transpose(stacked)[: len(sums)]


def attend_call(place, q, blocks, seg_q, seg_k):
    seqs, block, width = q.shape
    heads = width // HD
    kv_width = blocks[0].shape[2]
    group = heads // (kv_width // (2 * HD))
    seq_len = seg_k.shape[2]
    keys = pl.BlockSpec((1, block, kv_width), lambda s, p: (s, 0, 0))
    work = seqs * heads * block * seq_len
    return pl.pallas_call(
        functools.partial(attend_kernel, group),
        grid_spec=pltpu.PrefetchScalarGridSpec(
            num_scalar_prefetch=1,
            grid=(seqs,),
            in_specs=[
                pl.BlockSpec((1, block, width), lambda s, p: (s, 0, 0)),
                keys,
                keys,
                keys,
                keys,
                pl.BlockSpec((1, block, 1), lambda s, p: (s, 0, 0)),
                pl.BlockSpec((1, 1, seq_len), lambda s, p: (s, 0, 0)),
            ],
            out_specs=[
                pl.BlockSpec((1, block, width), lambda s, p: (s, 0, 0)),
                pl.BlockSpec((1, heads, block), lambda s, p: (s, 0, 0)),
            ],
        ),
        out_shape=[
            jax.ShapeDtypeStruct((seqs, block, width), BF),
            jax.ShapeDtypeStruct((seqs, heads, block), F32),
        ],
        cost_estimate=pl.CostEstimate(
            flops=4 * work * HD * 4, bytes_accessed=6 * q.size, transcendentals=work
        ),
        name="attend",
    )(place, q, *blocks, seg_q, seg_k)


def attend_back_kernel(
    group,
    place_ref,
    q_ref,
    k0,
    k1,
    k2,
    k3,
    segq_ref,
    segk_ref,
    out_ref,
    grad_ref,
    lse_ref,
    dq_ref,
    d0,
    d1,
    d2,
    d3,
    bias_ref,
    dsc_ref,
):
    block = q_ref.shape[1]
    kv_heads = k0.shape[2] // (2 * HD)
    me = place_ref[0]
    scale = LOG2E / math.sqrt(HD)
    back_scale = 1.0 / math.sqrt(HD)
    refs, d_refs = (k0, k1, k2, k3), (d0, d1, d2, d3)
    key_row = lax.broadcasted_iota(jnp.int32, (block, block), 0)
    q_col = lax.broadcasted_iota(jnp.int32, (block, block), 1)
    seg_q = segq_ref[0]
    for k in range(len(refs)):
        there = place_ref[1 + k]
        seg_k = segk_ref[0, pl.ds(pl.multiple_of(there * block, block), block), :]
        ahead = (there - me) * block
        allowed = (seg_q == seg_k) & (q_col >= key_row + ahead)
        bias_ref[k] = jnp.where(allowed, 0.0, NEG_FILL)
    width = group * block
    product = out_ref[0].astype(F32) * grad_ref[0].astype(F32)
    total_heads = kv_heads * group
    feature = lax.broadcasted_iota(jnp.int32, (total_heads, product.shape[1]), 1)
    owner = lax.broadcasted_iota(jnp.int32, (total_heads, product.shape[1]), 0)
    picks = jnp.where(feature // HD == owner, 1.0, 0.0).astype(F32)
    deltas = lax.dot_general(
        picks,
        product,
        (((1,), (1,)), ((), ())),
        preferred_element_type=F32,
        precision=lax.Precision.HIGHEST,
    )
    for g in range(kv_heads):
        heads = range(g * group, (g + 1) * group)
        q = jnp.concatenate([q_ref[0, :, h * HD : (h + 1) * HD] for h in heads], 0)
        grad = jnp.concatenate([grad_ref[0, :, h * HD : (h + 1) * HD] for h in heads], 0)
        d_query = None
        for k in range(len(refs)):
            keys = refs[k][0, :, g * HD : (g + 1) * HD]
            values = refs[k][0, :, (kv_heads + g) * HD : (kv_heads + g + 1) * HD]
            scores = dot_cols(keys, q)
            d_probs = dot_cols(values, grad)
            probs_low = []
            for j, h in enumerate(heads):
                cols = slice(j * block, (j + 1) * block)
                probs = jnp.exp2(
                    scores[:, cols] * scale + (bias_ref[k] - lse_ref[0, h : h + 1, :])
                )
                probs_low.append(probs.astype(BF))
                dsc_ref[:, cols] = (
                    probs * (d_probs[:, cols] - deltas[h : h + 1, :])
                ).astype(BF)
            d_scores = dsc_ref[...]
            d_value = dot_plain(jnp.concatenate(probs_low, 1), grad)
            d_key = dot_plain(d_scores, q) * back_scale
            d_refs[k][0, :, g * HD : (g + 1) * HD] = d_key.astype(BF)
            d_refs[k][0, :, (kv_heads + g) * HD : (kv_heads + g + 1) * HD] = d_value.astype(BF)
            part = dot_rows(d_scores, keys)
            d_query = part if d_query is None else d_query + part
        d_query = d_query * back_scale
        for j, h in enumerate(heads):
            dq_ref[0, :, h * HD : (h + 1) * HD] = d_query[j * block : (j + 1) * block].astype(BF)


def attend_back_call(place, q, blocks, seg_q, seg_k, out, grad, lse):
    seqs, block, width = q.shape
    heads = width // HD
    kv_width = blocks[0].shape[2]
    group = heads // (kv_width // (2 * HD))
    seq_len = seg_k.shape[1]
    keys = pl.BlockSpec((1, block, kv_width), lambda s, p: (s, 0, 0))
    rows = pl.BlockSpec((1, block, width), lambda s, p: (s, 0, 0))
    work = seqs * heads * block * seq_len
    return pl.pallas_call(
        functools.partial(attend_back_kernel, group),
        grid_spec=pltpu.PrefetchScalarGridSpec(
            num_scalar_prefetch=1,
            grid=(seqs,),
            in_specs=[
                rows,
                keys,
                keys,
                keys,
                keys,
                pl.BlockSpec((1, 1, block), lambda s, p: (s, 0, 0)),
                pl.BlockSpec((1, seq_len, 1), lambda s, p: (s, 0, 0)),
                rows,
                rows,
                pl.BlockSpec((1, heads, block), lambda s, p: (s, 0, 0)),
            ],
            out_specs=[rows, keys, keys, keys, keys],
            scratch_shapes=[
                pltpu.VMEM((4, block, block), F32),
                pltpu.VMEM((block, group * block), BF),
            ],
        ),
        out_shape=[jax.ShapeDtypeStruct(q.shape, BF)]
        + [jax.ShapeDtypeStruct(blocks[0].shape, BF)] * 4,
        cost_estimate=pl.CostEstimate(
            flops=10 * work * HD * 4, bytes_accessed=12 * q.size, transcendentals=work
        ),
        name="attend_back",
    )(place, q, *blocks, seg_q, seg_k, out, grad, lse)


def inverse_rms(values):
    return lax.rsqrt(jnp.mean(values * values, axis=-1, keepdims=True) + EPSILON)


def norm_back(values, gain, incoming):
    scale = inverse_rms(values)
    gain_terms = jnp.sum(incoming * values * scale, axis=0)
    weighted = incoming * gain
    inner = jnp.mean(weighted * values, axis=-1, keepdims=True)
    return scale * weighted - values * (scale * scale * scale) * inner, gain_terms


def per_device(
    tokens,
    segments,
    q_weight,
    k_weight,
    v_weight,
    o_weight,
    attn_gain,
    gate_weight,
    up_weight,
    down_weight,
    ffn_gain,
    cotangent,
):
    heads_axes = ("yy", "core")
    seqs, block, width = tokens.shape
    seq_len = segments.shape[1]
    parts = lax.axis_size(heads_axes)
    ways = lax.axis_size("tensor")
    owners = ("fsdp",) + heads_axes
    here = lax.axis_index(heads_axes)
    me = lax.axis_index("tensor")
    q_width, k_width = q_weight.shape[1], k_weight.shape[1]
    kv_width = 2 * k_width
    qkv_width = q_width + kv_width
    per_chunk = seqs // CHUNKS
    rows = per_chunk * block
    own_rows = rows // ways

    clock = Clock()
    slot = clock.slot
    where_all = positions(segments)
    where_here = lax.dynamic_slice_in_dim(where_all, here * block, block, 1)
    seg_here = lax.dynamic_slice_in_dim(segments, here * block, block, 1)
    lane = np.arange(128)
    frequency = jnp.asarray(
        ROPE_BASE ** (-2.0 * (np.arange(128) % 32).astype(np.float32) / HD), F32
    )
    angles = where_here.reshape(seqs * block, 1).astype(F32) * frequency
    cosine = jnp.cos(angles)
    sine = jnp.sin(angles) * jnp.asarray(np.where(lane % 64 < 32, -1.0, 1.0), F32)
    place = jnp.stack([here] + [here ^ k for k in range(parts)]).astype(jnp.int32)

    def chunk_of(x, c):
        return lax.slice_in_dim(x, c * per_chunk, (c + 1) * per_chunk, axis=0)

    def own(x):
        return lax.dynamic_slice_in_dim(x, me * own_rows, own_rows, 0)

    def blocks(x):
        return x.reshape(ways, own_rows, width)

    state = []
    for c in range(CHUNKS):
        s = {}
        tok = chunk_of(tokens, c).reshape(rows, width)
        s["tok"] = tok
        s["cot"] = chunk_of(cotangent, c).reshape(rows, width)
        s["cos"] = lax.slice_in_dim(cosine, c * rows, (c + 1) * rows, axis=0)
        s["sin"] = lax.slice_in_dim(sine, c * rows, (c + 1) * rows, axis=0)
        s["sin_back"] = -s["sin"]
        s["scale_one"] = inverse_rms(tok.astype(F32))
        seg_q, seg_k = chunk_of(seg_here, c), chunk_of(segments, c)
        s["seg_fwd"] = (seg_q[:, :, None], seg_k[:, None, :])
        s["seg_back"] = (seg_q[:, None, :], seg_k[:, :, None])
        state.append(s)
    first, second = state

    pad = jnp.zeros((q_weight.shape[0], 126), BF)
    packed = jnp.concatenate(
        [q_weight, o_weight, k_weight, v_weight, attn_gain[:, None], ffn_gain[:, None], pad],
        axis=1,
    )

    def gathered(shard):
        return lax.all_gather(shard, owners, axis=0, tiled=True)

    gather_near = NearGather(packed)
    slot([gather_near])
    for s in state:
        for name in ("cos", "sin", "sin_back", "scale_one"):
            clock.expect(s[name])
        for name in ("seg_fwd", "seg_back"):
            clock.last += s[name]
    clock.expect(place)
    slot([gather_near])
    slot([gather_near], lambda *shards: shards, (gate_weight, up_weight, down_weight))
    gate_weight, up_weight, down_weight = clock.last[-3:]
    full_g = gathered(gate_weight)
    full_u = gathered(up_weight)
    full_d = gathered(down_weight)
    packed = gather_near.result()
    at = 0
    columns = []
    for wide in (q_width, q_width, kv_width, 2):
        columns.append(packed[:, at : at + wide])
        at += wide
    full_q, full_o, full_kv, gains = columns
    gains = gains.T.astype(F32)
    gain_one, gain_two = gains[0:1], gains[1:2]

    def project_kv(s, tok):
        normed = (tok.astype(F32) * s["scale_one"] * gain_one).astype(BF)
        kv = turn_call(dot_plain(normed, full_kv), s["cos"], s["sin"], k_width)
        return normed, kv.reshape(per_chunk, block, kv_width)

    def project_q(s, normed):
        q = turn_call(dot_plain(normed, full_q), s["cos"], s["sin"], q_width)
        return (q.reshape(per_chunk, block, q_width),)

    def project(s, tok):
        normed, kv = project_kv(s, tok)
        return (normed, kv) + project_q(s, normed)

    def attend(s, q, *kv):
        attended, lse = attend_call(place, q, kv, *s["seg_fwd"])
        s["attended"], s["lse"] = attended, lse
        attn = dot_cols(attended.reshape(rows, q_width), full_o).astype(BF)
        return attended, lse, attn

    def enter_ffn(s, summed):
        s["residual"] = own(s["tok"]).astype(F32) + summed
        return (s["residual"] * inverse_rms(s["residual"]) * gain_two).astype(BF)

    turned = {}

    def turn_over(weight):
        return (transpose_call(weight),)

    cot_rows = cotangent.reshape(seqs * block, width)

    def ffn_mid(chunk, normed_two):
        return ffn_call(normed_two, cot_rows, full_g, full_u, full_d, chunk)

    def ffn_back(d_gate, d_up):
        return (product_call((d_gate, d_up), (turned["g"], turned["u"]), True),)

    def ffn_out(hidden):
        return (product_call((hidden,), (full_d,), False),)

    def leave_ffn(s, summed):
        d_norm, s["gain_two"] = norm_back(s["residual"], gain_two, summed)
        s["d_resid"] = own(s["cot"]).astype(F32) + d_norm
        return s["d_resid"].astype(BF)

    def attend_back(s, d_attn):
        d_attended = dot_plain(d_attn, full_o).astype(BF).reshape(per_chunk, block, q_width)
        return attend_back_call(
            place, s["q"], s["kv"], *s["seg_back"], s["attended"], d_attended, s["lse"]
        )

    def project_back(s, dq, b0, b1, b2, b3):
        from3 = lax.ppermute(b3, "core", FLIP)
        from1 = lax.ppermute(b1, "core", FLIP)
        far = (b2.astype(F32) + from3.astype(F32)).astype(BF)
        from2 = lax.ppermute(far, "yy", FLIP)
        d_kv = b0.astype(F32) + from1.astype(F32) + from2.astype(F32)
        d_q = turn_call(dq.reshape(rows, q_width), s["cos"], s["sin_back"], q_width)
        d_kv = turn_call(d_kv.reshape(rows, kv_width), s["cos"], s["sin_back"], k_width)
        d_qkv = jnp.concatenate([d_q, d_kv], axis=1)
        full_qkv = jnp.concatenate([full_q, full_kv], axis=1)
        return d_qkv, dot_cols(d_qkv, full_qkv).astype(BF)

    def leave_attention(s, summed):
        d_norm, s["gain_one"] = norm_back(own(s["tok"]).astype(F32), gain_one, summed)
        return (s["d_resid"] + d_norm).astype(BF)

    def scattered(grad):
        return lax.psum_scatter(grad, owners, scatter_dimension=0, tiled=True)

    def weight_grad(*halves):
        left = jnp.concatenate(halves[:-CHUNKS], axis=0)
        right = jnp.concatenate(halves[-CHUNKS:], axis=0)
        return (dot_rows(left, right).astype(BF),)

    def of_both(*names):
        return tuple(s[name] for name in names for s in state)

    def whole(rows_of):
        return rows_of.reshape(per_chunk, block, width)

    def leave_layer(s, ffn):
        mine = own(ffn).astype(F32) + s["residual"]
        ffn = lax.dynamic_update_slice_in_dim(ffn, mine.astype(BF), me * own_rows, 0)
        s["output"] = lax.psum(ffn, "tensor")

    axes = ("tensor", "core", "yy", "fsdp")
    first["normed_one"], kv = slot(
        [], functools.partial(project_kv, first), (first["tok"],)
    )
    keys = KeyExchange(kv)
    (first["q"],) = slot(
        [keys], functools.partial(project_q, first), (first["normed_one"],)
    )
    slot([keys])
    first["kv"] = keys.result()
    first["attended"], first["lse"], attn = slot(
        [], functools.partial(attend, first), (first["q"],) + first["kv"]
    )
    sum_a0 = LineSum(blocks(attn))
    second["normed_one"], kv, second["q"] = slot(
        [sum_a0], functools.partial(project, second), (second["tok"],)
    )
    keys = KeyExchange(kv)
    slot([sum_a0, keys])
    slot([sum_a0, keys])
    second["kv"] = keys.result()
    gather_a0 = LineGather(enter_ffn(first, sum_a0.result()))
    second["attended"], second["lse"], attn = slot(
        [gather_a0], functools.partial(attend, second), (second["q"],) + second["kv"]
    )
    sum_a1 = LineSum(blocks(attn))
    (turned["g"],) = slot([Both(gather_a0, sum_a1)], turn_over, (full_g,))
    (turned["u"],) = slot([Both(gather_a0, sum_a1)], turn_over, (full_u,))
    first["normed_two"] = gather_a0.result().reshape(rows, width)
    first["hidden"], first["d_gate"], first["d_up"] = slot(
        [sum_a1], functools.partial(ffn_mid, 0), (first["normed_two"],)
    )
    gather_a1 = LineGather(enter_ffn(second, sum_a1.result()))
    (back,) = slot([gather_a1], ffn_back, (first["d_gate"], first["d_up"]))
    sum_d0 = LineSum(blocks(back))
    (ffn,) = slot([Both(gather_a1, sum_d0)], ffn_out, (first["hidden"],))
    leave_layer(first, ffn)
    slot([Both(gather_a1, sum_d0)])
    second["normed_two"] = gather_a1.result().reshape(rows, width)
    second["hidden"], second["d_gate"], second["d_up"] = slot(
        [sum_d0], functools.partial(ffn_mid, 1), (second["normed_two"],)
    )
    gather_d0 = LineGather(leave_ffn(first, sum_d0.result()))
    (back,) = slot([gather_d0], ffn_back, (second["d_gate"], second["d_up"]))
    sum_d1 = LineSum(blocks(back))
    (grad,) = slot(
        [Both(gather_d0, sum_d1)],
        weight_grad,
        (cot_rows,) + of_both("hidden"),
    )
    (grad,) = slot(
        [Both(gather_d0, sum_d1)],
        weight_grad,
        of_both("normed_two", "d_gate"),
        scattered,
        grad,
    )
    down_grad = clock.launched
    first["d_attn"] = gather_d0.result().reshape(rows, width)
    pieces = slot(
        [sum_d1], functools.partial(attend_back, first), (first["d_attn"],), scattered, grad
    )
    gate_grad = clock.launched
    gather_d1 = LineGather(leave_ffn(second, sum_d1.result()))
    first["d_qkv"], back = slot(
        [gather_d1], functools.partial(project_back, first), pieces
    )
    sum_n0 = LineSum(blocks(back))
    (grad,) = slot(
        [Both(gather_d1, sum_n0)], weight_grad, of_both("normed_two", "d_up")
    )
    slot([Both(gather_d1, sum_n0)], None, (), scattered, grad)
    up_grad = clock.launched
    second["d_attn"] = gather_d1.result().reshape(rows, width)
    pieces = slot(
        [sum_n0], functools.partial(attend_back, second), (second["d_attn"],)
    )
    gather_n0 = LineGather(leave_attention(first, sum_n0.result()))
    second["d_qkv"], back = slot(
        [gather_n0], functools.partial(project_back, second), pieces
    )
    sum_n1 = LineSum(blocks(back))
    clock.expect(first["output"])
    (grad,) = slot(
        [Both(gather_n0, sum_n1)], weight_grad, of_both("normed_one", "d_qkv")
    )
    qkv_part = grad
    for s in state:
        s["attended_rows"] = s["attended"].reshape(rows, q_width)
    (grad,) = slot(
        [Both(gather_n0, sum_n1)],
        weight_grad,
        of_both("d_attn", "attended_rows"),
        scattered,
        qkv_part,
    )
    qkv_grad = clock.launched
    first["input_grad"] = gather_n0.result()
    (ffn,) = slot([sum_n1], ffn_out, (second["hidden"],), scattered, grad)
    sum_f1 = LineSum(blocks(ffn))
    o_grad = clock.launched
    gather_n1 = LineGather(leave_attention(second, sum_n1.result()))
    gains_one = Butterfly(
        jnp.stack([sum(s[name] for s in state) for name in ("gain_one", "gain_two")]), axes
    )
    slot([gather_n1, gains_one])
    slot([Both(gather_n1, sum_f1), gains_one])
    clock.expect(whole(first["input_grad"]))
    slot([Both(gather_n1, sum_f1), gains_one])
    second["input_grad"] = gather_n1.result()
    clock.expect(down_grad)
    slot([sum_f1, gains_one])
    input_grad = jnp.concatenate([whole(s["input_grad"]) for s in state], axis=0).astype(F32)
    gather_f1 = LineGather((second["residual"] + sum_f1.result()).astype(BF))
    clock.expect(gate_grad)
    slot([gather_f1, gains_one])
    clock.expect(input_grad)
    down_grad, gate_grad = down_grad.astype(F32), gate_grad.astype(F32)
    clock.expect(up_grad)
    slot([gather_f1])
    clock.expect(down_grad)
    clock.expect(gate_grad)
    up_grad = up_grad.astype(F32)
    clock.expect(up_grad)
    slot([gather_f1])
    second["output"] = gather_f1.result()
    while gains_one.moves:
        slot([gains_one])

    qkv_grad, o_grad = qkv_grad.astype(F32), o_grad.astype(F32)
    share = attn_gain.shape[0]
    index = lax.axis_index("fsdp") * parts + here

    def owned(gain):
        return lax.dynamic_slice_in_dim(gain, index * share, share, 0)

    gain_one_grad, gain_two_grad = gains_one.value

    return (
        jnp.concatenate([whole(s["output"]) for s in state], axis=0),
        input_grad,
        qkv_grad[:, :q_width],
        qkv_grad[:, q_width : q_width + k_width],
        qkv_grad[:, q_width + k_width :],
        o_grad,
        owned(gain_one_grad),
        gate_grad,
        up_grad,
        down_grad,
        owned(gain_two_grad),
    )


def solution(mesh):
    sizes = mesh.shape
    split = (sizes["fsdp"], sizes["heads"] // 2, 2, sizes["tensor"])
    mesh = jax.sharding.Mesh(mesh.devices.reshape(split), ("fsdp", "yy", "core", "tensor"))
    heads = ("yy", "core")
    rows = P("fsdp", heads, None)
    matrix = P(("fsdp",) + heads, "tensor")
    vector = P(("fsdp",) + heads)
    return jax.shard_map(
        per_device,
        mesh=mesh,
        in_specs=(
            rows,
            P("fsdp", None),
            matrix,
            matrix,
            matrix,
            matrix,
            vector,
            matrix,
            matrix,
            matrix,
            vector,
            rows,
        ),
        out_specs=(
            rows,
            rows,
            matrix,
            matrix,
            matrix,
            matrix,
            vector,
            matrix,
            matrix,
            matrix,
            vector,
        ),
        check_vma=False,
    )
```

```python
import functools
import math

import jax
import jax.numpy as jnp
import numpy as np
from jax import lax
from jax.experimental import pallas as pl
from jax.experimental.pallas import tpu as pltpu
from jax.sharding import PartitionSpec as P

HD = 64
EPSILON = 1e-05
ROPE_BASE = 500000.0
NEG_FILL = -1e30
LOG2E = math.log2(math.e)
BF = jnp.bfloat16
F32 = jnp.float32
CHUNKS = 2


def positions(segments):
    length_of = segments.shape[-1]
    column = jnp.arange(length_of, dtype=jnp.int32)
    before = jnp.concatenate([segments[..., :1] - 1, segments[..., :-1]], axis=-1)
    firsts = jnp.where(segments != before, column, jnp.zeros_like(column))
    starts = lax.cummax(firsts, axis=firsts.ndim - 1)
    return column - starts


def dot_plain(left_in, right_in):
    return jnp.dot(left_in, right_in, preferred_element_type=F32)


def dot_rows(left_in, right_in):
    return lax.dot_general(
        left_in, right_in, (((0,), (0,)), ((), ())), preferred_element_type=F32
    )


def dot_cols(left_in, right_in):
    return lax.dot_general(
        left_in, right_in, (((1,), (1,)), ((), ())), preferred_element_type=F32
    )


class LineSum:
    def __init__(self, parts):
        self.parts = parts
        self.step = 1
        self.from_left = self.from_right = None

    def pick(self, j):
        last = self.parts.shape[0] - 1
        return lax.dynamic_index_in_dim(self.parts, jnp.clip(j, 0, last), 0, keepdims=False)

    def sends(self):
        count, t = self.parts.shape[0], self.step
        me = lax.axis_index("tensor")
        to_right = self.pick(count - t + me)
        to_left = self.pick(t + me - count)
        if self.from_left is not None:
            to_right = (to_right.astype(F32) + self.from_left.astype(F32)).astype(BF)
            to_left = (to_left.astype(F32) + self.from_right.astype(F32)).astype(BF)
        return [
            (to_right, "tensor", [(k, k + 1) for k in range(t)]),
            (to_left, "tensor", [(count - 1 - k, count - 2 - k) for k in range(t)]),
        ]

    def take(self, moved):
        self.from_left, self.from_right = moved
        self.step += 1

    def result(self):
        own = self.pick(lax.axis_index("tensor"))
        return own.astype(F32) + self.from_left.astype(F32) + self.from_right.astype(F32)


class LineGather:
    def __init__(self, own):
        self.own = self.right = self.left = own
        self.step = 1
        self.from_left, self.from_right = {}, {}

    def sends(self):
        count, t = lax.axis_size("tensor"), self.step
        steps = range(t - 1, count - 1)
        return [
            (self.right, "tensor", [(k, k + 1) for k in steps]),
            (self.left, "tensor", [(count - 1 - k, count - 2 - k) for k in steps]),
        ]

    def take(self, moved):
        self.right, self.left = moved
        self.from_left[self.step], self.from_right[self.step] = moved
        self.step += 1

    def result(self):
        count = lax.axis_size("tensor")
        steps = range(1, count)
        return place_call(
            self.own, [self.from_left[t] for t in steps], [self.from_right[t] for t in steps]
        )


class Both:
    def __init__(self, gather, total):
        self.gather, self.total = gather, total

    def sends(self):
        me, count = lax.axis_index("tensor"), lax.axis_size("tensor")
        first = self.gather.step - 1
        out = []
        for rank, whole, part in zip(
            (me, count - 1 - me), self.gather.sends(), self.total.sends()
        ):
            value = jnp.where(rank >= first, whole[0], part[0])
            out.append((value, "tensor", sorted(whole[2] + part[2])))
        return out

    def take(self, moved):
        self.gather.take(moved)
        self.total.take(moved)


FLIP = [(0, 1), (1, 0)]


class NearGather:
    def __init__(self, shard):
        self.shard = shard
        self.step = 1
        self.near = lax.axis_size("fsdp") == 2 and lax.axis_size("yy") == 2

    def sends(self):
        if not self.near:
            return []
        half = self.shard.shape[0] // 2
        if self.step == 1:
            return [(self.shard, "fsdp", FLIP), (self.shard, "yy", FLIP)]
        if self.step == 2:
            return [(self.by_y[:half], "fsdp", FLIP), (self.by_x[half:], "yy", FLIP)]
        self.mine = jnp.concatenate([self.shard, self.by_y, self.by_x, self.lo, self.hi], axis=0)
        return [(self.mine, "core", FLIP)]

    def take(self, moved):
        if self.near:
            if self.step == 1:
                self.by_x, self.by_y = moved
            elif self.step == 2:
                self.lo, self.hi = moved
            else:
                (self.other,) = moved
        self.step += 1

    def result(self):
        if not self.near:
            return lax.all_gather(self.shard, ("fsdp", "yy", "core"), axis=0, tiled=True)
        return spread_call(self.mine, self.other)


class KeyExchange:
    def __init__(self, kv):
        self.kv = kv
        self.step = 1

    def sends(self):
        if self.step == 1:
            return [(self.kv, "yy", FLIP), (self.kv, "core", FLIP)]
        return [(self.kv2, "core", FLIP)]

    def take(self, moved):
        if self.step == 1:
            self.kv2, self.kv1 = moved
        else:
            (self.kv3,) = moved
        self.step += 1

    def result(self):
        return self.kv, self.kv1, self.kv2, self.kv3


class Butterfly:
    def __init__(self, value, axes):
        self.value = value
        self.moves = []
        for axis in axes:
            bit = 1
            while bit < lax.axis_size(axis):
                self.moves.append((axis, pairs(lax.axis_size(axis), bit)))
                bit *= 2

    def sends(self):
        axis, pattern = self.moves.pop(0)
        return [(self.value, axis, pattern)]

    def take(self, moved):
        self.value = self.value + moved[0]


class Clock:
    def __init__(self):
        self.last = ()

    def expect(self, value):
        self.last += (value,)

    def slot(self, tasks, work=None, args=(), launch=None, grad=None):
        sends = [task.sends() for task in tasks]
        flat = [send for group in sends for send in group]
        before = len(self.last)
        extra = () if launch is None else (grad,)
        gated = lax.optimization_barrier(
            tuple(self.last) + tuple(s[0] for s in flat) + tuple(args) + extra
        )[before:]
        if launch is not None:
            self.launched = launch(gated[-1])
        moved = [lax.ppermute(g, s[1], s[2]) for g, s in zip(gated, flat)]
        done = tuple(work(*gated[len(flat) : len(flat) + len(args)])) if work else ()
        self.last = tuple(moved) + done
        at = 0
        for task, group in zip(tasks, sends):
            task.take(moved[at : at + len(group)])
            at += len(group)
        return done


def pairs(count, bit):
    return [(k, k ^ bit) for k in range(count)]


def turn(values, cosine, sine):
    lane = lax.broadcasted_iota(jnp.int32, values.shape, 1)
    swapped = jnp.where(
        lax.rem(lane, 64) < 32, pltpu.roll(values, 96, 1), pltpu.roll(values, 32, 1)
    )
    return values * cosine + swapped * sine


def turn_back_kernel(k_width, dq_ref, b0_ref, b1_ref, b2_ref, cos_ref, sin_ref, out_ref):
    cosine, sine = cos_ref[...], sin_ref[...]
    q_width = dq_ref.shape[1]
    for begin in range(0, q_width, 128):
        piece = dq_ref[:, begin : begin + 128].astype(F32)
        out_ref[:, begin : begin + 128] = turn(piece, cosine, sine).astype(BF)
    for begin in range(0, b0_ref.shape[1], 128):
        piece = sum(
            ref[:, begin : begin + 128].astype(F32) for ref in (b0_ref, b1_ref, b2_ref)
        )
        if begin < k_width:
            piece = turn(piece, cosine, sine)
        out_ref[:, q_width + begin : q_width + begin + 128] = piece.astype(BF)


def turn_back_call(dq, parts, cosine, sine, k_width):
    rows, q_width = dq.shape
    kv_width = parts[0].shape[1]
    tile = min(256, rows)

    def tall(wide):
        return pl.BlockSpec((tile, wide), lambda i: (i, 0))

    return pl.pallas_call(
        functools.partial(turn_back_kernel, k_width),
        grid=(rows // tile,),
        in_specs=[tall(q_width)] + [tall(kv_width)] * 3 + [tall(128)] * 2,
        out_specs=tall(q_width + kv_width),
        out_shape=jax.ShapeDtypeStruct((rows, q_width + kv_width), BF),
        cost_estimate=pl.CostEstimate(
            flops=4 * rows * (q_width + kv_width),
            bytes_accessed=4 * rows * (q_width + 2 * kv_width),
            transcendentals=0,
        ),
        name="turn_back",
    )(dq, *parts, cosine, sine)


def place_kernel(count, me_ref, *refs):
    own, from_left, from_right = refs[0], refs[1:count], refs[count : 2 * count - 1]
    out = refs[2 * count - 1]
    me = me_ref[0]
    for k in range(count):
        todo = [(me == k, own)]
        for t in range(1, count):
            if k + t < count:
                todo.append((me == k + t, from_left[t - 1]))
            if k - t >= 0:
                todo.append((me == k - t, from_right[t - 1]))
        for chosen, source in todo:

            @pl.when(chosen)
            def _(source=source, k=k):
                out[k] = source[...]


def place_call(own, from_left, from_right):
    count = len(from_left) + 1
    rows, width = own.shape
    tile = min(64, rows)
    me = lax.axis_index("tensor").astype(jnp.int32)[None]
    return pl.pallas_call(
        functools.partial(place_kernel, count),
        grid_spec=pltpu.PrefetchScalarGridSpec(
            num_scalar_prefetch=1,
            grid=(rows // tile,),
            in_specs=[pl.BlockSpec((tile, width), lambda i, p: (i, 0))] * (2 * count - 1),
            out_specs=pl.BlockSpec((count, tile, width), lambda i, p: (0, i, 0)),
        ),
        out_shape=jax.ShapeDtypeStruct((count,) + own.shape, own.dtype),
        cost_estimate=pl.CostEstimate(
            flops=0, bytes_accessed=6 * count * own.size, transcendentals=0
        ),
        name="place",
    )(me, own, *from_left, *from_right)


def spread_kernel(at_ref, mine_ref, other_ref, out_ref):
    for core in range(2):

        @pl.when(at_ref[1] == core)
        def _(core=core):
            out_ref[0, core] = mine_ref[0]
            out_ref[0, 1 - core] = other_ref[0]


def spread_call(mine, other):
    rows, width = mine.shape[0] // 4, mine.shape[1]
    chip = lax.axis_index("fsdp") * 2 + lax.axis_index("yy")
    at = jnp.stack([chip, lax.axis_index("core")]).astype(jnp.int32)
    block = pl.BlockSpec((1, rows, width), lambda i, at: (jnp.bitwise_xor(i, at[0]), 0, 0))
    out = pl.pallas_call(
        spread_kernel,
        grid_spec=pltpu.PrefetchScalarGridSpec(
            num_scalar_prefetch=1,
            grid=(4,),
            in_specs=[block, block],
            out_specs=pl.BlockSpec((1, 2, rows, width), lambda i, at: (i, 0, 0, 0)),
        ),
        out_shape=jax.ShapeDtypeStruct((4, 2, rows, width), mine.dtype),
        cost_estimate=pl.CostEstimate(
            flops=0, bytes_accessed=8 * mine.size, transcendentals=0
        ),
        name="spread",
    )(at, mine.reshape(4, rows, width), other.reshape(4, rows, width))
    return out.reshape(8 * rows, width)


def ffn_kernel(x_ref, cot_ref, g_ref, u_ref, d_ref, hidden_ref, d_gate_ref, d_up_ref):
    x = x_ref[...]
    gate = dot_plain(x, g_ref[...])
    up = dot_plain(x, u_ref[...])
    d_hidden = dot_plain(cot_ref[...], d_ref[...])
    sig = jax.nn.sigmoid(gate)
    act = gate * sig
    hidden_ref[...] = (act * up).astype(BF)
    d_up_ref[...] = (d_hidden * act).astype(BF)
    d_gate_ref[...] = (d_hidden * up * (sig * (1.0 + gate * (1.0 - sig)))).astype(BF)


def ffn_call(x, cot, g, u, d, chunk):
    rows, width = x.shape
    units = g.shape[1]
    tile = min(512, units)
    whole = pl.BlockSpec((rows, width), lambda i: (0, 0))
    rows_of = pl.BlockSpec((rows, width), lambda i: (chunk, 0))
    weight = pl.BlockSpec((width, tile), lambda i: (0, i))
    part = pl.BlockSpec((rows, tile), lambda i: (0, i))
    return pl.pallas_call(
        ffn_kernel,
        grid=(units // tile,),
        in_specs=[whole, rows_of, weight, weight, weight],
        out_specs=[part] * 3,
        out_shape=[jax.ShapeDtypeStruct((rows, units), BF)] * 3,
        cost_estimate=pl.CostEstimate(
            flops=6 * rows * width * units,
            bytes_accessed=6 * width * units + 6 * rows * units,
            transcendentals=rows * units,
        ),
        name="ffn",
    )(x, cot, g, u, d)


def product_kernel(count, turned, *refs):
    total = None
    for k in range(count):
        dot = dot_plain if turned else dot_cols
        part = dot(refs[k][...], refs[count + k][...])
        total = part if total is None else total + part
    refs[2 * count][...] = total.astype(BF)


def product_call(lefts, rights, turned):
    count = len(lefts)
    rows, depth = lefts[0].shape
    width = rights[0].shape[1 if turned else 0]
    tile = min(512 if turned else 256, width)
    weight = (
        pl.BlockSpec((depth, tile), lambda i: (0, i))
        if turned
        else pl.BlockSpec((tile, depth), lambda i: (i, 0))
    )
    return pl.pallas_call(
        functools.partial(product_kernel, count, turned),
        grid=(width // tile,),
        in_specs=[pl.BlockSpec((rows, depth), lambda i: (0, 0))] * count
        + [weight] * count,
        out_specs=pl.BlockSpec((rows, tile), lambda i: (0, i)),
        out_shape=jax.ShapeDtypeStruct((rows, width), BF),
        cost_estimate=pl.CostEstimate(
            flops=2 * count * rows * depth * width,
            bytes_accessed=2 * count * depth * (rows + width),
            transcendentals=0,
        ),
        name="product",
    )(*lefts, *rights)


def transpose_kernel(x_ref, out_ref):
    out_ref[...] = jnp.transpose(x_ref[...])


def transpose_call(x):
    rows, columns = x.shape
    tile = min(256, rows)
    return pl.pallas_call(
        transpose_kernel,
        grid=(rows // tile,),
        in_specs=[pl.BlockSpec((tile, columns), lambda i: (i, 0))],
        out_specs=pl.BlockSpec((columns, tile), lambda i: (0, i)),
        out_shape=jax.ShapeDtypeStruct((columns, rows), x.dtype),
        cost_estimate=pl.CostEstimate(
            flops=0, bytes_accessed=4 * x.size, transcendentals=0
        ),
        name="turn_over",
    )(x)


def turn_kernel(turned, x_ref, cos_ref, sin_ref, out_ref):
    cosine, sine = cos_ref[...], sin_ref[...]
    for begin in range(0, x_ref.shape[1], 128):
        piece = x_ref[:, begin : begin + 128].astype(F32)
        if begin < turned:
            piece = turn(piece, cosine, sine)
        out_ref[:, begin : begin + 128] = piece.astype(out_ref.dtype)


def turn_call(x, cosine, sine, turned):
    rows, width = x.shape
    tile = min(256, rows)
    return pl.pallas_call(
        functools.partial(turn_kernel, turned),
        grid=(rows // tile,),
        in_specs=[
            pl.BlockSpec((tile, width), lambda i: (i, 0)),
            pl.BlockSpec((tile, 128), lambda i: (i, 0)),
            pl.BlockSpec((tile, 128), lambda i: (i, 0)),
        ],
        out_specs=pl.BlockSpec((tile, width), lambda i: (i, 0)),
        out_shape=jax.ShapeDtypeStruct((rows, width), BF),
        cost_estimate=pl.CostEstimate(
            flops=4 * rows * width, bytes_accessed=6 * rows * width, transcendentals=0
        ),
        name="turn",
    )(x, cosine, sine)


def attend_kernel(
    group, place_ref, q_ref, k0, k1, k2, k3, segq_ref, segk_ref, out_ref, lse_ref
):
    block = q_ref.shape[1]
    kv_heads = k0.shape[2] // (2 * HD)
    me = place_ref[0]
    scale = LOG2E / math.sqrt(HD)
    row = lax.broadcasted_iota(jnp.int32, (block, block), 0)
    col = lax.broadcasted_iota(jnp.int32, (block, block), 1)
    seg_q = segq_ref[0]
    refs = (k0, k1, k2, k3)
    bias = []
    for k in range(len(refs)):
        there = place_ref[1 + k]
        seg_k = segk_ref[0, :, pl.ds(pl.multiple_of(there * block, block), block)]
        ahead = (there - me) * block
        allowed = (seg_q == seg_k) & (row >= col + ahead)
        bias.append(jnp.where(allowed, 0.0, NEG_FILL))
    sums = []
    for g in range(kv_heads):
        keys = [r[0, :, g * HD : (g + 1) * HD] for r in refs]
        values = [r[0, :, (kv_heads + g) * HD : (kv_heads + g + 1) * HD] for r in refs]
        for j in range(group):
            head = g * group + j
            q = q_ref[0, :, head * HD : (head + 1) * HD]
            scores = [
                dot_cols(q, keys[k]) * scale + bias[k] for k in range(len(refs))
            ]
            peak = functools.reduce(jnp.maximum, scores)
            peak = jnp.max(peak, axis=1, keepdims=True)
            weights = [jnp.exp2(s - peak) for s in scores]
            total = functools.reduce(jnp.add, weights)
            total = jnp.sum(total, axis=1, keepdims=True)
            mixed = functools.reduce(
                jnp.add, [dot_plain(w.astype(BF), v) for w, v in zip(weights, values)]
            )
            out_ref[0, :, head * HD : (head + 1) * HD] = (mixed / total).astype(BF)
            sums.append(peak + jnp.log2(total))
    lane = lax.broadcasted_iota(jnp.int32, (block, 128), 1)
    stacked = jnp.zeros((block, 128), F32)
    for head, value in enumerate(sums):
        stacked = jnp.where(lane == head, value, stacked)
    lse_ref[0] = jnp.transpose(stacked)[: len(sums)]


def attend_call(place, q, blocks, seg_q, seg_k):
    seqs, block, width = q.shape
    heads = width // HD
    kv_width = blocks[0].shape[2]
    group = heads // (kv_width // (2 * HD))
    seq_len = seg_k.shape[2]
    keys = pl.BlockSpec((1, block, kv_width), lambda s, p: (s, 0, 0))
    work = seqs * heads * block * seq_len
    return pl.pallas_call(
        functools.partial(attend_kernel, group),
        grid_spec=pltpu.PrefetchScalarGridSpec(
            num_scalar_prefetch=1,
            grid=(seqs,),
            in_specs=[
                pl.BlockSpec((1, block, width), lambda s, p: (s, 0, 0)),
                keys,
                keys,
                keys,
                keys,
                pl.BlockSpec((1, block, 1), lambda s, p: (s, 0, 0)),
                pl.BlockSpec((1, 1, seq_len), lambda s, p: (s, 0, 0)),
            ],
            out_specs=[
                pl.BlockSpec((1, block, width), lambda s, p: (s, 0, 0)),
                pl.BlockSpec((1, heads, block), lambda s, p: (s, 0, 0)),
            ],
        ),
        out_shape=[
            jax.ShapeDtypeStruct((seqs, block, width), BF),
            jax.ShapeDtypeStruct((seqs, heads, block), F32),
        ],
        cost_estimate=pl.CostEstimate(
            flops=4 * work * HD * 4, bytes_accessed=6 * q.size, transcendentals=work
        ),
        name="attend",
    )(place, q, *blocks, seg_q, seg_k)


def attend_back_kernel(
    group,
    place_ref,
    q_ref,
    k0,
    k1,
    k2,
    k3,
    segq_ref,
    segk_ref,
    out_ref,
    grad_ref,
    lse_ref,
    dq_ref,
    d0,
    d1,
    d2,
    d3,
    bias_ref,
    dsc_ref,
):
    block = q_ref.shape[1]
    kv_heads = k0.shape[2] // (2 * HD)
    me = place_ref[0]
    scale = LOG2E / math.sqrt(HD)
    back_scale = 1.0 / math.sqrt(HD)
    refs, d_refs = (k0, k1, k2, k3), (d0, d1, d2, d3)
    key_row = lax.broadcasted_iota(jnp.int32, (block, block), 0)
    q_col = lax.broadcasted_iota(jnp.int32, (block, block), 1)
    seg_q = segq_ref[0]
    for k in range(len(refs)):
        there = place_ref[1 + k]
        seg_k = segk_ref[0, pl.ds(pl.multiple_of(there * block, block), block), :]
        ahead = (there - me) * block
        allowed = (seg_q == seg_k) & (q_col >= key_row + ahead)
        bias_ref[k] = jnp.where(allowed, 0.0, NEG_FILL)
    width = group * block
    product = out_ref[0].astype(F32) * grad_ref[0].astype(F32)
    total_heads = kv_heads * group
    feature = lax.broadcasted_iota(jnp.int32, (total_heads, product.shape[1]), 1)
    owner = lax.broadcasted_iota(jnp.int32, (total_heads, product.shape[1]), 0)
    picks = jnp.where(feature // HD == owner, 1.0, 0.0).astype(F32)
    deltas = lax.dot_general(
        picks,
        product,
        (((1,), (1,)), ((), ())),
        preferred_element_type=F32,
        precision=lax.Precision.HIGHEST,
    )
    for g in range(kv_heads):
        heads = range(g * group, (g + 1) * group)
        q = jnp.concatenate([q_ref[0, :, h * HD : (h + 1) * HD] for h in heads], 0)
        grad = jnp.concatenate([grad_ref[0, :, h * HD : (h + 1) * HD] for h in heads], 0)
        d_query = None
        for k in range(len(refs)):
            keys = refs[k][0, :, g * HD : (g + 1) * HD]
            values = refs[k][0, :, (kv_heads + g) * HD : (kv_heads + g + 1) * HD]
            scores = dot_cols(keys, q)
            d_probs = dot_cols(values, grad)
            probs_low = []
            for j, h in enumerate(heads):
                cols = slice(j * block, (j + 1) * block)
                probs = jnp.exp2(
                    scores[:, cols] * scale + (bias_ref[k] - lse_ref[0, h : h + 1, :])
                )
                probs_low.append(probs.astype(BF))
                dsc_ref[:, cols] = (
                    probs * (d_probs[:, cols] - deltas[h : h + 1, :])
                ).astype(BF)
            d_scores = dsc_ref[...]
            d_value = dot_plain(jnp.concatenate(probs_low, 1), grad)
            d_key = dot_plain(d_scores, q) * back_scale
            d_refs[k][0, :, g * HD : (g + 1) * HD] = d_key.astype(BF)
            d_refs[k][0, :, (kv_heads + g) * HD : (kv_heads + g + 1) * HD] = d_value.astype(BF)
            part = dot_rows(d_scores, keys)
            d_query = part if d_query is None else d_query + part
        d_query = d_query * back_scale
        for j, h in enumerate(heads):
            dq_ref[0, :, h * HD : (h + 1) * HD] = d_query[j * block : (j + 1) * block].astype(BF)


def attend_back_call(place, q, blocks, seg_q, seg_k, out, grad, lse):
    seqs, block, width = q.shape
    heads = width // HD
    kv_width = blocks[0].shape[2]
    group = heads // (kv_width // (2 * HD))
    seq_len = seg_k.shape[1]
    keys = pl.BlockSpec((1, block, kv_width), lambda s, p: (s, 0, 0))
    rows = pl.BlockSpec((1, block, width), lambda s, p: (s, 0, 0))
    work = seqs * heads * block * seq_len
    return pl.pallas_call(
        functools.partial(attend_back_kernel, group),
        grid_spec=pltpu.PrefetchScalarGridSpec(
            num_scalar_prefetch=1,
            grid=(seqs,),
            in_specs=[
                rows,
                keys,
                keys,
                keys,
                keys,
                pl.BlockSpec((1, 1, block), lambda s, p: (s, 0, 0)),
                pl.BlockSpec((1, seq_len, 1), lambda s, p: (s, 0, 0)),
                rows,
                rows,
                pl.BlockSpec((1, heads, block), lambda s, p: (s, 0, 0)),
            ],
            out_specs=[rows, keys, keys, keys, keys],
            scratch_shapes=[
                pltpu.VMEM((4, block, block), F32),
                pltpu.VMEM((block, group * block), BF),
            ],
        ),
        out_shape=[jax.ShapeDtypeStruct(q.shape, BF)]
        + [jax.ShapeDtypeStruct(blocks[0].shape, BF)] * 4,
        cost_estimate=pl.CostEstimate(
            flops=10 * work * HD * 4, bytes_accessed=12 * q.size, transcendentals=work
        ),
        name="attend_back",
    )(place, q, *blocks, seg_q, seg_k, out, grad, lse)


def inverse_rms(values):
    return lax.rsqrt(jnp.mean(values * values, axis=-1, keepdims=True) + EPSILON)


def norm_back(values, gain, incoming):
    scale = inverse_rms(values)
    gain_terms = jnp.sum(incoming * values * scale, axis=0)
    weighted = incoming * gain
    inner = jnp.mean(weighted * values, axis=-1, keepdims=True)
    return scale * weighted - values * (scale * scale * scale) * inner, gain_terms


def per_device(
    tokens,
    segments,
    q_weight,
    k_weight,
    v_weight,
    o_weight,
    attn_gain,
    gate_weight,
    up_weight,
    down_weight,
    ffn_gain,
    cotangent,
):
    heads_axes = ("yy", "core")
    seqs, block, width = tokens.shape
    seq_len = segments.shape[1]
    parts = lax.axis_size(heads_axes)
    ways = lax.axis_size("tensor")
    owners = ("fsdp",) + heads_axes
    here = lax.axis_index(heads_axes)
    me = lax.axis_index("tensor")
    q_width, k_width = q_weight.shape[1], k_weight.shape[1]
    kv_width = 2 * k_width
    qkv_width = q_width + kv_width
    per_chunk = seqs // CHUNKS
    rows = per_chunk * block
    own_rows = rows // ways

    clock = Clock()
    slot = clock.slot
    where_all = positions(segments)
    where_here = lax.dynamic_slice_in_dim(where_all, here * block, block, 1)
    seg_here = lax.dynamic_slice_in_dim(segments, here * block, block, 1)
    lane = np.arange(128)
    frequency = jnp.asarray(
        ROPE_BASE ** (-2.0 * (np.arange(128) % 32).astype(np.float32) / HD), F32
    )
    angles = where_here.reshape(seqs * block, 1).astype(F32) * frequency
    cosine = jnp.cos(angles)
    sine = jnp.sin(angles) * jnp.asarray(np.where(lane % 64 < 32, -1.0, 1.0), F32)
    place = jnp.stack([here] + [here ^ k for k in range(parts)]).astype(jnp.int32)

    def chunk_of(x, c):
        return lax.slice_in_dim(x, c * per_chunk, (c + 1) * per_chunk, axis=0)

    def own(x):
        return lax.dynamic_slice_in_dim(x, me * own_rows, own_rows, 0)

    def own_of(x, chunk):
        flat = x.reshape(seqs * block, width)
        return lax.dynamic_slice_in_dim(flat, chunk * rows + me * own_rows, own_rows, 0)

    def blocks(x):
        return x.reshape(ways, own_rows, width)

    state = []
    for c in range(CHUNKS):
        s = {}
        tok = chunk_of(tokens, c).reshape(rows, width)
        s["tok"] = tok
        s["own_tok"], s["own_cot"] = own_of(tokens, c), own_of(cotangent, c)
        s["cos"] = lax.slice_in_dim(cosine, c * rows, (c + 1) * rows, axis=0)
        s["sin"] = lax.slice_in_dim(sine, c * rows, (c + 1) * rows, axis=0)
        s["sin_back"] = -s["sin"]
        s["scale_one"] = inverse_rms(tok.astype(F32))
        seg_q, seg_k = chunk_of(seg_here, c), chunk_of(segments, c)
        s["seg_fwd"] = (seg_q[:, :, None], seg_k[:, None, :])
        s["seg_back"] = (seg_q[:, None, :], seg_k[:, :, None])
        state.append(s)
    first, second = state

    pad = jnp.zeros((q_weight.shape[0], 126), BF)
    packed = jnp.concatenate(
        [q_weight, o_weight, k_weight, v_weight, attn_gain[:, None], ffn_gain[:, None], pad],
        axis=1,
    )

    def gathered(shard):
        return lax.all_gather(shard, owners, axis=0, tiled=True)

    gather_near = NearGather(packed)
    slot([gather_near])
    for s in state:
        for name in ("cos", "sin", "sin_back", "scale_one"):
            clock.expect(s[name])
        for name in ("seg_fwd", "seg_back"):
            clock.last += s[name]
    clock.expect(place)
    slot([gather_near])
    slot([gather_near], lambda *shards: shards, (gate_weight, up_weight, down_weight))
    gate_weight, up_weight, down_weight = clock.last[-3:]
    full_g = gathered(gate_weight)
    full_u = gathered(up_weight)
    full_d = gathered(down_weight)
    packed = gather_near.result()
    at = 0
    columns = []
    for wide in (q_width, q_width, kv_width, 2):
        columns.append(packed[:, at : at + wide])
        at += wide
    full_q, full_o, full_kv, gains = columns
    gains = gains.T.astype(F32)
    gain_one, gain_two = gains[0:1], gains[1:2]

    def project_kv(s, tok):
        normed = (tok.astype(F32) * s["scale_one"] * gain_one).astype(BF)
        kv = turn_call(dot_plain(normed, full_kv), s["cos"], s["sin"], k_width)
        return normed, kv.reshape(per_chunk, block, kv_width)

    def project_q(s, normed):
        q = turn_call(dot_plain(normed, full_q), s["cos"], s["sin"], q_width)
        return (q.reshape(per_chunk, block, q_width),)

    def project(s, tok):
        normed, kv = project_kv(s, tok)
        return (normed, kv) + project_q(s, normed)

    def attend(s, q, *kv):
        attended, lse = attend_call(place, q, kv, *s["seg_fwd"])
        s["attended"], s["lse"] = attended, lse
        attn = dot_cols(attended.reshape(rows, q_width), full_o).astype(BF)
        return attended, lse, attn

    def enter_ffn(s, summed):
        s["residual"] = s["own_tok"].astype(F32) + summed
        return (s["residual"] * inverse_rms(s["residual"]) * gain_two).astype(BF)

    turned = {}

    def turn_over(weight):
        return (transpose_call(weight),)

    cot_rows = cotangent.reshape(seqs * block, width)

    def ffn_mid(chunk, normed_two):
        return ffn_call(normed_two, cot_rows, full_g, full_u, full_d, chunk)

    def ffn_back(d_gate, d_up):
        return (product_call((d_gate, d_up), (turned["g"], turned["u"]), True),)

    def ffn_out(hidden):
        return (product_call((hidden,), (full_d,), False),)

    def leave_ffn(s, summed):
        d_norm, s["gain_two"] = norm_back(s["residual"], gain_two, summed)
        s["d_resid"] = s["own_cot"].astype(F32) + d_norm
        return s["d_resid"].astype(BF)

    def attend_back(s, d_attn):
        d_attended = dot_plain(d_attn, full_o).astype(BF).reshape(per_chunk, block, q_width)
        return attend_back_call(
            place, s["q"], s["kv"], *s["seg_back"], s["attended"], d_attended, s["lse"]
        )

    def project_back(s, dq, b0, b1, b2, b3):
        from3 = lax.ppermute(b3, "core", FLIP)
        from1 = lax.ppermute(b1, "core", FLIP)
        far = (b2.astype(F32) + from3.astype(F32)).astype(BF)
        from2 = lax.ppermute(far, "yy", FLIP)
        kv_parts = [x.reshape(rows, kv_width) for x in (b0, from1, from2)]
        d_qkv = turn_back_call(
            dq.reshape(rows, q_width), kv_parts, s["cos"], s["sin_back"], k_width
        )
        full_qkv = jnp.concatenate([full_q, full_kv], axis=1)
        return d_qkv, dot_cols(d_qkv, full_qkv).astype(BF)

    def leave_attention(s, summed):
        d_norm, s["gain_one"] = norm_back(s["own_tok"].astype(F32), gain_one, summed)
        return (s["d_resid"] + d_norm).astype(BF)

    def scattered(grad):
        return lax.psum_scatter(grad, owners, scatter_dimension=0, tiled=True)

    def weight_grad(*halves):
        left = jnp.concatenate(halves[:-CHUNKS], axis=0)
        right = jnp.concatenate(halves[-CHUNKS:], axis=0)
        return (dot_rows(left, right).astype(BF),)

    def of_both(*names):
        return tuple(s[name] for name in names for s in state)

    def whole(rows_of):
        return rows_of.reshape(per_chunk, block, width)

    axes = ("tensor", "core", "yy", "fsdp")
    first["normed_one"], kv = slot(
        [], functools.partial(project_kv, first), (first["tok"],)
    )
    keys = KeyExchange(kv)
    (first["q"],) = slot(
        [keys], functools.partial(project_q, first), (first["normed_one"],)
    )
    slot([keys])
    first["kv"] = keys.result()
    first["attended"], first["lse"], attn = slot(
        [], functools.partial(attend, first), (first["q"],) + first["kv"]
    )
    sum_a0 = LineSum(blocks(attn))
    second["normed_one"], kv, second["q"] = slot(
        [sum_a0], functools.partial(project, second), (second["tok"],)
    )
    keys = KeyExchange(kv)
    slot([sum_a0, keys])
    slot([sum_a0, keys])
    second["kv"] = keys.result()
    gather_a0 = LineGather(enter_ffn(first, sum_a0.result()))
    second["attended"], second["lse"], attn = slot(
        [gather_a0], functools.partial(attend, second), (second["q"],) + second["kv"]
    )
    sum_a1 = LineSum(blocks(attn))
    (turned["g"],) = slot([Both(gather_a0, sum_a1)], turn_over, (full_g,))
    (turned["u"],) = slot([Both(gather_a0, sum_a1)], turn_over, (full_u,))
    first["normed_two"] = gather_a0.result().reshape(rows, width)
    first["hidden"], first["d_gate"], first["d_up"] = slot(
        [sum_a1], functools.partial(ffn_mid, 0), (first["normed_two"],)
    )
    gather_a1 = LineGather(enter_ffn(second, sum_a1.result()))
    (back,) = slot([gather_a1], ffn_back, (first["d_gate"], first["d_up"]))
    sum_d0 = LineSum(blocks(back))
    (ffn,) = slot([Both(gather_a1, sum_d0)], ffn_out, (first["hidden"],))
    sum_f0 = LineSum(blocks(ffn))
    slot([Both(gather_a1, sum_d0)])
    second["normed_two"] = gather_a1.result().reshape(rows, width)
    second["hidden"], second["d_gate"], second["d_up"] = slot(
        [sum_d0], functools.partial(ffn_mid, 1), (second["normed_two"],)
    )
    gather_d0 = LineGather(leave_ffn(first, sum_d0.result()))
    (back,) = slot([gather_d0], ffn_back, (second["d_gate"], second["d_up"]))
    sum_d1 = LineSum(blocks(back))
    (grad,) = slot(
        [Both(gather_d0, sum_d1)],
        weight_grad,
        (cot_rows,) + of_both("hidden"),
    )
    (grad,) = slot(
        [Both(gather_d0, sum_d1), sum_f0],
        weight_grad,
        of_both("normed_two", "d_gate"),
        scattered,
        grad,
    )
    down_grad = clock.launched
    first["d_attn"] = gather_d0.result().reshape(rows, width)
    pieces = slot(
        [sum_d1, sum_f0], functools.partial(attend_back, first), (first["d_attn"],), scattered, grad
    )
    gate_grad = clock.launched
    gather_d1 = LineGather(leave_ffn(second, sum_d1.result()))
    first["d_qkv"], back = slot(
        [gather_d1, sum_f0], functools.partial(project_back, first), pieces
    )
    sum_n0 = LineSum(blocks(back))
    gather_f0 = LineGather((first["residual"] + sum_f0.result()).astype(BF))
    (grad,) = slot(
        [Both(gather_d1, sum_n0), gather_f0], weight_grad, of_both("normed_two", "d_up")
    )
    slot([Both(gather_d1, sum_n0), gather_f0], None, (), scattered, grad)
    up_grad = clock.launched
    second["d_attn"] = gather_d1.result().reshape(rows, width)
    pieces = slot(
        [sum_n0, gather_f0], functools.partial(attend_back, second), (second["d_attn"],)
    )
    gather_n0 = LineGather(leave_attention(first, sum_n0.result()))
    second["d_qkv"], back = slot(
        [gather_n0], functools.partial(project_back, second), pieces
    )
    sum_n1 = LineSum(blocks(back))
    first["output"] = gather_f0.result()
    (grad,) = slot(
        [Both(gather_n0, sum_n1)], weight_grad, of_both("normed_one", "d_qkv")
    )
    qkv_part = grad
    for s in state:
        s["attended_rows"] = s["attended"].reshape(rows, q_width)
    (grad,) = slot(
        [Both(gather_n0, sum_n1)],
        weight_grad,
        of_both("d_attn", "attended_rows"),
        scattered,
        qkv_part,
    )
    qkv_grad = clock.launched
    first["input_grad"] = gather_n0.result()
    (ffn,) = slot([sum_n1], ffn_out, (second["hidden"],), scattered, grad)
    sum_f1 = LineSum(blocks(ffn))
    o_grad = clock.launched
    gather_n1 = LineGather(leave_attention(second, sum_n1.result()))
    gains_one = Butterfly(
        jnp.stack([sum(s[name] for s in state) for name in ("gain_one", "gain_two")]), axes
    )
    slot([gather_n1, gains_one])
    slot([Both(gather_n1, sum_f1), gains_one])
    clock.expect(whole(first["input_grad"]))
    clock.expect(first["output"])
    slot([Both(gather_n1, sum_f1), gains_one])
    second["input_grad"] = gather_n1.result()
    clock.expect(down_grad)
    slot([sum_f1, gains_one])
    input_grad = jnp.concatenate([whole(s["input_grad"]) for s in state], axis=0).astype(F32)
    gather_f1 = LineGather((second["residual"] + sum_f1.result()).astype(BF))
    clock.expect(gate_grad)
    slot([gather_f1, gains_one])
    clock.expect(input_grad)
    down_grad, gate_grad = down_grad.astype(F32), gate_grad.astype(F32)
    clock.expect(up_grad)
    slot([gather_f1])
    clock.expect(down_grad)
    clock.expect(gate_grad)
    up_grad = up_grad.astype(F32)
    clock.expect(up_grad)
    slot([gather_f1])
    second["output"] = gather_f1.result()
    while gains_one.moves:
        slot([gains_one])

    qkv_grad, o_grad = qkv_grad.astype(F32), o_grad.astype(F32)
    share = attn_gain.shape[0]
    index = lax.axis_index("fsdp") * parts + here

    def owned(gain):
        return lax.dynamic_slice_in_dim(gain, index * share, share, 0)

    gain_one_grad, gain_two_grad = gains_one.value

    return (
        jnp.concatenate([whole(s["output"]) for s in state], axis=0),
        input_grad,
        qkv_grad[:, :q_width],
        qkv_grad[:, q_width : q_width + k_width],
        qkv_grad[:, q_width + k_width :],
        o_grad,
        owned(gain_one_grad),
        gate_grad,
        up_grad,
        down_grad,
        owned(gain_two_grad),
    )


def solution(mesh):
    sizes = mesh.shape
    split = (sizes["fsdp"], sizes["heads"] // 2, 2, sizes["tensor"])
    mesh = jax.sharding.Mesh(mesh.devices.reshape(split), ("fsdp", "yy", "core", "tensor"))
    heads = ("yy", "core")
    rows = P("fsdp", heads, None)
    matrix = P(("fsdp",) + heads, "tensor")
    vector = P(("fsdp",) + heads)
    return jax.shard_map(
        per_device,
        mesh=mesh,
        in_specs=(
            rows,
            P("fsdp", None),
            matrix,
            matrix,
            matrix,
            matrix,
            vector,
            matrix,
            matrix,
            matrix,
            vector,
            rows,
        ),
        out_specs=(
            rows,
            rows,
            matrix,
            matrix,
            matrix,
            matrix,
            vector,
            matrix,
            matrix,
            matrix,
            vector,
        ),
        check_vma=False,
    )
```

```python
import functools
import math

import jax
import jax.numpy as jnp
import numpy as np
from jax import lax
from jax.experimental import pallas as pl
from jax.experimental.pallas import tpu as pltpu
from jax.sharding import PartitionSpec as P

HD = 64
EPSILON = 1e-05
ROPE_BASE = 500000.0
NEG_FILL = -1e30
LOG2E = math.log2(math.e)
BF = jnp.bfloat16
F32 = jnp.float32
CHUNKS = 2


def positions(segments):
    length_of = segments.shape[-1]
    column = jnp.arange(length_of, dtype=jnp.int32)
    before = jnp.concatenate([segments[..., :1] - 1, segments[..., :-1]], axis=-1)
    firsts = jnp.where(segments != before, column, jnp.zeros_like(column))
    starts = lax.cummax(firsts, axis=firsts.ndim - 1)
    return column - starts


def dot_plain(left_in, right_in):
    return jnp.dot(left_in, right_in, preferred_element_type=F32)


def dot_rows(left_in, right_in):
    return lax.dot_general(
        left_in, right_in, (((0,), (0,)), ((), ())), preferred_element_type=F32
    )


def dot_cols(left_in, right_in):
    return lax.dot_general(
        left_in, right_in, (((1,), (1,)), ((), ())), preferred_element_type=F32
    )


class LineSum:
    def __init__(self, parts):
        self.parts = parts
        self.step = 1
        self.from_left = self.from_right = None

    def pick(self, j):
        last = self.parts.shape[0] - 1
        return lax.dynamic_index_in_dim(self.parts, jnp.clip(j, 0, last), 0, keepdims=False)

    def sends(self):
        count, t = self.parts.shape[0], self.step
        me = lax.axis_index("tensor")
        to_right = self.pick(count - t + me)
        to_left = self.pick(t + me - count)
        if self.from_left is not None:
            to_right = (to_right.astype(F32) + self.from_left.astype(F32)).astype(BF)
            to_left = (to_left.astype(F32) + self.from_right.astype(F32)).astype(BF)
        return [
            (to_right, "tensor", [(k, k + 1) for k in range(t)]),
            (to_left, "tensor", [(count - 1 - k, count - 2 - k) for k in range(t)]),
        ]

    def take(self, moved):
        self.from_left, self.from_right = moved
        self.step += 1

    def result(self):
        own = self.pick(lax.axis_index("tensor"))
        return own.astype(F32) + self.from_left.astype(F32) + self.from_right.astype(F32)


class LineGather:
    def __init__(self, own):
        self.own = self.right = self.left = own
        self.step = 1
        self.from_left, self.from_right = {}, {}

    def sends(self):
        count, t = lax.axis_size("tensor"), self.step
        steps = range(t - 1, count - 1)
        return [
            (self.right, "tensor", [(k, k + 1) for k in steps]),
            (self.left, "tensor", [(count - 1 - k, count - 2 - k) for k in steps]),
        ]

    def take(self, moved):
        self.right, self.left = moved
        self.from_left[self.step], self.from_right[self.step] = moved
        self.step += 1

    def result(self):
        count = lax.axis_size("tensor")
        steps = range(1, count)
        return place_call(
            self.own, [self.from_left[t] for t in steps], [self.from_right[t] for t in steps]
        )


class Both:
    def __init__(self, gather, total):
        self.gather, self.total = gather, total

    def sends(self):
        me, count = lax.axis_index("tensor"), lax.axis_size("tensor")
        first = self.gather.step - 1
        out = []
        for rank, whole, part in zip(
            (me, count - 1 - me), self.gather.sends(), self.total.sends()
        ):
            value = jnp.where(rank >= first, whole[0], part[0])
            out.append((value, "tensor", sorted(whole[2] + part[2])))
        return out

    def take(self, moved):
        self.gather.take(moved)
        self.total.take(moved)


FLIP = [(0, 1), (1, 0)]


class NearGather:
    def __init__(self, shard):
        self.shard = shard
        self.step = 1
        self.near = lax.axis_size("fsdp") == 2 and lax.axis_size("yy") == 2

    def sends(self):
        if not self.near:
            return []
        half = self.shard.shape[0] // 2
        if self.step == 1:
            return [(self.shard, "fsdp", FLIP), (self.shard, "yy", FLIP)]
        if self.step == 2:
            return [(self.by_y[:half], "fsdp", FLIP), (self.by_x[half:], "yy", FLIP)]
        self.mine = jnp.concatenate([self.shard, self.by_y, self.by_x, self.lo, self.hi], axis=0)
        return [(self.mine, "core", FLIP)]

    def take(self, moved):
        if self.near:
            if self.step == 1:
                self.by_x, self.by_y = moved
            elif self.step == 2:
                self.lo, self.hi = moved
            else:
                (self.other,) = moved
        self.step += 1

    def result(self):
        if not self.near:
            return lax.all_gather(self.shard, ("fsdp", "yy", "core"), axis=0, tiled=True)
        return spread_call(self.mine, self.other)


class KeyExchange:
    def __init__(self, kv):
        self.kv = kv
        self.step = 1

    def sends(self):
        if self.step == 1:
            return [(self.kv, "yy", FLIP), (self.kv, "core", FLIP)]
        return [(self.kv2, "core", FLIP)]

    def take(self, moved):
        if self.step == 1:
            self.kv2, self.kv1 = moved
        else:
            (self.kv3,) = moved
        self.step += 1

    def result(self):
        return self.kv, self.kv1, self.kv2, self.kv3


class Butterfly:
    def __init__(self, value, axes):
        self.value = value
        self.moves = []
        for axis in axes:
            bit = 1
            while bit < lax.axis_size(axis):
                self.moves.append((axis, pairs(lax.axis_size(axis), bit)))
                bit *= 2

    def sends(self):
        axis, pattern = self.moves.pop(0)
        return [(self.value, axis, pattern)]

    def take(self, moved):
        self.value = self.value + moved[0]


class Clock:
    def __init__(self):
        self.last = ()

    def expect(self, value):
        self.last += (value,)

    def slot(self, tasks, work=None, args=(), launch=None, grad=None):
        sends = [task.sends() for task in tasks]
        flat = [send for group in sends for send in group]
        before = len(self.last)
        extra = () if launch is None else (grad,)
        gated = lax.optimization_barrier(
            tuple(self.last) + tuple(s[0] for s in flat) + tuple(args) + extra
        )[before:]
        if launch is not None:
            self.launched = launch(gated[-1])
        moved = [lax.ppermute(g, s[1], s[2]) for g, s in zip(gated, flat)]
        done = tuple(work(*gated[len(flat) : len(flat) + len(args)])) if work else ()
        self.last = tuple(moved) + done
        at = 0
        for task, group in zip(tasks, sends):
            task.take(moved[at : at + len(group)])
            at += len(group)
        return done


def pairs(count, bit):
    return [(k, k ^ bit) for k in range(count)]


def turn(values, cosine, sine):
    lane = lax.broadcasted_iota(jnp.int32, values.shape, 1)
    swapped = jnp.where(
        lax.rem(lane, 64) < 32, pltpu.roll(values, 96, 1), pltpu.roll(values, 32, 1)
    )
    return values * cosine + swapped * sine


def turn_back_kernel(k_width, dq_ref, b0_ref, b1_ref, b2_ref, cos_ref, sin_ref, out_ref):
    cosine, sine = cos_ref[...], sin_ref[...]
    q_width = dq_ref.shape[1]
    for begin in range(0, q_width, 128):
        piece = dq_ref[:, begin : begin + 128].astype(F32)
        out_ref[:, begin : begin + 128] = turn(piece, cosine, sine).astype(BF)
    for begin in range(0, b0_ref.shape[1], 128):
        piece = sum(
            ref[:, begin : begin + 128].astype(F32) for ref in (b0_ref, b1_ref, b2_ref)
        )
        if begin < k_width:
            piece = turn(piece, cosine, sine)
        out_ref[:, q_width + begin : q_width + begin + 128] = piece.astype(BF)


def turn_back_call(dq, parts, cosine, sine, k_width):
    rows, q_width = dq.shape
    kv_width = parts[0].shape[1]
    tile = min(256, rows)

    def tall(wide):
        return pl.BlockSpec((tile, wide), lambda i: (i, 0))

    return pl.pallas_call(
        functools.partial(turn_back_kernel, k_width),
        grid=(rows // tile,),
        in_specs=[tall(q_width)] + [tall(kv_width)] * 3 + [tall(128)] * 2,
        out_specs=tall(q_width + kv_width),
        out_shape=jax.ShapeDtypeStruct((rows, q_width + kv_width), BF),
        cost_estimate=pl.CostEstimate(
            flops=4 * rows * (q_width + kv_width),
            bytes_accessed=4 * rows * (q_width + 2 * kv_width),
            transcendentals=0,
        ),
        name="turn_back",
    )(dq, *parts, cosine, sine)


def place_kernel(count, me_ref, *refs):
    own, from_left, from_right = refs[0], refs[1:count], refs[count : 2 * count - 1]
    out = refs[2 * count - 1]
    me = me_ref[0]
    for k in range(count):
        todo = [(me == k, own)]
        for t in range(1, count):
            if k + t < count:
                todo.append((me == k + t, from_left[t - 1]))
            if k - t >= 0:
                todo.append((me == k - t, from_right[t - 1]))
        for chosen, source in todo:

            @pl.when(chosen)
            def _(source=source, k=k):
                out[k] = source[...]


def place_call(own, from_left, from_right):
    count = len(from_left) + 1
    rows, width = own.shape
    tile = min(64, rows)
    me = lax.axis_index("tensor").astype(jnp.int32)[None]
    return pl.pallas_call(
        functools.partial(place_kernel, count),
        grid_spec=pltpu.PrefetchScalarGridSpec(
            num_scalar_prefetch=1,
            grid=(rows // tile,),
            in_specs=[pl.BlockSpec((tile, width), lambda i, p: (i, 0))] * (2 * count - 1),
            out_specs=pl.BlockSpec((count, tile, width), lambda i, p: (0, i, 0)),
        ),
        out_shape=jax.ShapeDtypeStruct((count,) + own.shape, own.dtype),
        cost_estimate=pl.CostEstimate(
            flops=0, bytes_accessed=6 * count * own.size, transcendentals=0
        ),
        name="place",
    )(me, own, *from_left, *from_right)


def spread_kernel(at_ref, mine_ref, other_ref, out_ref):
    for core in range(2):

        @pl.when(at_ref[1] == core)
        def _(core=core):
            out_ref[0, core] = mine_ref[0]
            out_ref[0, 1 - core] = other_ref[0]


def spread_call(mine, other):
    rows, width = mine.shape[0] // 4, mine.shape[1]
    chip = lax.axis_index("fsdp") * 2 + lax.axis_index("yy")
    at = jnp.stack([chip, lax.axis_index("core")]).astype(jnp.int32)
    block = pl.BlockSpec((1, rows, width), lambda i, at: (jnp.bitwise_xor(i, at[0]), 0, 0))
    out = pl.pallas_call(
        spread_kernel,
        grid_spec=pltpu.PrefetchScalarGridSpec(
            num_scalar_prefetch=1,
            grid=(4,),
            in_specs=[block, block],
            out_specs=pl.BlockSpec((1, 2, rows, width), lambda i, at: (i, 0, 0, 0)),
        ),
        out_shape=jax.ShapeDtypeStruct((4, 2, rows, width), mine.dtype),
        cost_estimate=pl.CostEstimate(
            flops=0, bytes_accessed=8 * mine.size, transcendentals=0
        ),
        name="spread",
    )(at, mine.reshape(4, rows, width), other.reshape(4, rows, width))
    return out.reshape(8 * rows, width)


def ffn_kernel(x_ref, cot_ref, g_ref, u_ref, d_ref, hidden_ref, d_gate_ref, d_up_ref):
    x = x_ref[...]
    gate = dot_plain(x, g_ref[...])
    up = dot_plain(x, u_ref[...])
    d_hidden = dot_plain(cot_ref[...], d_ref[...])
    sig = jax.nn.sigmoid(gate)
    act = gate * sig
    hidden_ref[...] = (act * up).astype(BF)
    d_up_ref[...] = (d_hidden * act).astype(BF)
    d_gate_ref[...] = (d_hidden * up * (sig * (1.0 + gate * (1.0 - sig)))).astype(BF)


def ffn_call(x, cot, g, u, d, chunk):
    rows, width = x.shape
    units = g.shape[1]
    tile = min(512, units)
    whole = pl.BlockSpec((rows, width), lambda i: (0, 0))
    rows_of = pl.BlockSpec((rows, width), lambda i: (chunk, 0))
    weight = pl.BlockSpec((width, tile), lambda i: (0, i))
    part = pl.BlockSpec((rows, tile), lambda i: (0, i))
    return pl.pallas_call(
        ffn_kernel,
        grid=(units // tile,),
        in_specs=[whole, rows_of, weight, weight, weight],
        out_specs=[part] * 3,
        out_shape=[jax.ShapeDtypeStruct((rows, units), BF)] * 3,
        cost_estimate=pl.CostEstimate(
            flops=6 * rows * width * units,
            bytes_accessed=6 * width * units + 6 * rows * units,
            transcendentals=rows * units,
        ),
        name="ffn",
    )(x, cot, g, u, d)


def product_kernel(count, turned, *refs):
    total = None
    for k in range(count):
        dot = dot_plain if turned else dot_cols
        part = dot(refs[k][...], refs[count + k][...])
        total = part if total is None else total + part
    refs[2 * count][...] = total.astype(BF)


def product_call(lefts, rights, turned):
    count = len(lefts)
    rows, depth = lefts[0].shape
    width = rights[0].shape[1 if turned else 0]
    tile = min(512 if turned else 256, width)
    weight = (
        pl.BlockSpec((depth, tile), lambda i: (0, i))
        if turned
        else pl.BlockSpec((tile, depth), lambda i: (i, 0))
    )
    return pl.pallas_call(
        functools.partial(product_kernel, count, turned),
        grid=(width // tile,),
        in_specs=[pl.BlockSpec((rows, depth), lambda i: (0, 0))] * count
        + [weight] * count,
        out_specs=pl.BlockSpec((rows, tile), lambda i: (0, i)),
        out_shape=jax.ShapeDtypeStruct((rows, width), BF),
        cost_estimate=pl.CostEstimate(
            flops=2 * count * rows * depth * width,
            bytes_accessed=2 * count * depth * (rows + width),
            transcendentals=0,
        ),
        name="product",
    )(*lefts, *rights)


def transpose_kernel(x_ref, out_ref):
    out_ref[...] = jnp.transpose(x_ref[...])


def transpose_call(x):
    rows, columns = x.shape
    tile = min(256, rows)
    return pl.pallas_call(
        transpose_kernel,
        grid=(rows // tile,),
        in_specs=[pl.BlockSpec((tile, columns), lambda i: (i, 0))],
        out_specs=pl.BlockSpec((columns, tile), lambda i: (0, i)),
        out_shape=jax.ShapeDtypeStruct((columns, rows), x.dtype),
        cost_estimate=pl.CostEstimate(
            flops=0, bytes_accessed=4 * x.size, transcendentals=0
        ),
        name="turn_over",
    )(x)


def turn_kernel(turned, x_ref, cos_ref, sin_ref, out_ref):
    cosine, sine = cos_ref[...], sin_ref[...]
    for begin in range(0, x_ref.shape[1], 128):
        piece = x_ref[:, begin : begin + 128].astype(F32)
        if begin < turned:
            piece = turn(piece, cosine, sine)
        out_ref[:, begin : begin + 128] = piece.astype(out_ref.dtype)


def turn_call(x, cosine, sine, turned):
    rows, width = x.shape
    tile = min(256, rows)
    return pl.pallas_call(
        functools.partial(turn_kernel, turned),
        grid=(rows // tile,),
        in_specs=[
            pl.BlockSpec((tile, width), lambda i: (i, 0)),
            pl.BlockSpec((tile, 128), lambda i: (i, 0)),
            pl.BlockSpec((tile, 128), lambda i: (i, 0)),
        ],
        out_specs=pl.BlockSpec((tile, width), lambda i: (i, 0)),
        out_shape=jax.ShapeDtypeStruct((rows, width), BF),
        cost_estimate=pl.CostEstimate(
            flops=4 * rows * width, bytes_accessed=6 * rows * width, transcendentals=0
        ),
        name="turn",
    )(x, cosine, sine)


def attend_kernel(
    group, place_ref, q_ref, k0, k1, k2, k3, segq_ref, segk_ref, out_ref, lse_ref
):
    block = q_ref.shape[1]
    kv_heads = k0.shape[2] // (2 * HD)
    me = place_ref[0]
    scale = LOG2E / math.sqrt(HD)
    row = lax.broadcasted_iota(jnp.int32, (block, block), 0)
    col = lax.broadcasted_iota(jnp.int32, (block, block), 1)
    seg_q = segq_ref[0]
    refs = (k0, k1, k2, k3)
    bias = []
    for k in range(len(refs)):
        there = place_ref[1 + k]
        seg_k = segk_ref[0, :, pl.ds(pl.multiple_of(there * block, block), block)]
        ahead = (there - me) * block
        allowed = (seg_q == seg_k) & (row >= col + ahead)
        bias.append(jnp.where(allowed, 0.0, NEG_FILL))
    sums = []
    for g in range(kv_heads):
        keys = [r[0, :, g * HD : (g + 1) * HD] for r in refs]
        values = [r[0, :, (kv_heads + g) * HD : (kv_heads + g + 1) * HD] for r in refs]
        for j in range(group):
            head = g * group + j
            q = q_ref[0, :, head * HD : (head + 1) * HD]
            scores = [
                dot_cols(q, keys[k]) * scale + bias[k] for k in range(len(refs))
            ]
            peak = functools.reduce(jnp.maximum, scores)
            peak = jnp.max(peak, axis=1, keepdims=True)
            weights = [jnp.exp2(s - peak) for s in scores]
            total = functools.reduce(jnp.add, weights)
            total = jnp.sum(total, axis=1, keepdims=True)
            mixed = functools.reduce(
                jnp.add, [dot_plain(w.astype(BF), v) for w, v in zip(weights, values)]
            )
            out_ref[0, :, head * HD : (head + 1) * HD] = (mixed / total).astype(BF)
            sums.append(peak + jnp.log2(total))
    lane = lax.broadcasted_iota(jnp.int32, (block, 128), 1)
    stacked = jnp.zeros((block, 128), F32)
    for head, value in enumerate(sums):
        stacked = jnp.where(lane == head, value, stacked)
    lse_ref[0] = jnp.transpose(stacked)[: len(sums)]


def attend_call(place, q, blocks, seg_q, seg_k):
    seqs, block, width = q.shape
    heads = width // HD
    kv_width = blocks[0].shape[2]
    group = heads // (kv_width // (2 * HD))
    seq_len = seg_k.shape[2]
    keys = pl.BlockSpec((1, block, kv_width), lambda s, p: (s, 0, 0))
    work = seqs * heads * block * seq_len
    return pl.pallas_call(
        functools.partial(attend_kernel, group),
        grid_spec=pltpu.PrefetchScalarGridSpec(
            num_scalar_prefetch=1,
            grid=(seqs,),
            in_specs=[
                pl.BlockSpec((1, block, width), lambda s, p: (s, 0, 0)),
                keys,
                keys,
                keys,
                keys,
                pl.BlockSpec((1, block, 1), lambda s, p: (s, 0, 0)),
                pl.BlockSpec((1, 1, seq_len), lambda s, p: (s, 0, 0)),
            ],
            out_specs=[
                pl.BlockSpec((1, block, width), lambda s, p: (s, 0, 0)),
                pl.BlockSpec((1, heads, block), lambda s, p: (s, 0, 0)),
            ],
        ),
        out_shape=[
            jax.ShapeDtypeStruct((seqs, block, width), BF),
            jax.ShapeDtypeStruct((seqs, heads, block), F32),
        ],
        cost_estimate=pl.CostEstimate(
            flops=4 * work * HD * 4, bytes_accessed=6 * q.size, transcendentals=work
        ),
        name="attend",
    )(place, q, *blocks, seg_q, seg_k)


def attend_back_kernel(
    group,
    place_ref,
    q_ref,
    k0,
    k1,
    k2,
    k3,
    segq_ref,
    segk_ref,
    out_ref,
    grad_ref,
    lse_ref,
    dq_ref,
    d0,
    d1,
    d2,
    d3,
    bias_ref,
    dsc_ref,
):
    block = q_ref.shape[1]
    kv_heads = k0.shape[2] // (2 * HD)
    me = place_ref[0]
    scale = LOG2E / math.sqrt(HD)
    back_scale = 1.0 / math.sqrt(HD)
    refs, d_refs = (k0, k1, k2, k3), (d0, d1, d2, d3)
    key_row = lax.broadcasted_iota(jnp.int32, (block, block), 0)
    q_col = lax.broadcasted_iota(jnp.int32, (block, block), 1)
    seg_q = segq_ref[0]
    for k in range(len(refs)):
        there = place_ref[1 + k]
        seg_k = segk_ref[0, pl.ds(pl.multiple_of(there * block, block), block), :]
        ahead = (there - me) * block
        allowed = (seg_q == seg_k) & (q_col >= key_row + ahead)
        bias_ref[k] = jnp.where(allowed, 0.0, NEG_FILL)
    width = group * block
    product = out_ref[0].astype(F32) * grad_ref[0].astype(F32)
    total_heads = kv_heads * group
    feature = lax.broadcasted_iota(jnp.int32, (total_heads, product.shape[1]), 1)
    owner = lax.broadcasted_iota(jnp.int32, (total_heads, product.shape[1]), 0)
    picks = jnp.where(feature // HD == owner, 1.0, 0.0).astype(F32)
    deltas = lax.dot_general(
        picks,
        product,
        (((1,), (1,)), ((), ())),
        preferred_element_type=F32,
        precision=lax.Precision.HIGHEST,
    )
    for g in range(kv_heads):
        heads = range(g * group, (g + 1) * group)
        q = jnp.concatenate([q_ref[0, :, h * HD : (h + 1) * HD] for h in heads], 0)
        grad = jnp.concatenate([grad_ref[0, :, h * HD : (h + 1) * HD] for h in heads], 0)
        d_query = None
        for k in range(len(refs)):
            keys = refs[k][0, :, g * HD : (g + 1) * HD]
            values = refs[k][0, :, (kv_heads + g) * HD : (kv_heads + g + 1) * HD]
            scores = dot_cols(keys, q)
            d_probs = dot_cols(values, grad)
            probs_low = []
            for j, h in enumerate(heads):
                cols = slice(j * block, (j + 1) * block)
                probs = jnp.exp2(
                    scores[:, cols] * scale + (bias_ref[k] - lse_ref[0, h : h + 1, :])
                )
                probs_low.append(probs.astype(BF))
                dsc_ref[:, cols] = (
                    probs * (d_probs[:, cols] - deltas[h : h + 1, :])
                ).astype(BF)
            d_scores = dsc_ref[...]
            d_value = dot_plain(jnp.concatenate(probs_low, 1), grad)
            d_key = dot_plain(d_scores, q) * back_scale
            d_refs[k][0, :, g * HD : (g + 1) * HD] = d_key.astype(BF)
            d_refs[k][0, :, (kv_heads + g) * HD : (kv_heads + g + 1) * HD] = d_value.astype(BF)
            part = dot_rows(d_scores, keys)
            d_query = part if d_query is None else d_query + part
        d_query = d_query * back_scale
        for j, h in enumerate(heads):
            dq_ref[0, :, h * HD : (h + 1) * HD] = d_query[j * block : (j + 1) * block].astype(BF)


def attend_back_call(place, q, blocks, seg_q, seg_k, out, grad, lse):
    seqs, block, width = q.shape
    heads = width // HD
    kv_width = blocks[0].shape[2]
    group = heads // (kv_width // (2 * HD))
    seq_len = seg_k.shape[1]
    keys = pl.BlockSpec((1, block, kv_width), lambda s, p: (s, 0, 0))
    rows = pl.BlockSpec((1, block, width), lambda s, p: (s, 0, 0))
    work = seqs * heads * block * seq_len
    return pl.pallas_call(
        functools.partial(attend_back_kernel, group),
        grid_spec=pltpu.PrefetchScalarGridSpec(
            num_scalar_prefetch=1,
            grid=(seqs,),
            in_specs=[
                rows,
                keys,
                keys,
                keys,
                keys,
                pl.BlockSpec((1, 1, block), lambda s, p: (s, 0, 0)),
                pl.BlockSpec((1, seq_len, 1), lambda s, p: (s, 0, 0)),
                rows,
                rows,
                pl.BlockSpec((1, heads, block), lambda s, p: (s, 0, 0)),
            ],
            out_specs=[rows, keys, keys, keys, keys],
            scratch_shapes=[
                pltpu.VMEM((4, block, block), F32),
                pltpu.VMEM((block, group * block), BF),
            ],
        ),
        out_shape=[jax.ShapeDtypeStruct(q.shape, BF)]
        + [jax.ShapeDtypeStruct(blocks[0].shape, BF)] * 4,
        cost_estimate=pl.CostEstimate(
            flops=10 * work * HD * 4, bytes_accessed=12 * q.size, transcendentals=work
        ),
        name="attend_back",
    )(place, q, *blocks, seg_q, seg_k, out, grad, lse)


def inverse_rms(values):
    return lax.rsqrt(jnp.mean(values * values, axis=-1, keepdims=True) + EPSILON)


def norm_back(values, gain, incoming):
    scale = inverse_rms(values)
    gain_terms = jnp.sum(incoming * values * scale, axis=0)
    weighted = incoming * gain
    inner = jnp.mean(weighted * values, axis=-1, keepdims=True)
    return scale * weighted - values * (scale * scale * scale) * inner, gain_terms


def per_device(
    tokens,
    segments,
    q_weight,
    k_weight,
    v_weight,
    o_weight,
    attn_gain,
    gate_weight,
    up_weight,
    down_weight,
    ffn_gain,
    cotangent,
):
    heads_axes = ("yy", "core")
    seqs, block, width = tokens.shape
    seq_len = segments.shape[1]
    parts = lax.axis_size(heads_axes)
    ways = lax.axis_size("tensor")
    owners = ("fsdp",) + heads_axes
    here = lax.axis_index(heads_axes)
    me = lax.axis_index("tensor")
    q_width, k_width = q_weight.shape[1], k_weight.shape[1]
    kv_width = 2 * k_width
    qkv_width = q_width + kv_width
    per_chunk = seqs // CHUNKS
    rows = per_chunk * block
    own_rows = rows // ways

    clock = Clock()
    slot = clock.slot
    where_all = positions(segments)
    where_here = lax.dynamic_slice_in_dim(where_all, here * block, block, 1)
    seg_here = lax.dynamic_slice_in_dim(segments, here * block, block, 1)
    lane = np.arange(128)
    frequency = jnp.asarray(
        ROPE_BASE ** (-2.0 * (np.arange(128) % 32).astype(np.float32) / HD), F32
    )
    angles = where_here.reshape(seqs * block, 1).astype(F32) * frequency
    cosine = jnp.cos(angles)
    sine = jnp.sin(angles) * jnp.asarray(np.where(lane % 64 < 32, -1.0, 1.0), F32)
    place = jnp.stack([here] + [here ^ k for k in range(parts)]).astype(jnp.int32)

    def chunk_of(x, c):
        return lax.slice_in_dim(x, c * per_chunk, (c + 1) * per_chunk, axis=0)

    def own(x):
        return lax.dynamic_slice_in_dim(x, me * own_rows, own_rows, 0)

    def own_of(x, chunk):
        flat = x.reshape(seqs * block, width)
        return lax.dynamic_slice_in_dim(flat, chunk * rows + me * own_rows, own_rows, 0)

    def blocks(x):
        return x.reshape(ways, own_rows, width)

    state = []
    for c in range(CHUNKS):
        s = {}
        tok = chunk_of(tokens, c).reshape(rows, width)
        s["tok"] = tok
        s["own_tok"], s["own_cot"] = own_of(tokens, c), own_of(cotangent, c)
        s["cos"] = lax.slice_in_dim(cosine, c * rows, (c + 1) * rows, axis=0)
        s["sin"] = lax.slice_in_dim(sine, c * rows, (c + 1) * rows, axis=0)
        s["sin_back"] = -s["sin"]
        s["scale_one"] = inverse_rms(tok.astype(F32))
        seg_q, seg_k = chunk_of(seg_here, c), chunk_of(segments, c)
        s["seg_fwd"] = (seg_q[:, :, None], seg_k[:, None, :])
        s["seg_back"] = (seg_q[:, None, :], seg_k[:, :, None])
        state.append(s)
    first, second = state

    pad = jnp.zeros((q_weight.shape[0], 126), BF)
    packed = jnp.concatenate(
        [q_weight, o_weight, k_weight, v_weight, attn_gain[:, None], ffn_gain[:, None], pad],
        axis=1,
    )

    def gathered(shard):
        return lax.all_gather(shard, owners, axis=0, tiled=True)

    gather_near = NearGather(packed)
    slot([gather_near])
    for s in state:
        for name in ("cos", "sin", "sin_back", "scale_one"):
            clock.expect(s[name])
        for name in ("seg_fwd", "seg_back"):
            clock.last += s[name]
    clock.expect(place)
    slot([gather_near])
    slot([gather_near], lambda *shards: shards, (gate_weight, up_weight, down_weight))
    gate_weight, up_weight, down_weight = clock.last[-3:]
    full_g = gathered(gate_weight)
    full_u = gathered(up_weight)
    full_d = gathered(down_weight)
    packed = gather_near.result()
    at = 0
    columns = []
    for wide in (q_width, q_width, kv_width, 2):
        columns.append(packed[:, at : at + wide])
        at += wide
    full_q, full_o, full_kv, gains = columns
    gains = gains.T.astype(F32)
    gain_one, gain_two = gains[0:1], gains[1:2]

    def project_kv(s, tok):
        normed = (tok.astype(F32) * s["scale_one"] * gain_one).astype(BF)
        kv = turn_call(dot_plain(normed, full_kv), s["cos"], s["sin"], k_width)
        return normed, kv.reshape(per_chunk, block, kv_width)

    def project_q(s, normed):
        q = turn_call(dot_plain(normed, full_q), s["cos"], s["sin"], q_width)
        return (q.reshape(per_chunk, block, q_width),)

    def project(s, tok):
        normed, kv = project_kv(s, tok)
        return (normed, kv) + project_q(s, normed)

    def attend(s, q, *kv):
        attended, lse = attend_call(place, q, kv, *s["seg_fwd"])
        s["attended"], s["lse"] = attended, lse
        attn = dot_cols(attended.reshape(rows, q_width), full_o).astype(BF)
        return attended, lse, attn

    def enter_ffn(s, summed):
        s["residual"] = s["own_tok"].astype(F32) + summed
        return (s["residual"] * inverse_rms(s["residual"]) * gain_two).astype(BF)

    turned = {}

    def turn_over(weight):
        return (transpose_call(weight),)

    cot_rows = cotangent.reshape(seqs * block, width)

    def ffn_mid(chunk, normed_two):
        return ffn_call(normed_two, cot_rows, full_g, full_u, full_d, chunk)

    def ffn_back(d_gate, d_up):
        return (product_call((d_gate, d_up), (turned["g"], turned["u"]), True),)

    def ffn_out(hidden):
        return (product_call((hidden,), (full_d,), False),)

    def leave_ffn(s, summed):
        d_norm, s["gain_two"] = norm_back(s["residual"], gain_two, summed)
        s["d_resid"] = s["own_cot"].astype(F32) + d_norm
        return s["d_resid"].astype(BF)

    def attend_back(s, d_attn):
        d_attended = dot_plain(d_attn, full_o).astype(BF).reshape(per_chunk, block, q_width)
        return attend_back_call(
            place, s["q"], s["kv"], *s["seg_back"], s["attended"], d_attended, s["lse"]
        )

    def project_back(s, dq, b0, b1, b2, b3):
        from3 = lax.ppermute(b3, "core", FLIP)
        from1 = lax.ppermute(b1, "core", FLIP)
        far = (b2.astype(F32) + from3.astype(F32)).astype(BF)
        from2 = lax.ppermute(far, "yy", FLIP)
        kv_parts = [x.reshape(rows, kv_width) for x in (b0, from1, from2)]
        d_qkv = turn_back_call(
            dq.reshape(rows, q_width), kv_parts, s["cos"], s["sin_back"], k_width
        )
        full_qkv = jnp.concatenate([full_q, full_kv], axis=1)
        return d_qkv, dot_cols(d_qkv, full_qkv).astype(BF)

    def leave_attention(s, summed):
        d_norm, s["gain_one"] = norm_back(s["own_tok"].astype(F32), gain_one, summed)
        return (s["d_resid"] + d_norm).astype(BF)

    def scattered(grad):
        return lax.psum_scatter(grad, owners, scatter_dimension=0, tiled=True)

    def weight_grad(*halves):
        left = jnp.concatenate(halves[:-CHUNKS], axis=0)
        right = jnp.concatenate(halves[-CHUNKS:], axis=0)
        return (dot_rows(left, right).astype(BF),)

    def of_both(*names):
        return tuple(s[name] for name in names for s in state)

    def whole(rows_of):
        return rows_of.reshape(per_chunk, block, width)

    axes = ("tensor", "core", "yy", "fsdp")
    first["normed_one"], kv = slot(
        [], functools.partial(project_kv, first), (first["tok"],)
    )
    keys = KeyExchange(kv)
    (first["q"],) = slot(
        [keys], functools.partial(project_q, first), (first["normed_one"],)
    )
    slot([keys])
    first["kv"] = keys.result()
    first["attended"], first["lse"], attn = slot(
        [], functools.partial(attend, first), (first["q"],) + first["kv"]
    )
    sum_a0 = LineSum(blocks(attn))
    second["normed_one"], kv, second["q"] = slot(
        [sum_a0], functools.partial(project, second), (second["tok"],)
    )
    keys = KeyExchange(kv)
    slot([sum_a0, keys])
    slot([sum_a0, keys])
    second["kv"] = keys.result()
    gather_a0 = LineGather(enter_ffn(first, sum_a0.result()))
    second["attended"], second["lse"], attn = slot(
        [gather_a0], functools.partial(attend, second), (second["q"],) + second["kv"]
    )
    sum_a1 = LineSum(blocks(attn))
    (turned["g"],) = slot([Both(gather_a0, sum_a1)], turn_over, (full_g,))
    (turned["u"],) = slot([Both(gather_a0, sum_a1)], turn_over, (full_u,))
    first["normed_two"] = gather_a0.result().reshape(rows, width)
    first["hidden"], first["d_gate"], first["d_up"] = slot(
        [sum_a1], functools.partial(ffn_mid, 0), (first["normed_two"],)
    )
    gather_a1 = LineGather(enter_ffn(second, sum_a1.result()))
    (back,) = slot([gather_a1], ffn_back, (first["d_gate"], first["d_up"]))
    sum_d0 = LineSum(blocks(back))
    (ffn,) = slot([Both(gather_a1, sum_d0)], ffn_out, (first["hidden"],))
    sum_f0 = LineSum(blocks(ffn))
    slot([Both(gather_a1, sum_d0)])
    second["normed_two"] = gather_a1.result().reshape(rows, width)
    second["hidden"], second["d_gate"], second["d_up"] = slot(
        [sum_d0], functools.partial(ffn_mid, 1), (second["normed_two"],)
    )
    gather_d0 = LineGather(leave_ffn(first, sum_d0.result()))
    (back,) = slot([gather_d0], ffn_back, (second["d_gate"], second["d_up"]))
    sum_d1 = LineSum(blocks(back))
    (grad,) = slot(
        [Both(gather_d0, sum_d1)],
        weight_grad,
        (cot_rows,) + of_both("hidden"),
    )
    (grad,) = slot(
        [Both(gather_d0, sum_d1), sum_f0],
        weight_grad,
        of_both("normed_two", "d_gate"),
        scattered,
        grad,
    )
    down_grad = clock.launched
    first["d_attn"] = gather_d0.result().reshape(rows, width)
    pieces = slot(
        [sum_d1, sum_f0], functools.partial(attend_back, first), (first["d_attn"],), scattered, grad
    )
    gate_grad = clock.launched
    gather_d1 = LineGather(leave_ffn(second, sum_d1.result()))
    first["d_qkv"], back = slot(
        [gather_d1, sum_f0], functools.partial(project_back, first), pieces
    )
    sum_n0 = LineSum(blocks(back))
    gather_f0 = LineGather((first["residual"] + sum_f0.result()).astype(BF))
    (grad,) = slot(
        [Both(gather_d1, sum_n0), gather_f0], weight_grad, of_both("normed_two", "d_up")
    )
    slot([Both(gather_d1, sum_n0), gather_f0], None, (), scattered, grad)
    up_grad = clock.launched
    second["d_attn"] = gather_d1.result().reshape(rows, width)
    pieces = slot(
        [sum_n0, gather_f0], functools.partial(attend_back, second), (second["d_attn"],)
    )
    gather_n0 = LineGather(leave_attention(first, sum_n0.result()))
    second["d_qkv"], back = slot(
        [gather_n0], functools.partial(project_back, second), pieces
    )
    sum_n1 = LineSum(blocks(back))
    first["output"] = gather_f0.result()
    (grad,) = slot(
        [Both(gather_n0, sum_n1)], weight_grad, of_both("normed_one", "d_qkv")
    )
    qkv_part = grad
    for s in state:
        s["attended_rows"] = s["attended"].reshape(rows, q_width)
    (grad,) = slot(
        [Both(gather_n0, sum_n1)],
        weight_grad,
        of_both("d_attn", "attended_rows"),
        scattered,
        qkv_part,
    )
    qkv_grad = clock.launched
    first["input_grad"] = gather_n0.result()
    (ffn,) = slot([sum_n1], ffn_out, (second["hidden"],), scattered, grad)
    sum_f1 = LineSum(blocks(ffn))
    o_grad = clock.launched
    gather_n1 = LineGather(leave_attention(second, sum_n1.result()))
    gains_one = Butterfly(
        jnp.stack([sum(s[name] for s in state) for name in ("gain_one", "gain_two")]), axes
    )
    slot([gather_n1, gains_one])
    slot([Both(gather_n1, sum_f1), gains_one])
    clock.expect(whole(first["input_grad"]))
    output = whole(first["output"])
    output = lax.optimization_barrier(
        jnp.concatenate([output, jnp.zeros_like(output)], axis=0)
    )
    clock.expect(output)
    slot([Both(gather_n1, sum_f1), gains_one])
    second["input_grad"] = gather_n1.result()
    clock.expect(down_grad)
    slot([sum_f1, gains_one])
    input_grad = jnp.concatenate([whole(s["input_grad"]) for s in state], axis=0).astype(F32)
    gather_f1 = LineGather((second["residual"] + sum_f1.result()).astype(BF))
    clock.expect(gate_grad)
    slot([gather_f1, gains_one])
    clock.expect(input_grad)
    down_grad, gate_grad = down_grad.astype(F32), gate_grad.astype(F32)
    clock.expect(up_grad)
    slot([gather_f1])
    clock.expect(down_grad)
    clock.expect(gate_grad)
    up_grad = up_grad.astype(F32)
    clock.expect(up_grad)
    slot([gather_f1])
    second["output"] = gather_f1.result()
    while gains_one.moves:
        slot([gains_one])

    qkv_grad, o_grad = qkv_grad.astype(F32), o_grad.astype(F32)
    share = attn_gain.shape[0]
    index = lax.axis_index("fsdp") * parts + here

    def owned(gain):
        return lax.dynamic_slice_in_dim(gain, index * share, share, 0)

    gain_one_grad, gain_two_grad = gains_one.value

    return (
        lax.dynamic_update_slice_in_dim(output, whole(second["output"]), per_chunk, 0),
        input_grad,
        qkv_grad[:, :q_width],
        qkv_grad[:, q_width : q_width + k_width],
        qkv_grad[:, q_width + k_width :],
        o_grad,
        owned(gain_one_grad),
        gate_grad,
        up_grad,
        down_grad,
        owned(gain_two_grad),
    )


def solution(mesh):
    sizes = mesh.shape
    split = (sizes["fsdp"], sizes["heads"] // 2, 2, sizes["tensor"])
    mesh = jax.sharding.Mesh(mesh.devices.reshape(split), ("fsdp", "yy", "core", "tensor"))
    heads = ("yy", "core")
    rows = P("fsdp", heads, None)
    matrix = P(("fsdp",) + heads, "tensor")
    vector = P(("fsdp",) + heads)
    return jax.shard_map(
        per_device,
        mesh=mesh,
        in_specs=(
            rows,
            P("fsdp", None),
            matrix,
            matrix,
            matrix,
            matrix,
            vector,
            matrix,
            matrix,
            matrix,
            vector,
            rows,
        ),
        out_specs=(
            rows,
            rows,
            matrix,
            matrix,
            matrix,
            matrix,
            vector,
            matrix,
            matrix,
            matrix,
            vector,
        ),
        check_vma=False,
    )
```
